32 devices in a mesh: wide: 8 (over y, x, core), narrow: 4 (over z).
Axes of the slice: x: 2, y: 2, z: 4, core: 2. Of those that a mesh axis runs over, the one named last changes fastest.
Arguments:
- tokens: bfloat16 [64, 128, 1120], P(('wide', 'narrow')), may hold values from -6 to 6
- lengths: int32 [64], P(('wide', 'narrow')), may hold values from 1 to 128, 5120 in all
- ln1_gain: bfloat16 [1120], P('narrow'), may hold values from 0.5 to 1.5
- ln1_bias: bfloat16 [1120], P('narrow'), may hold values from -1 to 1
- w_qkv: bfloat16 [1120, 3360], P('narrow'), may hold values from -0.1875 to 0.1875
- w_out: bfloat16 [1120, 1120], P('narrow'), may hold values from -0.5 to 0.5
- ln2_gain: bfloat16 [1120], P('narrow'), may hold values from 0.5 to 1.5
- ln2_bias: bfloat16 [1120], P('narrow'), may hold values from -1 to 1
- w_fc: bfloat16 [1120, 4480], P('narrow'), may hold values from -0.1875 to 0.1875
- w_proj: bfloat16 [4480, 1120], P('narrow'), may hold values from -0.09375 to 0.09375
- cotangent: bfloat16 [64, 128, 1120], P(('wide', 'narrow')), may hold values from -6 to 6
Outputs:
- result: bfloat16 [64, 128, 1120], P(('wide', 'narrow'))
- grad_tokens: bfloat16 [64, 128, 1120], P(('wide', 'narrow'))
- grad_ln1_gain: float32 [1120], P('narrow')
- grad_ln1_bias: float32 [1120], P('narrow')
- grad_w_qkv: float32 [1120, 3360], P('narrow')
- grad_w_out: float32 [1120, 1120], P('narrow')
- grad_ln2_gain: float32 [1120], P('narrow')
- grad_ln2_bias: float32 [1120], P('narrow')
- grad_w_fc: float32 [1120, 4480], P('narrow')
- grad_w_proj: float32 [4480, 1120], P('narrow')
The draws below stay inside these ranges and needn't reach their ends.
All inputs are finite; a program needn't handle non-finite values. No bound on the sum of `lengths` on one device may be relied on, other than what follows from the above.
Results may differ from the reference program's by a relative error of at most 0.015.
Values may be sent and summed in bfloat16 or wider, within the bound.
A program may use at most 256 MiB of HBM per device.

```python
import math
import jax
import jax.numpy as jnp
import numpy as np
from jax import lax

D = 1120
HEADS = 20
HEAD = 56
FF = 4480
SEQ = 128
CELLS = 64


def steps_of(stream_key, dims, shards, least, top_value):
    def one(axis_at, blocks):
        draws = jax.random.uniform(jax.random.fold_in(jax.random.fold_in(stream_key, 6), axis_at), (blocks,), jnp.float32, least / len(shards), top_value / len(shards))
        return jnp.repeat(jnp.exp(draws), dims[axis_at] // blocks).reshape((-1,) + (1,) * (len(dims) - axis_at - 1))

    loudness = one(*shards[0])
    for cut in shards[1:]:
        loudness = loudness * one(*cut)
    return loudness


def length_profile(amount, total, reach, slope):
    loads = [(1 << 20) // math.isqrt(grade ** slope) + 1 for grade in range(2, amount + 1)]
    spare, given = total - reach - (amount - 1), [1] * (amount - 1)
    while spare > 0:
        candidates = [i for i in range(amount - 1) if given[i] < reach]
        mass, left = sum([loads[i] for i in candidates]), spare
        for i in candidates:
            more = min(reach - given[i], max(1, left * loads[i] // mass), spare)
            given[i] = given[i] + more
            spare = spare - more
    return np.array([reach] + given)


def ragged_sizes(stream_key, number_of, total, limit, skew):
    if number_of == 2:
        one = jax.random.randint(stream_key, (), max(1, total - limit), min(limit, total - 1) + 1)
        return jnp.stack([one, total - one])
    tallies = jnp.asarray(length_profile(number_of, total, limit, skew), jnp.int32)
    pairs = (number_of - 1) // 2
    donor, receiver = tallies[1:1 + 2 * pairs:2], tallies[2:2 + 2 * pairs:2]
    slack = jnp.minimum(donor - 1, limit - receiver)
    shifted = jax.random.randint(jax.random.fold_in(stream_key, 1), (pairs,), 0, 1 << 20) % (slack + 1)
    tallies = tallies.at[1:1 + 2 * pairs:2].set(donor - shifted).at[2:2 + 2 * pairs:2].set(receiver + shifted)
    return tallies[jax.random.permutation(jax.random.fold_in(stream_key, 2), number_of)]


def gaussian(own_key, shape, scale, bound, cuts=(), dtype=jnp.bfloat16):
    entries = jax.random.normal(own_key, shape, jnp.float32) * scale
    if len(cuts) > 0:
        entries = steps_of(own_key, shape, cuts, -0.22, 0.18) * entries
    return jnp.clip(entries, min=-bound, max=bound).astype(dtype)


def setup_inputs(seed: int = 0) -> dict:
    arg_keys = jax.random.split(jax.random.key(seed), 12)
    return {
        "tokens": gaussian(arg_keys[0], (CELLS, SEQ, D), 1.0, 6.0, ((0, 32),)),
        "lengths": ragged_sizes(arg_keys[1], CELLS, CELLS * SEQ * 5 // 8, SEQ, 2).astype(jnp.int32),
        "ln1_gain": jnp.clip(1.0 + 0.1 * jax.random.normal(arg_keys[2], (D,), jnp.float32), 0.5, 1.5).astype(jnp.bfloat16),
        "ln1_bias": gaussian(arg_keys[3], (D,), 0.2, 1.0, ((0, 4),)),
        "w_qkv": gaussian(arg_keys[4], (D, 3 * D), D ** -0.5, 0.1875, ((0, 4),)),
        "w_out": gaussian(arg_keys[5], (D, D), (D // 8) ** -0.5, 0.5, ((0, 4),)),
        "ln2_gain": jnp.clip(1.0 + 0.1 * jax.random.normal(arg_keys[6], (D,), jnp.float32), 0.5, 1.5).astype(jnp.bfloat16),
        "ln2_bias": gaussian(arg_keys[7], (D,), 0.2, 1.0, ((0, 4),)),
        "w_fc": gaussian(arg_keys[8], (D, FF), D ** -0.5, 0.1875, ((0, 4),)),
        "w_proj": gaussian(arg_keys[9], (FF, D), FF ** -0.5, 0.09375, ((0, 4),)),
        "cotangent": gaussian(arg_keys[10], (CELLS, SEQ, D), 1.0, 6.0, ((0, 32),)),
    }


@jax.custom_vjp
def low(v):
    return lax.optimization_barrier(v.astype(jnp.bfloat16)).astype(jnp.float32)

@jax.custom_vjp
def low_back(v):
    return v

def low_keep(v):
    return (low(v), None)

def low_pass(kept, grad):
    return (grad,)

def back_keep(v):
    return (v, None)

def back_low(kept, grad):
    return (low(grad),)
low.defvjp(low_keep, low_pass)
low_back.defvjp(back_keep, back_low)
HIGH = lax.Precision.HIGHEST
EPS = 1e-05
MASKED = -1e+30

def layer_norm(in_rows, gain_vec, shift_vec):
    row_mean = lax.optimization_barrier(jnp.mean(in_rows, axis=-1, keepdims=True))
    centered = in_rows - row_mean
    inv_std = lax.rsqrt(lax.optimization_barrier(jnp.mean(centered * centered, axis=-1, keepdims=True)) + EPS)
    return centered * inv_std * gain_vec + shift_vec

def matmul_high(left, right):
    return jnp.dot(left, right, precision=HIGH)

def round_both(value):
    return low(low_back(value))

def cell_layer(in_rows, length, param_set):
    gain_one, shift_one, weight_qkv, weight_out, gain_two, shift_two, weight_fc, weight_proj = param_set
    first_norm = low(layer_norm(in_rows, gain_one, shift_one))
    projected = matmul_high(first_norm, weight_qkv)
    queries = round_both(projected[:, :D]).reshape(SEQ, HEADS, HEAD)
    key_rows = round_both(projected[:, D:2 * D]).reshape(SEQ, HEADS, HEAD)
    value_rows = round_both(projected[:, 2 * D:]).reshape(SEQ, HEADS, HEAD)
    scores = jnp.einsum('qhd,khd->hqk', queries, key_rows, precision=HIGH) * HEAD ** (-0.5)
    scores = low_back(scores)
    query_pos = lax.broadcasted_iota(jnp.int32, (SEQ, SEQ), 0)
    key_pos = lax.broadcasted_iota(jnp.int32, (SEQ, SEQ), 1)
    allowed = (key_pos <= query_pos) & (key_pos < length)
    scores = jnp.where(allowed[None], scores, MASKED)
    attn_prob = jax.nn.softmax(scores, axis=-1)
    heads_out = jnp.einsum('hqk,khd->qhd', low(attn_prob), value_rows, precision=HIGH)
    attended = round_both(heads_out.reshape(SEQ, D))
    mixed_rows = in_rows + low_back(matmul_high(attended, weight_out))
    second_norm = low(layer_norm(mixed_rows, gain_two, shift_two))
    pre_act = low_back(matmul_high(second_norm, weight_fc))
    gelu_out = low(jax.nn.gelu(pre_act, approximate=True))
    return mixed_rows + low_back(matmul_high(gelu_out, weight_proj))

def reference(tokens, lengths, ln1_gain, ln1_bias, w_qkv, w_out, ln2_gain, ln2_bias, w_fc, w_proj, cotangent):
    params = (ln1_gain.astype(jnp.float32), ln1_bias.astype(jnp.float32), w_qkv.astype(jnp.float32), w_out.astype(jnp.float32), ln2_gain.astype(jnp.float32), ln2_bias.astype(jnp.float32), w_fc.astype(jnp.float32), w_proj.astype(jnp.float32))
    group = math.gcd(CELLS, max(1, 4096 // SEQ))
    groups = CELLS // group
    lens_grouped = lengths.reshape(groups, group)

    def whole(rows_all, param_set):

        def one_group(pair):
            return jax.vmap(cell_layer, in_axes=(0, 0, None))(pair[0], pair[1], param_set)
        grouped = lax.map(jax.checkpoint(one_group), (rows_all.reshape(groups, group, SEQ, D), lens_grouped))
        return grouped.reshape(CELLS, SEQ, D)
    output, pull = jax.vjp(whole, tokens.astype(jnp.float32), params)
    grad_rows, grad_params = pull(cotangent.astype(jnp.float32))
    return (output.astype(jnp.bfloat16), grad_rows.astype(jnp.bfloat16), grad_params[0], grad_params[1], grad_params[2], grad_params[3], grad_params[4], grad_params[5], grad_params[6], grad_params[7])
```

```python
from functools import partial

import jax
import jax.numpy as jnp
from jax import lax
from jax.sharding import PartitionSpec as P

HEADS = 20


EPS = 1e-05
MASKED = -1e30


def layer_norm(in_rows, gain_vec, shift_vec):
    row_mean = jnp.mean(in_rows, axis=-1, keepdims=True)
    centered = in_rows - row_mean
    inv_std = lax.rsqrt(jnp.mean(centered * centered, axis=-1, keepdims=True) + EPS)
    normed = centered * inv_std
    return (normed * gain_vec + shift_vec, normed, inv_std)


def norm_grad(grad_rows, gain_vec, normed, inv_std):
    scaled = grad_rows * gain_vec
    return inv_std * (
        scaled
        - jnp.mean(scaled, axis=-1, keepdims=True)
        - normed * jnp.mean(scaled * normed, axis=-1, keepdims=True)
    )


def inner_rows(left, right):
    return lax.dot_general(
        left, right, (((0,), (0,)), ((), ())), preferred_element_type=jnp.float32
    )


def times_trans(left, right):
    return lax.dot_general(
        left, right, (((1,), (1,)), ((), ())), preferred_element_type=jnp.float32
    )


def attn_scores(queries, key_rows, length):
    seq_len = queries.shape[0]
    head_size = queries.shape[2]
    scores = jnp.einsum(
        "qhd,khd->hqk", queries, key_rows, preferred_element_type=jnp.float32
    ) * head_size ** (-0.5)
    query_pos = lax.broadcasted_iota(jnp.int32, (seq_len, seq_len), 0)
    key_pos = lax.broadcasted_iota(jnp.int32, (seq_len, seq_len), 1)
    allowed = (key_pos <= query_pos) & (key_pos < length)
    return jnp.where(allowed[None], scores, MASKED)


def forward_cell(in_rows, length, weights):
    gain_one, shift_one, weight_qkv, weight_out, gain_two, shift_two, weight_fc, weight_proj = (
        weights
    )
    seq_len, model_width = in_rows.shape
    head_size = model_width // HEADS
    first_norm, normed_one, inv_one = layer_norm(
        in_rows, gain_one.astype(jnp.float32), shift_one.astype(jnp.float32)
    )
    first_low = first_norm.astype(jnp.bfloat16)
    projected = jnp.dot(first_low, weight_qkv, preferred_element_type=jnp.float32)
    queries = projected[:, :model_width].astype(jnp.bfloat16).reshape(seq_len, HEADS, head_size)
    key_rows = (
        projected[:, model_width : 2 * model_width]
        .astype(jnp.bfloat16)
        .reshape(seq_len, HEADS, head_size)
    )
    value_rows = (
        projected[:, 2 * model_width :].astype(jnp.bfloat16).reshape(seq_len, HEADS, head_size)
    )
    scores = attn_scores(queries, key_rows, length)
    row_max = jnp.max(scores, axis=-1, keepdims=True)
    exp_scores = jnp.exp(scores - row_max)
    row_total = jnp.sum(exp_scores, axis=-1, keepdims=True)
    attn_prob = exp_scores / row_total
    log_total = row_max + jnp.log(row_total)
    heads_out = jnp.einsum(
        "hqk,khd->qhd",
        attn_prob.astype(jnp.bfloat16),
        value_rows,
        preferred_element_type=jnp.float32,
    )
    attended = heads_out.reshape(seq_len, model_width).astype(jnp.bfloat16)
    mixed_rows = in_rows + jnp.dot(attended, weight_out, preferred_element_type=jnp.float32)
    second_norm, normed_two, inv_two = layer_norm(
        mixed_rows, gain_two.astype(jnp.float32), shift_two.astype(jnp.float32)
    )
    second_low = second_norm.astype(jnp.bfloat16)
    pre_act = jnp.dot(second_low, weight_fc, preferred_element_type=jnp.float32)
    gelu_out = jax.nn.gelu(pre_act, approximate=True).astype(jnp.bfloat16)
    result = mixed_rows + jnp.dot(gelu_out, weight_proj, preferred_element_type=jnp.float32)
    saved_acts = (
        normed_one,
        inv_one,
        first_low,
        queries,
        key_rows,
        value_rows,
        log_total,
        attended,
        normed_two,
        inv_two,
        second_low,
        pre_act,
        gelu_out,
    )
    return (result, saved_acts)


def backward_cell(grad_rows, length, saved_acts, weights):
    gain_one, shift_one, weight_qkv, weight_out, gain_two, shift_two, weight_fc, weight_proj = (
        weights
    )
    (
        normed_one,
        inv_one,
        first_low,
        queries,
        key_rows,
        value_rows,
        log_total,
        attended,
        normed_two,
        inv_two,
        second_low,
        pre_act,
        gelu_out,
    ) = saved_acts
    seq_len, model_width = grad_rows.shape
    head_size = model_width // HEADS
    grad_low = grad_rows.astype(jnp.bfloat16)
    grad_wproj = inner_rows(gelu_out, grad_low)
    grad_gelu = times_trans(grad_low, weight_proj)
    unused, gelu_pull = jax.vjp(partial(jax.nn.gelu, approximate=True), pre_act)
    grad_pre = gelu_pull(grad_gelu)[0].astype(jnp.bfloat16)
    grad_wfc = inner_rows(second_low, grad_pre)
    grad_second = times_trans(grad_pre, weight_fc)
    grad_gain_two = jnp.sum(grad_second * normed_two, axis=0)
    grad_shift_two = jnp.sum(grad_second, axis=0)
    grad_mixed = grad_rows + norm_grad(
        grad_second, gain_two.astype(jnp.float32), normed_two, inv_two
    )
    mixed_low = grad_mixed.astype(jnp.bfloat16)
    grad_wout = inner_rows(attended, mixed_low)
    grad_attended = (
        times_trans(mixed_low, weight_out).astype(jnp.bfloat16).reshape(seq_len, HEADS, head_size)
    )
    scores = attn_scores(queries, key_rows, length)
    attn_prob = jnp.exp(scores - log_total)
    grad_value = jnp.einsum(
        "hqk,qhd->khd",
        attn_prob.astype(jnp.bfloat16),
        grad_attended,
        preferred_element_type=jnp.float32,
    )
    grad_prob = jnp.einsum(
        "qhd,khd->hqk", grad_attended, value_rows, preferred_element_type=jnp.float32
    )
    grad_scores = attn_prob * (grad_prob - jnp.sum(attn_prob * grad_prob, axis=-1, keepdims=True))
    grad_scores = grad_scores.astype(jnp.bfloat16)
    scale_factor = head_size ** (-0.5)
    grad_query = (
        jnp.einsum("hqk,khd->qhd", grad_scores, key_rows, preferred_element_type=jnp.float32)
        * scale_factor
    )
    grad_key = (
        jnp.einsum("hqk,qhd->khd", grad_scores, queries, preferred_element_type=jnp.float32)
        * scale_factor
    )
    grad_proj_in = jnp.concatenate(
        [
            grad_query.reshape(seq_len, model_width),
            grad_key.reshape(seq_len, model_width),
            grad_value.reshape(seq_len, model_width),
        ],
        axis=1,
    ).astype(jnp.bfloat16)
    grad_wqkv = inner_rows(first_low, grad_proj_in)
    grad_first = times_trans(grad_proj_in, weight_qkv)
    grad_gain_one = jnp.sum(grad_first * normed_one, axis=0)
    grad_shift_one = jnp.sum(grad_first, axis=0)
    grad_input = grad_mixed + norm_grad(
        grad_first, gain_one.astype(jnp.float32), normed_one, inv_one
    )
    grads = (
        grad_gain_one,
        grad_shift_one,
        grad_wqkv,
        grad_wout,
        grad_gain_two,
        grad_shift_two,
        grad_wfc,
        grad_wproj,
    )
    return (grads, grad_input)


def shards(
    tokens, lengths, ln1_gain, ln1_bias, w_qkv, w_out, ln2_gain, ln2_bias, w_fc, w_proj, cotangent
):
    outputs = []
    input_grads = []
    running = None
    held = None
    held = (
        lax.all_gather(ln1_gain, "narrow", axis=0, tiled=True),
        lax.all_gather(ln1_bias, "narrow", axis=0, tiled=True),
        lax.all_gather(w_qkv, "narrow", axis=0, tiled=True),
        lax.all_gather(w_out, "narrow", axis=0, tiled=True),
        lax.all_gather(ln2_gain, "narrow", axis=0, tiled=True),
        lax.all_gather(ln2_bias, "narrow", axis=0, tiled=True),
        lax.all_gather(w_fc, "narrow", axis=0, tiled=True),
        lax.all_gather(w_proj, "narrow", axis=0, tiled=True),
    )
    for micro_step in range(tokens.shape[0]):
        in_rows = tokens[micro_step].astype(jnp.float32)
        result, saved_acts = forward_cell(in_rows, lengths[micro_step], held)
        grads, grad_input = backward_cell(
            cotangent[micro_step].astype(jnp.float32), lengths[micro_step], saved_acts, held
        )
        running = grads if running is None else jax.tree.map(jnp.add, running, grads)
        outputs.append(result.astype(jnp.bfloat16))
        input_grads.append(grad_input.astype(jnp.bfloat16))
    totals = []
    for grad in running:
        part = lax.psum_scatter(
            grad.astype(jnp.bfloat16), "narrow", scatter_dimension=0, tiled=True
        )
        if part.ndim == 2:
            part = lax.psum(part, "wide").astype(jnp.float32)
        else:
            part = lax.psum(part.astype(jnp.float32), "wide")
        totals.append(part)
    return (
        jnp.stack(outputs),
        jnp.stack(input_grads),
        totals[0],
        totals[1],
        totals[2],
        totals[3],
        totals[4],
        totals[5],
        totals[6],
        totals[7],
    )


def solution(mesh):
    placed = (
        P(("wide", "narrow"), None, None),
        P(("wide", "narrow")),
        P("narrow"),
        P("narrow"),
        P("narrow", None),
        P("narrow", None),
        P("narrow"),
        P("narrow"),
        P("narrow", None),
        P("narrow", None),
        P(("wide", "narrow"), None, None),
    )
    return jax.shard_map(
        shards,
        mesh=mesh,
        in_specs=placed,
        out_specs=(
            P(("wide", "narrow"), None, None),
            P(("wide", "narrow"), None, None),
            P("narrow"),
            P("narrow"),
            P("narrow", None),
            P("narrow", None),
            P("narrow"),
            P("narrow"),
            P("narrow", None),
            P("narrow", None),
        ),
        check_vma=False,
    )
```

```python
import math

import jax
import jax.numpy as jnp
from jax import lax
from jax.experimental import pallas as pl
from jax.experimental.pallas import tpu as pltpu
from jax.sharding import PartitionSpec as P

HEADS = 20
EPS = 1e-05
MASKED = -1e30
BF, F32 = jnp.bfloat16, jnp.float32
MESH = pl.DeviceIdType.MESH

NZ = 4
NT = 4
WAVES = 2
SEQ = 128
NB = NT * WAVES
GELU_C = math.sqrt(2.0 / math.pi)
GELU_A = 0.044715


def up16(n):
    return -(-n // 16) * 16


def up128(n):
    return -(-n // 128) * 128


def nn(a, b):
    return lax.dot_general(a, b, (((1,), (0,)), ((), ())), preferred_element_type=F32)


def nt(a, b):
    return lax.dot_general(a, b, (((1,), (1,)), ((), ())), preferred_element_type=F32)


def tn(a, b):
    return lax.dot_general(a, b, (((0,), (0,)), ((), ())), preferred_element_type=F32)


def layer_kernel(
    dim, ff,
    tok_h, dy_h, wq_h, wo_h, wf_h, wp_h, len_s, lnv,
    res_o, gtok_o, gq_o, go_o, gf_o, gp_o, gln_o,
    tok, dys, xown, wq, wo, wf, wp, first, qs, ks, vs, pm, att, part, ra, sb, rb, mix, dmix,
    sec, act, gel, datt, dqkv, gq, go, gf, gp, yq, yo, yf, yp, zq, zo, zf, zp,
    lnr, vec, lens, lg, lr, lz,
    raw_sem, ag_sem, rs_sem, fin_sem, xs_sem, xa_sem, ln_sem,
):
    blk = dim // NZ
    bp = up16(blk)
    hb = bp // 2
    dp = NZ * bp
    nq = wq.shape[1]
    head = dim // HEADS
    nh = HEADS // NT
    inv_dim = 1.0 / dim
    scale = head ** (-0.5)

    w = lax.axis_index("wide")
    z = lax.axis_index("narrow")
    c = lax.rem(w, 2)
    x = lax.rem(w // 2, 2)
    y = lax.rem(w // 4, 2)
    t = 2 * x + c
    core_dev = (w + 1 - 2 * c, z)
    x_dev = (w + 2 - 4 * x, z)
    y_dev = (w + 4 - 8 * y, z)
    up_dev = (w, z + 1)
    down_dev = (w, z - 1)

    ends = []

    def remote(src, dst, ssem, rsem, dev):
        return pltpu.make_async_remote_copy(
            src_ref=src, dst_ref=dst, send_sem=ssem, recv_sem=rsem, device_id=dev, device_id_type=MESH
        )

    def send(make, cond=None, track=True):
        if cond is None:
            make().start()
        else:
            pl.when(cond())(lambda: make().start())
        if track:
            ends.append((cond, make))

    def both(a, b):
        return jnp.logical_and(a, b)

    lane = lax.broadcasted_iota(jnp.int32, (1, dp), 1)
    live = lax.rem(lane, bp) < blk
    livef = live.astype(F32)

    barrier = pltpu.get_barrier_semaphore()
    others = [(w, lax.rem(z + k, NZ)) for k in range(1, NZ)]
    for dev in [core_dev, x_dev, y_dev] + others:
        pl.semaphore_signal(barrier, inc=1, device_id=dev, device_id_type=MESH)
    pl.semaphore_wait(barrier, 3 + len(others))

    def rows_of(s, yy, r0=0, nr=None):
        return pl.ds(pl.multiple_of(bp * s + hb * yy + r0, 16), hb if nr is None else nr)

    q_pieces = [(0, 80), (80, hb - 80)]
    gathers = {
        "q": (wq, 0, q_pieces),
        "f": (wf, 4 * len(q_pieces), [(0, hb)]),
        "p": (wp, 4 * len(q_pieces) + 4, [(0, hb)]),
        "o": (wo, 4 * len(q_pieces) + 8, [(0, hb)]),
    }

    def ag_view(name, s, yy, piece):
        ref, base, pieces = gathers[name]
        r0, nr = pieces[piece]
        if name == "o":
            return ref.at[rows_of(0, yy, r0, nr)]
        return ref.at[rows_of(s, yy, r0, nr)]

    def ag_id(name, s, piece):
        ref, base, pieces = gathers[name]
        return base if name == "o" else base + 4 * piece + s

    def ag_z(name, s, piece, up):
        v = ag_view(name, s, y, piece)
        i = ag_id(name, s, piece)
        return remote(v, v, ag_sem.at[i, 0 if up else 1], ag_sem.at[i, 2], up_dev if up else down_dev)

    def ag_y(name, s, yy, piece):
        v = ag_view(name, s, yy, piece)
        i = ag_id(name, s, piece)
        return remote(v, v, ag_sem.at[i, 3], ag_sem.at[i, 4], y_dev)

    def ag_start(name):
        for piece in range(len(gathers[name][2])):
            def own():
                return (t == z) if name == "o" else (z >= 0)

            send(lambda p=piece: ag_z(name, z, p, True), lambda: both(own(), z < NZ - 1))
            send(lambda p=piece: ag_z(name, z, p, False), lambda: both(own(), z > 0))

    def ag_forward(name, k):
        for piece in range(len(gathers[name][2])):
            for up in (True, False):
                s = z - k if up else z + k
                ok = (z >= k) if up else (z + k <= NZ - 1)
                if name == "o":
                    ok = t == s
                more = (z < NZ - 1) if up else (z > 0)
                pl.when(ok)(lambda s=s, p=piece, u=up: ag_z(name, s, p, u).wait_recv())
                send(lambda s=s, p=piece, u=up: ag_z(name, s, p, u), lambda ok=ok, more=more: both(ok, more))
                send(lambda s=s, p=piece: ag_y(name, s, y, p), lambda ok=ok: ok)

    def ag_finish(name):
        for piece in range(len(gathers[name][2])):
            if name == "o":
                pl.when(z != t)(lambda p=piece: ag_y(name, 0, 1 - y, p).wait_recv())
            else:
                for s in range(NZ):
                    pl.when(z != s)(lambda s=s, p=piece: ag_y(name, s, 1 - y, p).wait_recv())

    def blk_of(s, cc, xx):
        return s * NT + cc * 2 + xx

    def xg(ref, e, s, kind):
        i = 2 * e + s
        if kind == "x":
            v = ref.at[blk_of(s, c, x)]
            return remote(v, v, xs_sem.at[i, 0], xs_sem.at[i, 1], x_dev)
        if kind == "own":
            v = ref.at[blk_of(s, c, x)]
            return remote(v, v, xs_sem.at[i, 2], xs_sem.at[i, 3], core_dev)
        v = ref.at[blk_of(s, c, 1 - x)]
        return remote(v, v, xs_sem.at[i, 4], xs_sem.at[i, 5], core_dev)

    def xg_start(ref, e, s, track=True):
        send(lambda: xg(ref, e, s, "x"), track=track)
        send(lambda: xg(ref, e, s, "own"), track=track)

    def xg_forward(ref, e, s, track=True):
        xg(ref, e, s, "x").wait_recv()
        send(lambda: xg(ref, e, s, "fwd"), track=track)

    def xg_finish(ref, e, s):
        xg(ref, e, s, "own").wait_recv()
        xg(ref, e, s, "fwd").wait_recv()

    def xg_sent(ref, e, s):
        for kind in ("x", "own", "fwd"):
            xg(ref, e, s, kind).wait_send()

    def ex_a(e, s):
        i = 2 * e + s
        return remote(
            part.at[pl.ds(s * NT + (1 - c) * 2, 2)], ra.at[int(e == 1), s],
            xa_sem.at[i, 0], xa_sem.at[i, 1], core_dev,
        )

    def ex_b(e, s):
        i = 2 * e + s
        return remote(sb.at[int(e == 1), s], rb.at[int(e == 1), s], xa_sem.at[i, 2], xa_sem.at[i, 3], x_dev)

    def ex_relay(e, s):
        ex_a(e, s).wait_recv()
        sb[int(e == 1), s] = (
            part[blk_of(s, c, 1 - x)].astype(F32) + ra[int(e == 1), s, 1 - x].astype(F32)
        ).astype(BF)
        ex_b(e, s).start()

    def ex_sum(e, s):
        ex_b(e, s).wait_recv()
        return (
            part[blk_of(s, c, x)].astype(F32)
            + ra[int(e == 1), s, x].astype(F32)
            + rb[int(e == 1), s].astype(F32)
        )

    def ex_sent(e):
        for s in range(WAVES):
            ex_a(e, s).wait_send()
            ex_b(e, s).wait_send()

    reduces = {"q": (gq, yq, zq, 0), "f": (gf, yf, zf, 1), "p": (gp, yp, zp, 2), "o": (go, yo, zo, 3)}

    def rs_y(name, d):
        g, yr, zr, i = reduces[name]
        if name == "o":
            return remote(g.at[rows_of(0, 1 - y)], yr.at[0], rs_sem.at[i, 0], rs_sem.at[i, 4], y_dev)
        return remote(g.at[rows_of(d, 1 - y)], yr.at[d], rs_sem.at[i, d], rs_sem.at[i, 4 + d], y_dev)

    def rs_z(name, d, slot, up):
        g, yr, zr, i = reduces[name]
        dd = 0 if name == "o" else d
        return remote(yr.at[dd], zr.at[slot], rs_sem.at[i, 8 + dd], rs_sem.at[i, 12 + slot], up_dev if up else down_dev)

    def add_up(dst, srcs):
        step = 48

        def body(j, carry):
            r = pl.ds(pl.multiple_of(j * step, step), step)
            total = srcs[0][r, :].astype(F32)
            for src in srcs[1:]:
                total = total + src[r, :].astype(F32)
            dst[r, :] = total.astype(BF)
            return carry

        lax.fori_loop(0, hb // step, body, 0)

    def rs_start(name, dests=(3, 0, 2, 1)):
        for d in (0,) if name == "o" else dests:
            send(lambda d=d: rs_y(name, d))

    def rs_stage(name, d, j):
        g, yr, zr, i = reduces[name]

        def side(pos, up):
            def run():
                rs_y(name, d).wait_recv()
                own = g.at[rows_of(0 if name == "o" else d, y)]
                mine = yr.at[0 if name == "o" else d]
                srcs = [own, mine]
                slot = 0 if name == "o" else d
                if j > 0:
                    rs_z(name, d, slot, up).wait_recv()
                    srcs.append(zr.at[slot])
                add_up(mine, srcs)

            nxt = pos + 1 if up else pos - 1
            if name == "o":
                last = t == nxt
                cond = both(z == pos, (t > pos) if up else (t < pos))
                pl.when(cond)(run)
                if up:
                    send(lambda: rs_z(name, 0, 1, True), lambda: both(cond, last))
                    send(lambda: rs_z(name, 0, 0, True), lambda: both(cond, jnp.logical_not(last)))
                else:
                    send(lambda: rs_z(name, 0, 0, False), lambda: cond)
            else:
                cond = z == pos
                pl.when(cond)(run)
                slot = NZ if (up and nxt == d) else d
                send(lambda: rs_z(name, d, slot, up), lambda: cond)

        if name == "o":
            if j < NZ - 1:
                side(j, True)
                side(NZ - 1 - j, False)
            return
        if j < d:
            side(j, True)
        if NZ - 1 - j > d:
            side(NZ - 1 - j, False)

    def rs_final(name):
        g, yr, zr, i = reduces[name]
        out = name == "o"
        me = 0 if out else z
        here = (t == z) if out else (z >= 0)
        above = 0 if out else z
        below = 1 if out else NZ

        def run(has_above, has_below):
            def go_():
                rs_y(name, me).wait_recv()
                srcs = [g.at[rows_of(me, y)], yr.at[me]]
                if has_above:
                    rs_z(name, me, above, True).wait_recv()
                    srcs.append(zr.at[above])
                if has_below:
                    rs_z(name, me, below, True).wait_recv()
                    srcs.append(zr.at[below])
                add_up(yr.at[me], srcs)
            return go_

        pl.when(both(here, z == 0))(run(True, False))
        pl.when(both(here, z == NZ - 1))(run(False, True))
        pl.when(both(here, both(z > 0, z < NZ - 1)))(run(True, True))

    outs = {"q": gq_o, "f": gf_o, "p": gp_o, "o": go_o}

    def fin_view(name, tt, yy):
        return outs[name].at[yy] if name == "o" else outs[name].at[tt * 2 + yy]

    def fin_copy(name, src, tt, yy, k, dev):
        i = reduces[name][3]
        slot = yy if name == "o" else tt * 2 + yy
        return remote(src, fin_view(name, tt, yy), fin_sem.at[i, k], fin_sem.at[i, 8 + slot], dev)

    def own_block(name):
        yr = reduces[name][1]
        return yr.at[0] if name == "o" else yr.at[z]

    def keep_own(name):
        return pltpu.make_async_copy(own_block(name), fin_view(name, t, y), fin_sem.at[reduces[name][3], 7])

    tx = 2 * (1 - x) + c

    def fin_start(name):
        here = (lambda: t == z) if name == "o" else None
        if here is None:
            keep_own(name).start()
        else:
            pl.when(here())(lambda: keep_own(name).start())
        send(lambda: fin_copy(name, own_block(name), t, y, 0, y_dev), here)
        send(lambda: fin_copy(name, own_block(name), t, y, 1, x_dev), here)
        send(lambda: fin_copy(name, own_block(name), t, y, 2, core_dev), here)

    def fin_wait(name, tt, yy):
        fin_copy(name, fin_view(name, tt, yy), tt, yy, 0, core_dev).wait_recv()

    def fin_forward_y(name):
        here = (t == z) if name == "o" else (z >= 0)
        pl.when(here)(lambda: fin_wait(name, t, 1 - y))
        v = fin_view(name, t, 1 - y)
        send(lambda: fin_copy(name, v, t, 1 - y, 3, x_dev), lambda: here)
        send(lambda: fin_copy(name, v, t, 1 - y, 4, core_dev), lambda: here)

    def fin_forward_x(name):
        here = (tx == z) if name == "o" else (z >= 0)
        for k, yy in ((5, y), (6, 1 - y)):
            pl.when(here)(lambda yy=yy: fin_wait(name, tx, yy))
            send(lambda k=k, yy=yy: fin_copy(name, fin_view(name, tx, yy), tx, yy, k, core_dev), lambda: here)

    def fin_finish(name):
        if name == "o":
            here = lax.rem(z, 2) != c
            for yy in range(2):
                pl.when(here)(lambda yy=yy: fin_wait(name, 0, yy))
            pl.when(t == z)(lambda: keep_own(name).wait())
        else:
            for xx in range(2):
                for yy in range(2):
                    fin_wait(name, 2 * xx + (1 - c), yy)
            keep_own(name).wait()

    base = pl.multiple_of(bp * z, 16)

    def prepare(rq, rt, ro, rd):
        loads = [
            pltpu.make_async_copy(wq_h, rq, raw_sem.at[0]),
            pltpu.make_async_copy(tok_h, rt, raw_sem.at[1]),
            pltpu.make_async_copy(wo_h, ro, raw_sem.at[2]),
            pltpu.make_async_copy(dy_h, rd, raw_sem.at[3]),
        ]
        for load in loads:
            load.start()
        lnr[z] = lnv[...]
        for k in range(1, NZ):
            send(lambda k=k: remote(lnv, lnr.at[z], ln_sem.at[k - 1], ln_sem.at[2 + k], others[k - 1]))

        loads[0].wait()
        wq[pl.ds(base, bp), :] = jnp.zeros((bp, nq), BF)
        for k in range(NT):
            @pl.when(t == k)
            def _(k=k):
                for j in range(3):
                    wq[pl.ds(base, blk), blk * j : blk * (j + 1)] = rq[:, dim * j + blk * k : dim * j + blk * (k + 1)]
        ag_start("q")

        def spread(dst, src):
            dst[...] = jnp.zeros((SEQ, dp), BF)
            for j in range(NZ):
                dst[:, bp * j : bp * j + blk] = src[:, blk * j : blk * (j + 1)]

        loads[1].wait()
        for s in range(WAVES):
            spread(xown.at[s], rt.at[pl.ds(SEQ * s, SEQ)])
            sent = jnp.where(lane == blk, len_s[s].astype(F32), xown[s].astype(F32))
            tok[blk_of(s, c, x)] = sent.astype(BF)
            xg_start(tok, 0, s, track=False)
        loads[2].wait()

        @pl.when(t == z)
        def _():
            wo[...] = jnp.zeros_like(wo)
            for j in range(NZ):
                wo[0:blk, bp * j : bp * j + blk] = ro[:, blk * j : blk * (j + 1)]
        ag_start("o")
        loads[3].wait()
        for s in range(WAVES):
            spread(dys.at[blk_of(s, c, x)], rd.at[pl.ds(SEQ * s, SEQ)])
            xg_start(dys, 1, s)

    def prepare_mlp(rf, rp):
        loads = [
            pltpu.make_async_copy(wf_h, rf, raw_sem.at[4]),
            pltpu.make_async_copy(wp_h.at[pl.ds(pl.multiple_of(blk * t, 8), blk)], rp, raw_sem.at[5]),
        ]
        for load in loads:
            load.start()
        loads[0].wait()
        wf[pl.ds(base, bp), :] = jnp.zeros((bp, dp), BF)
        for k in range(NT):
            @pl.when(t == k)
            def _(k=k):
                for j in range(NZ):
                    lo = (ff // NZ) * j + blk * k
                    wf[pl.ds(base, blk), bp * j : bp * j + blk] = rf[:, lo : lo + blk]
        loads[1].wait()
        wp[pl.ds(base, bp), :] = jnp.zeros((bp, dp), BF)
        for j in range(NZ):
            wp[pl.ds(base, blk), bp * j : bp * j + blk] = rp[:, blk * j : blk * (j + 1)]

    pl.run_scoped(
        prepare,
        pltpu.VMEM((blk, 3 * dim), BF),
        pltpu.VMEM((WAVES * SEQ, dim), BF),
        pltpu.VMEM((blk, dim), BF),
        pltpu.VMEM((WAVES * SEQ, dim), BF),
    )
    pl.run_scoped(prepare_mlp, pltpu.VMEM((blk, ff), BF), pltpu.VMEM((blk, dim), BF))

    for k in range(1, NZ):
        remote(lnv, lnr.at[lax.rem(z + NZ - k, NZ)], ln_sem.at[k - 1], ln_sem.at[2 + k], others[k - 1]).wait_recv()
    vec[...] = jnp.zeros_like(vec)
    for j in range(NZ):
        vec[:, bp * j : bp * j + blk] = lnr[j, :, 0:blk]
    lg[...] = jnp.zeros_like(lg)
    dqkv[...] = jnp.zeros_like(dqkv)

    def stats(rows):
        mean = jnp.sum(rows, axis=-1, keepdims=True) * inv_dim
        cen = (rows - mean) * livef
        inv = lax.rsqrt(jnp.sum(cen * cen, axis=-1, keepdims=True) * inv_dim + EPS)
        return cen * inv, inv

    def norm_back(e, n, inv):
        me = jnp.sum(e, axis=-1, keepdims=True) * inv_dim
        mn = jnp.sum(e * n, axis=-1, keepdims=True) * inv_dim
        return inv * (e - me - n * mn) * livef

    def ln_first(s):
        def body(i, carry):
            b = s * NT + i
            raw = tok[b].astype(F32)
            lens[b] = jnp.broadcast_to(raw[0:8, blk : blk + 1], (8, SEQ))
            n, inv = stats(raw * livef)
            first[b] = (n * vec[0:1, :] + vec[1:2, :]).astype(BF)
            return carry
        lax.fori_loop(0, NT, body, 0)

    lane_h = lax.broadcasted_iota(jnp.int32, (1, bp), 1)
    head_masks = [(lane_h >= head * h) & (lane_h < head * (h + 1)) for h in range(nh)]

    def stack_heads(v):
        zero = jnp.zeros_like(v)
        return jnp.concatenate([jnp.where(m, v, zero) for m in head_masks], axis=0)

    def side_by_side(v):
        return jnp.concatenate([v[SEQ * h : SEQ * (h + 1)] for h in range(nh)], axis=1)

    def project(s):
        def body(i, carry):
            b = s * NT + i * 2
            rows = first[pl.ds(b, 2)].reshape(2 * SEQ, dp)
            out = nn(rows, wq[...])
            for j, ref in enumerate((qs, ks, vs)):
                ref[pl.ds(b, 2)] = out[:, blk * j : blk * j + bp].astype(BF).reshape(2, SEQ, bp)
            return carry
        lax.fori_loop(0, 2, body, 0)

    def attend(s):
        q_pos = lax.broadcasted_iota(jnp.int32, (SEQ, SEQ), 0)
        k_pos = lax.broadcasted_iota(jnp.int32, (SEQ, SEQ), 1)

        def body(i, carry):
            b = s * NT + i
            scores = nt(stack_heads(qs[b]), ks[b]) * scale
            ok = (k_pos <= q_pos) & (k_pos.astype(F32) < lens[b, 0:1, :])
            bias = jnp.concatenate([ok.astype(F32)] * nh, axis=0) > 0.5
            scores = jnp.where(bias, scores, MASKED)
            top = jnp.max(scores, axis=-1, keepdims=True)
            ex = jnp.exp(scores - top)
            prob = ex / jnp.sum(ex, axis=-1, keepdims=True)
            pm[b] = prob
            out = nn(side_by_side(prob.astype(BF)), stack_heads(vs[b]))
            att[b] = out.astype(BF)
            return carry
        lax.fori_loop(0, NT, body, 0)

    def matmul_part(src, weight, s, transposed):
        width = src.shape[2]

        def body(i, carry):
            b = s * NT + i * 2
            rows = src[pl.ds(b, 2)].reshape(2 * SEQ, width)
            out = nt(rows, weight[...]) if transposed else nn(rows, weight[...])
            part[pl.ds(b, 2)] = out.astype(BF).reshape(2, SEQ, dp)
            return carry
        lax.fori_loop(0, 2, body, 0)

    ag_forward("q", 1)
    xg_forward(tok, 0, 0, track=False)
    ag_forward("q", 2)
    ag_start("f")
    ag_forward("o", 1)
    xg_finish(tok, 0, 0)
    ln_first(0)
    xg_forward(tok, 0, 1, track=False)
    ag_forward("q", 3)
    xg_finish(tok, 0, 1)
    ln_first(1)
    ag_forward("o", 2)
    ag_start("p")
    ag_forward("f", 1)
    ag_forward("o", 3)
    ag_finish("q")
    project(0)
    attend(0)
    ag_finish("o")
    matmul_part(att, wo, 0, False)
    ex_a(0, 0).start()
    ag_forward("f", 2)
    project(1)
    attend(1)
    matmul_part(att, wo, 1, False)
    ex_a(0, 1).start()
    ex_relay(0, 0)
    ag_forward("f", 3)
    ag_forward("p", 1)
    ex_relay(0, 1)
    xg_forward(dys, 1, 0)
    xg_forward(dys, 1, 1)

    def mid(s):
        rows = xown[s].astype(F32) + ex_sum(0, s)
        mix[s] = rows
        n, inv = stats(rows)
        sec[blk_of(s, c, x)] = (n * vec[2:3, :] + vec[3:4, :]).astype(BF)
        xg_start(sec, 2, s)

    mid(0)
    mid(1)
    ag_forward("p", 2)
    xg_forward(sec, 2, 0)
    xg_forward(sec, 2, 1)
    ag_forward("p", 3)
    for s in range(WAVES):
        xg_sent(tok, 0, s)
    ex_sent(0)
    ag_finish("f")

    def expand(s):
        def body(i, carry):
            b = s * NT + i * 2
            rows = sec[pl.ds(b, 2)].reshape(2 * SEQ, dp)
            pre = nn(rows, wf[...])
            sq = pre * pre
            th = jnp.tanh(GELU_C * (pre + GELU_A * (pre * sq)))
            half = 0.5 * (1.0 + th)
            act[pl.ds(b, 2)] = (pre * half).astype(BF).reshape(2, SEQ, dp)
            slope = half + (0.5 * GELU_C) * pre * (1.0 - th * th) * (1.0 + (3.0 * GELU_A) * sq)
            gel[pl.ds(b, 2)] = slope.astype(BF).reshape(2, SEQ, dp)
            return carry
        lax.fori_loop(0, 2, body, 0)

    for s in range(WAVES):
        xg_finish(sec, 2, s)
        expand(s)
    for s in range(WAVES):
        xg_finish(dys, 1, s)

    def grad_of(dst, left, right):
        step = 384
        rows = NB * SEQ

        def body(j, carry):
            cols = pl.ds(pl.multiple_of(j * step, step), step)
            out = tn(left[:, :, cols].reshape(rows, step), right[...].reshape(rows, right.shape[2]))
            dst[cols, :] = out.astype(BF)
            return carry
        lax.fori_loop(0, dp // step, body, 0)

    grad_of(gp, act, dys)
    rs_start("p")
    ag_finish("p")

    def back_act(s):
        def body(i, carry):
            b = s * NT + i * 2
            d_act = nt(dys[pl.ds(b, 2)].reshape(2 * SEQ, dp), wp[...])
            slope = gel[pl.ds(b, 2)].reshape(2 * SEQ, dp).astype(F32)
            gel[pl.ds(b, 2)] = (d_act * slope).astype(BF).reshape(2, SEQ, dp)
            return carry
        lax.fori_loop(0, 2, body, 0)

    for s in range(WAVES):
        back_act(s)
        matmul_part(gel, wf, s, True)
        ex_a(2, s).start()
    rs_stage("p", 3, 0)
    rs_stage("p", 0, 0)
    ex_relay(2, 0)
    ex_relay(2, 1)
    grad_of(gf, sec, gel)
    rs_start("f")
    for d in (2, 1):
        rs_stage("p", d, 0)
    for d in (3, 0):
        rs_stage("p", d, 1)

    def back_mid(s):
        d2 = ex_sum(2, s)
        n, inv = stats(mix[s])
        lg[2:3, :] = lg[2:3, :] + jnp.sum(d2 * n, axis=0, keepdims=True)
        lg[3:4, :] = lg[3:4, :] + jnp.sum(d2, axis=0, keepdims=True)
        rows = dys[blk_of(s, c, x)].astype(F32) + norm_back(d2 * vec[2:3, :], n, inv)
        dmix[s] = rows
        tok[blk_of(s, c, x)] = rows.astype(BF)
        xg_start(tok, 3, s)

    back_mid(0)
    back_mid(1)
    ex_sent(2)
    for d in (2, 1):
        rs_stage("p", d, 1)
    for d in (3, 0):
        rs_stage("p", d, 2)
    for s in range(WAVES):
        matmul_part(act, wp, s, False)
        ex_a(1, s).start()
    xg_forward(tok, 3, 0)
    xg_forward(tok, 3, 1)
    ex_relay(1, 0)
    ex_relay(1, 1)
    rs_final("p")
    fin_start("p")

    def back_attend(s):
        def proj(i, carry):
            b = s * NT + i * 2
            out = nt(tok[pl.ds(b, 2)].reshape(2 * SEQ, dp), wo[...])
            datt[pl.ds(b, 2)] = out.astype(BF).reshape(2, SEQ, bp)
            return carry
        lax.fori_loop(0, 2, proj, 0)

        def body(i, carry):
            b = s * NT + i
            d_out = stack_heads(datt[b])
            prob = pm[b]
            d_prob = nt(d_out, vs[b])
            total = jnp.sum(prob * d_prob, axis=-1, keepdims=True)
            d_scores = (prob * (d_prob - total)).astype(BF)
            dqkv[b, :, 0:bp] = (nn(side_by_side(d_scores), stack_heads(ks[b])) * scale).astype(BF)
            dqkv[b, :, blk : blk + bp] = (tn(d_scores, stack_heads(qs[b])) * scale).astype(BF)
            dqkv[b, :, 2 * blk : 2 * blk + bp] = tn(prob.astype(BF), d_out).astype(BF)
            return carry
        lax.fori_loop(0, NT, body, 0)

    xg_finish(tok, 3, 0)
    back_attend(0)
    for d in (3, 0, 2, 1):
        rs_stage("f", d, 0)
    xg_finish(tok, 3, 1)
    back_attend(1)
    rows_all = NB * SEQ
    go[...] = tn(att[...].reshape(rows_all, bp), tok[...].reshape(rows_all, dp)).astype(BF)
    rs_start("o")
    grad_of(gq, first, dqkv)
    rs_start("q")
    for d in (3, 0, 2, 1):
        rs_stage("f", d, 1)

    for s in range(WAVES):
        rows = (mix[s] + ex_sum(1, s)).astype(BF)
        for j in range(NZ):
            res_o[SEQ * s : SEQ * (s + 1), blk * j : blk * (j + 1)] = rows[:, bp * j : bp * j + blk]
    ex_sent(1)
    for s in range(WAVES):
        matmul_part(dqkv, wq, s, True)
        ex_a(3, s).start()
    for d in (3, 0):
        rs_stage("f", d, 2)
    ex_relay(3, 0)
    ex_relay(3, 1)
    rs_final("f")
    fin_start("f")
    fin_forward_y("p")
    rs_stage("o", 0, 0)
    fin_forward_x("p")
    rs_stage("o", 0, 1)
    for d in (3, 0, 2, 1):
        rs_stage("q", d, 0)

    def back_first(s):
        d1 = ex_sum(3, s)
        n, inv = stats(xown[s].astype(F32))
        lg[0:1, :] = lg[0:1, :] + jnp.sum(d1 * n, axis=0, keepdims=True)
        lg[1:2, :] = lg[1:2, :] + jnp.sum(d1, axis=0, keepdims=True)
        rows = (dmix[s] + norm_back(d1 * vec[0:1, :], n, inv)).astype(BF)
        for j in range(NZ):
            gtok_o[SEQ * s : SEQ * (s + 1), blk * j : blk * (j + 1)] = rows[:, bp * j : bp * j + blk]

    back_first(0)
    back_first(1)
    ex_sent(3)
    rs_stage("o", 0, 2)
    for d in (3, 0, 2, 1):
        rs_stage("q", d, 1)
    rs_final("o")
    fin_start("o")
    fin_forward_y("f")
    fin_forward_x("f")

    for k, dev in enumerate((core_dev, x_dev, y_dev)):
        hop = remote(lg, lr.at[k], ln_sem.at[6 + 2 * k], ln_sem.at[7 + 2 * k], dev)
        hop.start()
        hop.wait()
        lg[...] = lg[...] + lr[k]
    for k in range(1, NZ):
        send(lambda k=k: remote(lg, lz.at[k - 1], ln_sem.at[11 + k], ln_sem.at[14 + k], others[k - 1]))
    for d in (3, 0):
        rs_stage("q", d, 2)
    rs_final("q")
    fin_start("q")
    fin_forward_y("o")
    for k in range(1, NZ):
        remote(lg, lz.at[k - 1], ln_sem.at[11 + k], ln_sem.at[14 + k], others[k - 1]).wait_recv()
    total = lg[...] + lz[0] + lz[1] + lz[2]
    for j in range(NZ):
        @pl.when(z == j)
        def _(j=j):
            gln_o[:, 0:blk] = total[:, bp * j : bp * j + blk]
    fin_forward_x("o")
    fin_forward_y("q")
    fin_forward_x("q")
    for name in ("p", "f", "o", "q"):
        fin_finish(name)
    for cond, make in ends:
        if cond is None:
            make().wait_send()
        else:
            pl.when(cond())(lambda make=make: make().wait_send())


def layer_call(dim, ff, tokens, cot, w_qkv, w_out, w_fc, w_proj, lengths, lnv):
    blk = dim // NZ
    bp = up16(blk)
    hb = bp // 2
    dp = NZ * bp
    nq = up128(3 * blk)
    rows = WAVES * SEQ
    vm, dma = pltpu.VMEM, pltpu.SemaphoreType.DMA
    big = (NB, SEQ, dp)
    scratch = [
        vm(big, BF), vm(big, BF), vm((WAVES, SEQ, dp), BF),
        vm((dp, nq), BF), vm((bp, dp), BF), vm((dp, dp), BF), vm((dp, dp), BF),
        vm(big, BF),
        vm((NB, SEQ, bp), BF), vm((NB, SEQ, bp), BF), vm((NB, SEQ, bp), BF),
        vm((NB, (HEADS // NT) * SEQ, SEQ), F32),
        vm((NB, SEQ, bp), BF),
        vm(big, BF),
        vm((2, WAVES, 2, SEQ, dp), BF), vm((2, WAVES, SEQ, dp), BF), vm((2, WAVES, SEQ, dp), BF),
        vm((WAVES, SEQ, dp), F32), vm((WAVES, SEQ, dp), F32),
        vm(big, BF), vm(big, BF), vm(big, BF),
        vm((NB, SEQ, bp), BF), vm((NB, SEQ, nq), BF),
        vm((dp, nq), BF), vm((bp, dp), BF), vm((dp, dp), BF), vm((dp, dp), BF),
        vm((NZ, hb, nq), BF), vm((1, hb, dp), BF), vm((NZ, hb, dp), BF), vm((NZ, hb, dp), BF),
        vm((NZ + 1, hb, nq), BF), vm((2, hb, dp), BF), vm((NZ + 1, hb, dp), BF), vm((NZ + 1, hb, dp), BF),
        vm((NZ, 8, up128(blk)), F32), vm((8, dp), F32), vm((NB, 8, SEQ), F32),
        vm((8, dp), F32), vm((3, 8, dp), F32), vm((3, 8, dp), F32),
        dma((6,)), dma((17, 5)), dma((4, 17)), dma((4, 16)), dma((8, 6)), dma((8, 4)), dma((18,)),
    ]
    hbm = pl.BlockSpec(memory_space=pl.ANY)
    inv = pl.BlockSpec(memory_space=pltpu.VMEM)
    shape = jax.ShapeDtypeStruct

    def body(*refs):
        layer_kernel(dim, ff, *refs)

    return pl.pallas_call(
        body,
        out_shape=(
            shape((rows, dim), BF), shape((rows, dim), BF),
            shape((8, hb, nq), BF), shape((2, hb, dp), BF), shape((8, hb, dp), BF), shape((8, hb, dp), BF),
            shape((8, up128(blk)), F32),
        ),
        in_specs=[hbm] * 6 + [pl.BlockSpec(memory_space=pltpu.SMEM), inv],
        out_specs=(inv, inv, hbm, hbm, hbm, hbm, inv),
        scratch_shapes=scratch,
        compiler_params=pltpu.CompilerParams(
            collective_id=0, has_side_effects=True, vmem_limit_bytes=67043328
        ),
    )(tokens, cot, w_qkv, w_out, w_fc, w_proj, lengths, lnv)


def sum_boxes(value, wide):
    total = value
    for k in range(1, wide // 8):
        total = total + lax.ppermute(value, "wide", [(i, (i + 8 * k) % wide) for i in range(wide)])
    return total


def solution(mesh):
    wide, narrow = mesh.shape["wide"], mesh.shape["narrow"]
    assert narrow == NZ and wide % 8 == 0

    def shards(tokens, lengths, ln1_gain, ln1_bias, w_qkv, w_out, ln2_gain, ln2_bias, w_fc, w_proj, cotangent):
        cells, seq, dim = tokens.shape
        assert cells == WAVES and seq == SEQ
        ff = w_fc.shape[1]
        blk = dim // NZ
        bp = up16(blk)
        lnv = jnp.pad(
            jnp.stack([ln1_gain, ln1_bias, ln2_gain, ln2_bias]).astype(F32), ((0, 4), (0, up128(blk) - blk))
        )
        res, gtok, gq, go, gf, gp, gln = layer_call(
            dim, ff, tokens.reshape(cells * seq, dim), cotangent.reshape(cells * seq, dim),
            w_qkv, w_out, w_fc, w_proj, lengths, lnv,
        )
        gq = gq.reshape(NT, bp, gq.shape[2])[:, :blk, : 3 * blk].astype(F32)
        gq = gq.reshape(NT, blk, 3, blk).transpose(1, 2, 0, 3).reshape(blk, 3 * dim)
        go = go.reshape(bp, NZ, bp)[:blk, :, :blk].astype(F32).reshape(blk, dim)
        gf = gf.reshape(NT, bp, NZ, bp)[:, :blk, :, :blk].astype(F32)
        gf = gf.transpose(1, 2, 0, 3).reshape(blk, ff)
        gp = gp.reshape(NT, bp, NZ, bp)[:, :blk, :, :blk].astype(F32).reshape(NT * blk, dim)
        grads = [sum_boxes(g, wide) for g in (gq, go, gf, gp, gln)]
        gq, go, gf, gp, gln = grads
        return (
            res.reshape(cells, seq, dim), gtok.reshape(cells, seq, dim),
            gln[0, :blk], gln[1, :blk], gq, go, gln[2, :blk], gln[3, :blk], gf, gp,
        )

    rows = P(("wide", "narrow"), None, None)
    vec, mat = P("narrow"), P("narrow", None)
    return jax.shard_map(
        shards,
        mesh=mesh,
        in_specs=(rows, P(("wide", "narrow")), vec, vec, mat, mat, vec, vec, mat, mat, rows),
        out_specs=(rows, rows, vec, vec, mat, mat, vec, vec, mat, mat),
        check_vma=False,
    )
```

```python
import math

import jax
import jax.numpy as jnp
from jax import lax
from jax.experimental import pallas as pl
from jax.experimental.pallas import tpu as pltpu
from jax.sharding import PartitionSpec as P

HEADS = 20
EPS = 1e-05
MASKED = -1e30
BF, F32 = jnp.bfloat16, jnp.float32
MESH = pl.DeviceIdType.MESH

NZ = 4
NT = 4
WAVES = 2
SEQ = 128
NB = NT * WAVES
GELU_C = math.sqrt(2.0 / math.pi)
GELU_A = 0.044715


def up16(n):
    return -(-n // 16) * 16


def up128(n):
    return -(-n // 128) * 128


def nn(a, b):
    return lax.dot_general(a, b, (((1,), (0,)), ((), ())), preferred_element_type=F32)


def nt(a, b):
    return lax.dot_general(a, b, (((1,), (1,)), ((), ())), preferred_element_type=F32)


def tn(a, b):
    return lax.dot_general(a, b, (((0,), (0,)), ((), ())), preferred_element_type=F32)


def layer_kernel(
    dim, ff,
    tok_h, dy_h, wq_h, wo_h, wf_h, wp_h, len_s, g1_i, b1_i, g2_i, b2_i,
    res_o, gtok_o, gq_o, go_o, gf_o, gp_o, gln_o,
    tok, dys, xown, wq, wo, wf, wp, first, qs, ks, vs, pm, att, part, ra, sb, rb, mix, dmix,
    sec, act, gel, datt, dqkv, gq, go, gf, gp, yq, yo, yf, yp, zq, zo, zf, zp,
    lnv, lnr, vec, lens, lg, lr, lz,
    raw_sem, ag_sem, rs_sem, fin_sem, xs_sem, xa_sem, ln_sem,
):
    blk = dim // NZ
    bp = up16(blk)
    hb = bp // 2
    dp = NZ * bp
    nq = wq.shape[1]
    head = dim // HEADS
    nh = HEADS // NT
    inv_dim = 1.0 / dim
    scale = head ** (-0.5)

    w = lax.axis_index("wide")
    z = lax.axis_index("narrow")
    c = lax.rem(w, 2)
    x = lax.rem(w // 2, 2)
    y = lax.rem(w // 4, 2)
    t = 2 * x + c
    core_dev = (w + 1 - 2 * c, z)
    x_dev = (w + 2 - 4 * x, z)
    y_dev = (w + 4 - 8 * y, z)
    up_dev = (w, z + 1)
    down_dev = (w, z - 1)

    ends = []

    def remote(src, dst, ssem, rsem, dev):
        return pltpu.make_async_remote_copy(
            src_ref=src, dst_ref=dst, send_sem=ssem, recv_sem=rsem, device_id=dev, device_id_type=MESH
        )

    def send(make, cond=None, track=True):
        if cond is None:
            make().start()
        else:
            pl.when(cond())(lambda: make().start())
        if track:
            ends.append((cond, make))

    def both(a, b):
        return jnp.logical_and(a, b)

    lane = lax.broadcasted_iota(jnp.int32, (1, dp), 1)
    live = lax.rem(lane, bp) < blk
    livef = live.astype(F32)

    barrier = pltpu.get_barrier_semaphore()
    others = [(w, lax.rem(z + k, NZ)) for k in range(1, NZ)]
    for dev in [core_dev, x_dev, y_dev] + others:
        pl.semaphore_signal(barrier, inc=1, device_id=dev, device_id_type=MESH)
    pl.semaphore_wait(barrier, 3 + len(others))

    def rows_of(s, yy, r0=0, nr=None):
        return pl.ds(pl.multiple_of(bp * s + hb * yy + r0, 16), hb if nr is None else nr)

    q_pieces = [(0, 80), (80, hb - 80)]
    gathers = {
        "q": (wq, 0, q_pieces),
        "f": (wf, 4 * len(q_pieces), [(0, hb)]),
        "p": (wp, 4 * len(q_pieces) + 4, [(0, hb)]),
        "o": (wo, 4 * len(q_pieces) + 8, [(0, hb)]),
    }

    def ag_view(name, s, yy, piece):
        ref, base, pieces = gathers[name]
        r0, nr = pieces[piece]
        if name == "o":
            return ref.at[rows_of(0, yy, r0, nr)]
        return ref.at[rows_of(s, yy, r0, nr)]

    def ag_id(name, s, piece):
        ref, base, pieces = gathers[name]
        return base if name == "o" else base + 4 * piece + s

    def ag_z(name, s, piece, up):
        v = ag_view(name, s, y, piece)
        i = ag_id(name, s, piece)
        return remote(v, v, ag_sem.at[i, 0 if up else 1], ag_sem.at[i, 2], up_dev if up else down_dev)

    def ag_y(name, s, yy, piece):
        v = ag_view(name, s, yy, piece)
        i = ag_id(name, s, piece)
        return remote(v, v, ag_sem.at[i, 3], ag_sem.at[i, 4], y_dev)

    def ag_start(name):
        for piece in range(len(gathers[name][2])):
            def own():
                return (t == z) if name == "o" else (z >= 0)

            send(lambda p=piece: ag_z(name, z, p, True), lambda: both(own(), z < NZ - 1))
            send(lambda p=piece: ag_z(name, z, p, False), lambda: both(own(), z > 0))

    def ag_forward(name, k):
        for piece in range(len(gathers[name][2])):
            for up in (True, False):
                s = z - k if up else z + k
                ok = (z >= k) if up else (z + k <= NZ - 1)
                if name == "o":
                    ok = t == s
                more = (z < NZ - 1) if up else (z > 0)
                pl.when(ok)(lambda s=s, p=piece, u=up: ag_z(name, s, p, u).wait_recv())
                send(lambda s=s, p=piece, u=up: ag_z(name, s, p, u), lambda ok=ok, more=more: both(ok, more))
                send(lambda s=s, p=piece: ag_y(name, s, y, p), lambda ok=ok: ok)

    def ag_finish(name):
        for piece in range(len(gathers[name][2])):
            if name == "o":
                pl.when(z != t)(lambda p=piece: ag_y(name, 0, 1 - y, p).wait_recv())
            else:
                for s in range(NZ):
                    pl.when(z != s)(lambda s=s, p=piece: ag_y(name, s, 1 - y, p).wait_recv())

    def blk_of(s, cc, xx):
        return s * NT + cc * 2 + xx

    def xg(ref, e, s, kind):
        i = 2 * e + s
        if kind == "x":
            v = ref.at[blk_of(s, c, x)]
            return remote(v, v, xs_sem.at[i, 0], xs_sem.at[i, 1], x_dev)
        if kind == "own":
            v = ref.at[blk_of(s, c, x)]
            return remote(v, v, xs_sem.at[i, 2], xs_sem.at[i, 3], core_dev)
        v = ref.at[blk_of(s, c, 1 - x)]
        return remote(v, v, xs_sem.at[i, 4], xs_sem.at[i, 5], core_dev)

    def xg_start(ref, e, s, track=True):
        send(lambda: xg(ref, e, s, "x"), track=track)
        send(lambda: xg(ref, e, s, "own"), track=track)

    def xg_forward(ref, e, s, track=True):
        xg(ref, e, s, "x").wait_recv()
        send(lambda: xg(ref, e, s, "fwd"), track=track)

    def xg_finish(ref, e, s):
        xg(ref, e, s, "own").wait_recv()
        xg(ref, e, s, "fwd").wait_recv()

    def xg_sent(ref, e, s):
        for kind in ("x", "own", "fwd"):
            xg(ref, e, s, kind).wait_send()

    def ex_a(e, s):
        i = 2 * e + s
        return remote(
            part.at[pl.ds(s * NT + (1 - c) * 2, 2)], ra.at[int(e == 1), s],
            xa_sem.at[i, 0], xa_sem.at[i, 1], core_dev,
        )

    def ex_b(e, s):
        i = 2 * e + s
        return remote(sb.at[int(e == 1), s], rb.at[int(e == 1), s], xa_sem.at[i, 2], xa_sem.at[i, 3], x_dev)

    def ex_relay(e, s):
        ex_a(e, s).wait_recv()
        sb[int(e == 1), s] = (
            part[blk_of(s, c, 1 - x)].astype(F32) + ra[int(e == 1), s, 1 - x].astype(F32)
        ).astype(BF)
        ex_b(e, s).start()

    def ex_sum(e, s):
        ex_b(e, s).wait_recv()
        return (
            part[blk_of(s, c, x)].astype(F32)
            + ra[int(e == 1), s, x].astype(F32)
            + rb[int(e == 1), s].astype(F32)
        )

    def ex_sent(e):
        for s in range(WAVES):
            ex_a(e, s).wait_send()
            ex_b(e, s).wait_send()

    reduces = {"q": (gq, yq, zq, 0), "f": (gf, yf, zf, 1), "p": (gp, yp, zp, 2), "o": (go, yo, zo, 3)}

    def rs_y(name, d):
        g, yr, zr, i = reduces[name]
        if name == "o":
            return remote(g.at[rows_of(0, 1 - y)], yr.at[0], rs_sem.at[i, 0], rs_sem.at[i, 4], y_dev)
        return remote(g.at[rows_of(d, 1 - y)], yr.at[d], rs_sem.at[i, d], rs_sem.at[i, 4 + d], y_dev)

    def rs_z(name, d, slot, up):
        g, yr, zr, i = reduces[name]
        dd = 0 if name == "o" else d
        return remote(yr.at[dd], zr.at[slot], rs_sem.at[i, 8 + dd], rs_sem.at[i, 12 + slot], up_dev if up else down_dev)

    def add_up(dst, srcs):
        step = 48

        def body(j, carry):
            r = pl.ds(pl.multiple_of(j * step, step), step)
            total = srcs[0][r, :].astype(F32)
            for src in srcs[1:]:
                total = total + src[r, :].astype(F32)
            dst[r, :] = total.astype(BF)
            return carry

        lax.fori_loop(0, hb // step, body, 0)

    def rs_start(name, dests=(3, 0, 2, 1)):
        for d in (0,) if name == "o" else dests:
            send(lambda d=d: rs_y(name, d))

    def rs_stage(name, d, j):
        g, yr, zr, i = reduces[name]

        def side(pos, up):
            def run():
                rs_y(name, d).wait_recv()
                own = g.at[rows_of(0 if name == "o" else d, y)]
                mine = yr.at[0 if name == "o" else d]
                srcs = [own, mine]
                slot = 0 if name == "o" else d
                if j > 0:
                    rs_z(name, d, slot, up).wait_recv()
                    srcs.append(zr.at[slot])
                add_up(mine, srcs)

            nxt = pos + 1 if up else pos - 1
            if name == "o":
                last = t == nxt
                cond = both(z == pos, (t > pos) if up else (t < pos))
                pl.when(cond)(run)
                if up:
                    send(lambda: rs_z(name, 0, 1, True), lambda: both(cond, last))
                    send(lambda: rs_z(name, 0, 0, True), lambda: both(cond, jnp.logical_not(last)))
                else:
                    send(lambda: rs_z(name, 0, 0, False), lambda: cond)
            else:
                cond = z == pos
                pl.when(cond)(run)
                slot = NZ if (up and nxt == d) else d
                send(lambda: rs_z(name, d, slot, up), lambda: cond)

        if name == "o":
            if j < NZ - 1:
                side(j, True)
                side(NZ - 1 - j, False)
            return
        if j < d:
            side(j, True)
        if NZ - 1 - j > d:
            side(NZ - 1 - j, False)

    def rs_final(name):
        g, yr, zr, i = reduces[name]
        out = name == "o"
        me = 0 if out else z
        here = (t == z) if out else (z >= 0)
        above = 0 if out else z
        below = 1 if out else NZ

        def run(has_above, has_below):
            def go_():
                rs_y(name, me).wait_recv()
                srcs = [g.at[rows_of(me, y)], yr.at[me]]
                if has_above:
                    rs_z(name, me, above, True).wait_recv()
                    srcs.append(zr.at[above])
                if has_below:
                    rs_z(name, me, below, True).wait_recv()
                    srcs.append(zr.at[below])
                add_up(yr.at[me], srcs)
            return go_

        pl.when(both(here, z == 0))(run(True, False))
        pl.when(both(here, z == NZ - 1))(run(False, True))
        pl.when(both(here, both(z > 0, z < NZ - 1)))(run(True, True))

    outs = {"q": gq_o, "f": gf_o, "p": gp_o, "o": go_o}

    def fin_view(name, tt, yy):
        return outs[name].at[yy] if name == "o" else outs[name].at[tt * 2 + yy]

    def fin_copy(name, src, tt, yy, k, dev):
        i = reduces[name][3]
        slot = yy if name == "o" else tt * 2 + yy
        return remote(src, fin_view(name, tt, yy), fin_sem.at[i, k], fin_sem.at[i, 8 + slot], dev)

    def own_block(name):
        yr = reduces[name][1]
        return yr.at[0] if name == "o" else yr.at[z]

    def keep_own(name):
        return pltpu.make_async_copy(own_block(name), fin_view(name, t, y), fin_sem.at[reduces[name][3], 7])

    tx = 2 * (1 - x) + c

    def fin_start(name):
        here = (lambda: t == z) if name == "o" else None
        if here is None:
            keep_own(name).start()
        else:
            pl.when(here())(lambda: keep_own(name).start())
        send(lambda: fin_copy(name, own_block(name), t, y, 0, y_dev), here)
        send(lambda: fin_copy(name, own_block(name), t, y, 1, x_dev), here)
        send(lambda: fin_copy(name, own_block(name), t, y, 2, core_dev), here)

    def fin_wait(name, tt, yy):
        fin_copy(name, fin_view(name, tt, yy), tt, yy, 0, core_dev).wait_recv()

    def fin_forward_y(name):
        here = (t == z) if name == "o" else (z >= 0)
        pl.when(here)(lambda: fin_wait(name, t, 1 - y))
        v = fin_view(name, t, 1 - y)
        send(lambda: fin_copy(name, v, t, 1 - y, 3, x_dev), lambda: here)
        send(lambda: fin_copy(name, v, t, 1 - y, 4, core_dev), lambda: here)

    def fin_forward_x(name):
        here = (tx == z) if name == "o" else (z >= 0)
        for k, yy in ((5, y), (6, 1 - y)):
            pl.when(here)(lambda yy=yy: fin_wait(name, tx, yy))
            send(lambda k=k, yy=yy: fin_copy(name, fin_view(name, tx, yy), tx, yy, k, core_dev), lambda: here)

    def fin_finish(name):
        if name == "o":
            here = lax.rem(z, 2) != c
            for yy in range(2):
                pl.when(here)(lambda yy=yy: fin_wait(name, 0, yy))
            pl.when(t == z)(lambda: keep_own(name).wait())
        else:
            for xx in range(2):
                for yy in range(2):
                    fin_wait(name, 2 * xx + (1 - c), yy)
            keep_own(name).wait()

    base = pl.multiple_of(bp * z, 16)

    def prepare(rq, rt, ro, rd, turned):
        loads = [
            pltpu.make_async_copy(wq_h, rq, raw_sem.at[0]),
            pltpu.make_async_copy(tok_h, rt, raw_sem.at[1]),
            pltpu.make_async_copy(wo_h, ro, raw_sem.at[2]),
            pltpu.make_async_copy(dy_h, rd, raw_sem.at[3]),
        ]
        for load in loads:
            load.start()
        lnv[...] = jnp.zeros_like(lnv)
        for k, ref in enumerate((g1_i, b1_i, g2_i, b2_i)):
            lnv[k : k + 1, 0:blk] = ref[...].astype(F32).reshape(1, blk)
        lnr[z] = lnv[...]
        for k in range(1, NZ):
            send(lambda k=k: remote(lnv, lnr.at[z], ln_sem.at[k - 1], ln_sem.at[2 + k], others[k - 1]))

        loads[0].wait()
        wq[pl.ds(base, bp), :] = jnp.zeros((bp, nq), BF)
        for k in range(NT):
            @pl.when(t == k)
            def _(k=k):
                for j in range(3):
                    wq[pl.ds(base, blk), blk * j : blk * (j + 1)] = rq[:, dim * j + blk * k : dim * j + blk * (k + 1)]
        ag_start("q")

        turned[...] = jnp.zeros_like(turned)

        def spread(dst, src):
            for j in range(NZ):
                turned[bp * j : bp * j + blk, :] = src[blk * j : blk * (j + 1), :]
            dst[...] = turned[...].T

        loads[1].wait()
        for s in range(WAVES):
            spread(xown.at[s], rt.at[s])
            sent = jnp.where(lane == blk, len_s[s].astype(F32), xown[s].astype(F32))
            tok[blk_of(s, c, x)] = sent.astype(BF)
            xg_start(tok, 0, s, track=False)
        loads[2].wait()

        @pl.when(t == z)
        def _():
            wo[...] = jnp.zeros_like(wo)
            for j in range(NZ):
                wo[0:blk, bp * j : bp * j + blk] = ro[:, blk * j : blk * (j + 1)]
        ag_start("o")
        loads[3].wait()
        for s in range(WAVES):
            spread(dys.at[blk_of(s, c, x)], rd.at[s])
            xg_start(dys, 1, s)

    def prepare_mlp(rf, rp):
        loads = [
            pltpu.make_async_copy(wf_h, rf, raw_sem.at[4]),
            pltpu.make_async_copy(wp_h.at[pl.ds(pl.multiple_of(blk * t, 8), blk)], rp, raw_sem.at[5]),
        ]
        for load in loads:
            load.start()
        loads[0].wait()
        wf[pl.ds(base, bp), :] = jnp.zeros((bp, dp), BF)
        for k in range(NT):
            @pl.when(t == k)
            def _(k=k):
                for j in range(NZ):
                    lo = (ff // NZ) * j + blk * k
                    wf[pl.ds(base, blk), bp * j : bp * j + blk] = rf[:, lo : lo + blk]
        loads[1].wait()
        wp[pl.ds(base, bp), :] = jnp.zeros((bp, dp), BF)
        for j in range(NZ):
            wp[pl.ds(base, blk), bp * j : bp * j + blk] = rp[:, blk * j : blk * (j + 1)]

    pl.run_scoped(
        prepare,
        pltpu.VMEM((blk, 3 * dim), BF),
        pltpu.VMEM((WAVES, dim, SEQ), BF),
        pltpu.VMEM((blk, dim), BF),
        pltpu.VMEM((WAVES, dim, SEQ), BF),
        pltpu.VMEM((dp, SEQ), BF),
    )
    pl.run_scoped(prepare_mlp, pltpu.VMEM((blk, ff), BF), pltpu.VMEM((blk, dim), BF))

    for k in range(1, NZ):
        remote(lnv, lnr.at[lax.rem(z + NZ - k, NZ)], ln_sem.at[k - 1], ln_sem.at[2 + k], others[k - 1]).wait_recv()
    vec[...] = jnp.zeros_like(vec)
    for j in range(NZ):
        vec[:, bp * j : bp * j + blk] = lnr[j, :, 0:blk]
    lg[...] = jnp.zeros_like(lg)
    dqkv[...] = jnp.zeros_like(dqkv)

    def stats(rows):
        mean = jnp.sum(rows, axis=-1, keepdims=True) * inv_dim
        cen = (rows - mean) * livef
        inv = lax.rsqrt(jnp.sum(cen * cen, axis=-1, keepdims=True) * inv_dim + EPS)
        return cen * inv, inv

    def norm_back(e, n, inv):
        me = jnp.sum(e, axis=-1, keepdims=True) * inv_dim
        mn = jnp.sum(e * n, axis=-1, keepdims=True) * inv_dim
        return inv * (e - me - n * mn) * livef

    def ln_first(s):
        def body(i, carry):
            b = s * NT + i
            raw = tok[b].astype(F32)
            lens[b] = jnp.broadcast_to(raw[0:8, blk : blk + 1], (8, SEQ))
            n, inv = stats(raw * livef)
            first[b] = (n * vec[0:1, :] + vec[1:2, :]).astype(BF)
            return carry
        lax.fori_loop(0, NT, body, 0)

    lane_h = lax.broadcasted_iota(jnp.int32, (1, bp), 1)
    head_masks = [(lane_h >= head * h) & (lane_h < head * (h + 1)) for h in range(nh)]

    def stack_heads(v):
        zero = jnp.zeros_like(v)
        return jnp.concatenate([jnp.where(m, v, zero) for m in head_masks], axis=0)

    def side_by_side(v):
        return jnp.concatenate([v[SEQ * h : SEQ * (h + 1)] for h in range(nh)], axis=1)

    def project(s):
        def body(i, carry):
            b = s * NT + i * 2
            rows = first[pl.ds(b, 2)].reshape(2 * SEQ, dp)
            out = nn(rows, wq[...])
            for j, ref in enumerate((qs, ks, vs)):
                ref[pl.ds(b, 2)] = out[:, blk * j : blk * j + bp].astype(BF).reshape(2, SEQ, bp)
            return carry
        lax.fori_loop(0, 2, body, 0)

    def attend(s):
        q_pos = lax.broadcasted_iota(jnp.int32, (SEQ, SEQ), 0)
        k_pos = lax.broadcasted_iota(jnp.int32, (SEQ, SEQ), 1)

        def body(i, carry):
            b = s * NT + i
            scores = nt(stack_heads(qs[b]), ks[b]) * scale
            ok = (k_pos <= q_pos) & (k_pos.astype(F32) < lens[b, 0:1, :])
            bias = jnp.concatenate([ok.astype(F32)] * nh, axis=0) > 0.5
            scores = jnp.where(bias, scores, MASKED)
            top = jnp.max(scores, axis=-1, keepdims=True)
            ex = jnp.exp(scores - top)
            prob = ex / jnp.sum(ex, axis=-1, keepdims=True)
            pm[b] = prob
            out = nn(side_by_side(prob.astype(BF)), stack_heads(vs[b]))
            att[b] = out.astype(BF)
            return carry
        lax.fori_loop(0, NT, body, 0)

    def matmul_part(src, weight, s, transposed):
        width = src.shape[2]

        def body(i, carry):
            b = s * NT + i * 2
            rows = src[pl.ds(b, 2)].reshape(2 * SEQ, width)
            out = nt(rows, weight[...]) if transposed else nn(rows, weight[...])
            part[pl.ds(b, 2)] = out.astype(BF).reshape(2, SEQ, dp)
            return carry
        lax.fori_loop(0, 2, body, 0)

    ag_forward("q", 1)
    xg_forward(tok, 0, 0, track=False)
    ag_forward("q", 2)
    ag_start("f")
    ag_forward("o", 1)
    xg_finish(tok, 0, 0)
    ln_first(0)
    xg_forward(tok, 0, 1, track=False)
    ag_forward("q", 3)
    xg_finish(tok, 0, 1)
    ln_first(1)
    ag_forward("o", 2)
    ag_start("p")
    ag_forward("f", 1)
    ag_forward("o", 3)
    ag_finish("q")
    project(0)
    attend(0)
    ag_finish("o")
    matmul_part(att, wo, 0, False)
    ex_a(0, 0).start()
    ag_forward("f", 2)
    project(1)
    attend(1)
    matmul_part(att, wo, 1, False)
    ex_a(0, 1).start()
    ex_relay(0, 0)
    ag_forward("f", 3)
    ag_forward("p", 1)
    ex_relay(0, 1)
    xg_forward(dys, 1, 0)
    xg_forward(dys, 1, 1)

    def mid(s):
        rows = xown[s].astype(F32) + ex_sum(0, s)
        mix[s] = rows
        n, inv = stats(rows)
        sec[blk_of(s, c, x)] = (n * vec[2:3, :] + vec[3:4, :]).astype(BF)
        xg_start(sec, 2, s)

    mid(0)
    mid(1)
    ag_forward("p", 2)
    xg_forward(sec, 2, 0)
    xg_forward(sec, 2, 1)
    ag_forward("p", 3)
    for s in range(WAVES):
        xg_sent(tok, 0, s)
    ex_sent(0)
    ag_finish("f")

    def expand(s):
        def body(i, carry):
            b = s * NT + i * 2
            rows = sec[pl.ds(b, 2)].reshape(2 * SEQ, dp)
            pre = nn(rows, wf[...])
            sq = pre * pre
            th = jnp.tanh(GELU_C * (pre + GELU_A * (pre * sq)))
            half = 0.5 * (1.0 + th)
            act[pl.ds(b, 2)] = (pre * half).astype(BF).reshape(2, SEQ, dp)
            slope = half + (0.5 * GELU_C) * pre * (1.0 - th * th) * (1.0 + (3.0 * GELU_A) * sq)
            gel[pl.ds(b, 2)] = slope.astype(BF).reshape(2, SEQ, dp)
            return carry
        lax.fori_loop(0, 2, body, 0)

    for s in range(WAVES):
        xg_finish(sec, 2, s)
        expand(s)
    for s in range(WAVES):
        xg_finish(dys, 1, s)

    def grad_of(dst, left, right):
        step = 384
        rows = NB * SEQ

        def body(j, carry):
            cols = pl.ds(pl.multiple_of(j * step, step), step)
            out = tn(left[:, :, cols].reshape(rows, step), right[...].reshape(rows, right.shape[2]))
            dst[cols, :] = out.astype(BF)
            return carry
        lax.fori_loop(0, dp // step, body, 0)

    grad_of(gp, act, dys)
    rs_start("p")
    ag_finish("p")

    def back_act(s):
        def body(i, carry):
            b = s * NT + i * 2
            d_act = nt(dys[pl.ds(b, 2)].reshape(2 * SEQ, dp), wp[...])
            slope = gel[pl.ds(b, 2)].reshape(2 * SEQ, dp).astype(F32)
            gel[pl.ds(b, 2)] = (d_act * slope).astype(BF).reshape(2, SEQ, dp)
            return carry
        lax.fori_loop(0, 2, body, 0)

    for s in range(WAVES):
        back_act(s)
        matmul_part(gel, wf, s, True)
        ex_a(2, s).start()
    rs_stage("p", 3, 0)
    rs_stage("p", 0, 0)
    ex_relay(2, 0)
    ex_relay(2, 1)
    grad_of(gf, sec, gel)
    rs_start("f")
    for d in (2, 1):
        rs_stage("p", d, 0)
    for d in (3, 0):
        rs_stage("p", d, 1)

    def back_mid(s):
        d2 = ex_sum(2, s)
        n, inv = stats(mix[s])
        lg[2:3, :] = lg[2:3, :] + jnp.sum(d2 * n, axis=0, keepdims=True)
        lg[3:4, :] = lg[3:4, :] + jnp.sum(d2, axis=0, keepdims=True)
        rows = dys[blk_of(s, c, x)].astype(F32) + norm_back(d2 * vec[2:3, :], n, inv)
        dmix[s] = rows
        tok[blk_of(s, c, x)] = rows.astype(BF)
        xg_start(tok, 3, s)

    back_mid(0)
    back_mid(1)
    ex_sent(2)
    for d in (2, 1):
        rs_stage("p", d, 1)
    for d in (3, 0):
        rs_stage("p", d, 2)
    for s in range(WAVES):
        matmul_part(act, wp, s, False)
        ex_a(1, s).start()
    xg_forward(tok, 3, 0)
    xg_forward(tok, 3, 1)
    ex_relay(1, 0)
    ex_relay(1, 1)
    rs_final("p")
    fin_start("p")

    def back_attend(s):
        def proj(i, carry):
            b = s * NT + i * 2
            out = nt(tok[pl.ds(b, 2)].reshape(2 * SEQ, dp), wo[...])
            datt[pl.ds(b, 2)] = out.astype(BF).reshape(2, SEQ, bp)
            return carry
        lax.fori_loop(0, 2, proj, 0)

        def body(i, carry):
            b = s * NT + i
            d_out = stack_heads(datt[b])
            prob = pm[b]
            d_prob = nt(d_out, vs[b])
            total = jnp.sum(prob * d_prob, axis=-1, keepdims=True)
            d_scores = (prob * (d_prob - total)).astype(BF)
            dqkv[b, :, 0:bp] = (nn(side_by_side(d_scores), stack_heads(ks[b])) * scale).astype(BF)
            dqkv[b, :, blk : blk + bp] = (tn(d_scores, stack_heads(qs[b])) * scale).astype(BF)
            dqkv[b, :, 2 * blk : 2 * blk + bp] = tn(prob.astype(BF), d_out).astype(BF)
            return carry
        lax.fori_loop(0, NT, body, 0)

    xg_finish(tok, 3, 0)
    back_attend(0)
    for d in (3, 0, 2, 1):
        rs_stage("f", d, 0)
    xg_finish(tok, 3, 1)
    back_attend(1)
    rows_all = NB * SEQ
    go[...] = tn(att[...].reshape(rows_all, bp), tok[...].reshape(rows_all, dp)).astype(BF)
    rs_start("o")
    grad_of(gq, first, dqkv)
    rs_start("q")
    for d in (3, 0, 2, 1):
        rs_stage("f", d, 1)

    for s in range(WAVES):
        res_o[s] = (mix[s] + ex_sum(1, s)).astype(BF)
    ex_sent(1)
    for s in range(WAVES):
        matmul_part(dqkv, wq, s, True)
        ex_a(3, s).start()
    for d in (3, 0):
        rs_stage("f", d, 2)
    ex_relay(3, 0)
    ex_relay(3, 1)
    rs_final("f")
    fin_start("f")
    fin_forward_y("p")
    rs_stage("o", 0, 0)
    fin_forward_x("p")
    rs_stage("o", 0, 1)
    for d in (3, 0, 2, 1):
        rs_stage("q", d, 0)

    def back_first(s):
        d1 = ex_sum(3, s)
        n, inv = stats(xown[s].astype(F32))
        lg[0:1, :] = lg[0:1, :] + jnp.sum(d1 * n, axis=0, keepdims=True)
        lg[1:2, :] = lg[1:2, :] + jnp.sum(d1, axis=0, keepdims=True)
        gtok_o[s] = (dmix[s] + norm_back(d1 * vec[0:1, :], n, inv)).astype(BF)

    back_first(0)
    back_first(1)
    ex_sent(3)
    rs_stage("o", 0, 2)
    for d in (3, 0, 2, 1):
        rs_stage("q", d, 1)
    rs_final("o")
    fin_start("o")
    fin_forward_y("f")
    fin_forward_x("f")

    for k, dev in enumerate((core_dev, x_dev, y_dev)):
        hop = remote(lg, lr.at[k], ln_sem.at[6 + 2 * k], ln_sem.at[7 + 2 * k], dev)
        hop.start()
        hop.wait()
        lg[...] = lg[...] + lr[k]
    for k in range(1, NZ):
        send(lambda k=k: remote(lg, lz.at[k - 1], ln_sem.at[11 + k], ln_sem.at[14 + k], others[k - 1]))
    for d in (3, 0):
        rs_stage("q", d, 2)
    rs_final("q")
    fin_start("q")
    fin_forward_y("o")
    for k in range(1, NZ):
        remote(lg, lz.at[k - 1], ln_sem.at[11 + k], ln_sem.at[14 + k], others[k - 1]).wait_recv()
    total = lg[...] + lz[0] + lz[1] + lz[2]
    for j in range(NZ):
        @pl.when(z == j)
        def _(j=j):
            gln_o[:, 0:blk] = total[:, bp * j : bp * j + blk]
    fin_forward_x("o")
    fin_forward_y("q")
    fin_forward_x("q")
    for name in ("p", "f", "o", "q"):
        fin_finish(name)
    for cond, make in ends:
        if cond is None:
            make().wait_send()
        else:
            pl.when(cond())(lambda make=make: make().wait_send())


def layer_call(dim, ff, tokens, cot, w_qkv, w_out, w_fc, w_proj, lengths, norms):
    blk = dim // NZ
    bp = up16(blk)
    hb = bp // 2
    dp = NZ * bp
    nq = up128(3 * blk)
    vm, dma = pltpu.VMEM, pltpu.SemaphoreType.DMA
    big = (NB, SEQ, dp)
    scratch = [
        vm(big, BF), vm(big, BF), vm((WAVES, SEQ, dp), BF),
        vm((dp, nq), BF), vm((bp, dp), BF), vm((dp, dp), BF), vm((dp, dp), BF),
        vm(big, BF),
        vm((NB, SEQ, bp), BF), vm((NB, SEQ, bp), BF), vm((NB, SEQ, bp), BF),
        vm((NB, (HEADS // NT) * SEQ, SEQ), F32),
        vm((NB, SEQ, bp), BF),
        vm(big, BF),
        vm((2, WAVES, 2, SEQ, dp), BF), vm((2, WAVES, SEQ, dp), BF), vm((2, WAVES, SEQ, dp), BF),
        vm((WAVES, SEQ, dp), F32), vm((WAVES, SEQ, dp), F32),
        vm(big, BF), vm(big, BF), vm(big, BF),
        vm((NB, SEQ, bp), BF), vm((NB, SEQ, nq), BF),
        vm((dp, nq), BF), vm((bp, dp), BF), vm((dp, dp), BF), vm((dp, dp), BF),
        vm((NZ, hb, nq), BF), vm((1, hb, dp), BF), vm((NZ, hb, dp), BF), vm((NZ, hb, dp), BF),
        vm((NZ + 1, hb, nq), BF), vm((2, hb, dp), BF), vm((NZ + 1, hb, dp), BF), vm((NZ + 1, hb, dp), BF),
        vm((8, up128(blk)), F32), vm((NZ, 8, up128(blk)), F32), vm((8, dp), F32), vm((NB, 8, SEQ), F32),
        vm((8, dp), F32), vm((3, 8, dp), F32), vm((3, 8, dp), F32),
        dma((6,)), dma((17, 5)), dma((4, 17)), dma((4, 16)), dma((8, 6)), dma((8, 4)), dma((18,)),
    ]
    hbm = pl.BlockSpec(memory_space=pl.ANY)
    inv = pl.BlockSpec(memory_space=pltpu.VMEM)
    shape = jax.ShapeDtypeStruct

    def body(*refs):
        layer_kernel(dim, ff, *refs)

    return pl.pallas_call(
        body,
        out_shape=(
            shape((WAVES, SEQ, dp), BF), shape((WAVES, SEQ, dp), BF),
            shape((8, hb, nq), BF), shape((2, hb, dp), BF), shape((8, hb, dp), BF), shape((8, hb, dp), BF),
            shape((8, up128(blk)), F32),
        ),
        in_specs=[hbm] * 6 + [pl.BlockSpec(memory_space=pltpu.SMEM)] + [inv] * 4,
        out_specs=(inv, inv, hbm, hbm, hbm, hbm, inv),
        scratch_shapes=scratch,
        compiler_params=pltpu.CompilerParams(
            collective_id=0, has_side_effects=True, vmem_limit_bytes=67043328
        ),
    )(tokens, cot, w_qkv, w_out, w_fc, w_proj, lengths, *norms)


def finish_kernel(dim, ff, res, gtok, gq, go, gf, gp, gln, res_o, gtok_o, gq_o, go_o, gf_o, gp_o, *norms_o):
    blk = dim // NZ
    bp = up16(blk)
    for j in range(NZ):
        there = slice(bp * j, bp * j + blk)
        go_o[:, blk * j : blk * (j + 1)] = go[:, there].astype(F32)
        for t in range(NT):
            gp_o[t, :, blk * j : blk * (j + 1)] = gp[t, :, there].astype(F32)
            lo = (ff // NZ) * j + blk * t
            gf_o[:, lo : lo + blk] = gf[t, :, there].astype(F32)
    for j in range(3):
        for t in range(NT):
            lo = dim * j + blk * t
            gq_o[:, lo : lo + blk] = gq[t, :, blk * j : blk * (j + 1)].astype(F32)

    @pl.when(pl.program_id(0) == 0)
    def _():
        for k, ref in enumerate(norms_o):
            ref[...] = gln[k : k + 1, 0:blk].reshape(blk)
        for src, dst in ((res, res_o), (gtok, gtok_o)):
            for s in range(WAVES):
                turned = src[s].T
                for j in range(NZ):
                    dst[s, blk * j : blk * (j + 1), :] = turned[bp * j : bp * j + blk, :]


def finish_call(dim, ff, res, gtok, gq, go, gf, gp, gln):
    blk = dim // NZ
    bp = up16(blk)
    dp = NZ * bp
    nq = gq.shape[2]
    step = 56
    shape, spec = jax.ShapeDtypeStruct, pl.BlockSpec
    whole = spec(memory_space=pltpu.VMEM)
    quarters = lambda n: spec((NT, step, n), lambda i: (0, i, 0))
    lines = lambda n: spec((step, n), lambda i: (i, 0))
    return pl.pallas_call(
        lambda *refs: finish_kernel(dim, ff, *refs),
        grid=(blk // step,),
        in_specs=[whole, whole, quarters(nq), lines(dp), quarters(dp), quarters(dp), whole],
        out_specs=[whole, whole, lines(3 * dim), lines(dim), lines(ff), quarters(dim)] + [whole] * 4,
        out_shape=[
            shape((WAVES, dim, SEQ), BF), shape((WAVES, dim, SEQ), BF),
            shape((blk, 3 * dim), F32), shape((blk, dim), F32), shape((blk, ff), F32), shape((NT, blk, dim), F32),
        ] + [shape((blk,), F32)] * 4,
        compiler_params=pltpu.CompilerParams(vmem_limit_bytes=67043328),
    )(
        res, gtok, gq.reshape(NT, bp, nq), go.reshape(bp, dp), gf.reshape(NT, bp, dp), gp.reshape(NT, bp, dp), gln
    )


def sum_boxes(value, wide):
    total = value
    for k in range(1, wide // 8):
        total = total + lax.ppermute(value, "wide", [(i, (i + 8 * k) % wide) for i in range(wide)])
    return total


def solution(mesh):
    wide, narrow = mesh.shape["wide"], mesh.shape["narrow"]
    assert narrow == NZ and wide % 8 == 0

    def shards(tokens, lengths, ln1_gain, ln1_bias, w_qkv, w_out, ln2_gain, ln2_bias, w_fc, w_proj, cotangent):
        cells, seq, dim = tokens.shape
        assert cells == WAVES and seq == SEQ
        ff = w_fc.shape[1]
        blk = dim // NZ
        bp = up16(blk)
        res, gtok, gq, go, gf, gp, gln = layer_call(
            dim, ff, tokens.transpose(0, 2, 1), cotangent.transpose(0, 2, 1),
            w_qkv, w_out, w_fc, w_proj, lengths, (ln1_gain, ln1_bias, ln2_gain, ln2_bias),
        )
        res, gtok, *grads = finish_call(dim, ff, res, gtok, gq, go, gf, gp, gln)
        gq, go, gf, gp, g1, b1, g2, b2 = [sum_boxes(g, wide) for g in grads]
        return (
            res.transpose(0, 2, 1), gtok.transpose(0, 2, 1), g1, b1, gq, go, g2, b2, gf, gp.reshape(ff // NZ, dim)
        )

    rows = P(("wide", "narrow"), None, None)
    vec, mat = P("narrow"), P("narrow", None)
    return jax.shard_map(
        shards,
        mesh=mesh,
        in_specs=(rows, P(("wide", "narrow")), vec, vec, mat, mat, vec, vec, mat, mat, rows),
        out_specs=(rows, rows, vec, vec, mat, mat, vec, vec, mat, mat),
        check_vma=False,
    )
```

```python
import math

import jax
import jax.numpy as jnp
from jax import lax
from jax.experimental import pallas as pl
from jax.experimental.pallas import tpu as pltpu
from jax.sharding import PartitionSpec as P

HEADS = 20
EPS = 1e-05
MASKED = -1e30
BF, F32 = jnp.bfloat16, jnp.float32
MESH = pl.DeviceIdType.MESH

NZ = 4
NT = 4
WAVES = 2
SEQ = 128
NB = NT * WAVES
GELU_C = math.sqrt(2.0 / math.pi)
GELU_A = 0.044715
ZFIRST = ("p",)


def up16(n):
    return -(-n // 16) * 16


def up128(n):
    return -(-n // 128) * 128


def nn(a, b):
    return lax.dot_general(a, b, (((1,), (0,)), ((), ())), preferred_element_type=F32)


def nt(a, b):
    return lax.dot_general(a, b, (((1,), (1,)), ((), ())), preferred_element_type=F32)


def tn(a, b):
    return lax.dot_general(a, b, (((0,), (0,)), ((), ())), preferred_element_type=F32)


def layer_kernel(
    dim, ff,
    tok_h, dy_h, wq_h, wo_h, wf_h, wp_h, len_s, g1_i, b1_i, g2_i, b2_i,
    res_o, gtok_o, gq_o, go_o, gf_o, gp_o, gln_o,
    tok, dys, xown, wq, wo, wf, wp, qs, ks, vs, att, part, part1, ra, sb, rb, mix, dmix,
    sec, act, gel, datt, dqkv, gq, go, gf, gp, yq, yo, yf, yp, zq, zo, zf, zp,
    lnv, lnr, vec, lens, lg, lr, lz,
    raw_sem, ag_sem, rs_sem, fin_sem, xs_sem, xa_sem, ln_sem,
):
    blk = dim // NZ
    bp = up16(blk)
    hb = bp // 2
    dp = NZ * bp
    nq = wq.shape[1]
    head = dim // HEADS
    nh = HEADS // NT
    inv_dim = 1.0 / dim
    scale = head ** (-0.5)

    w = lax.axis_index("wide")
    z = lax.axis_index("narrow")
    c = lax.rem(w, 2)
    x = lax.rem(w // 2, 2)
    y = lax.rem(w // 4, 2)
    t = 2 * x + c
    core_dev = (w + 1 - 2 * c, z)
    x_dev = (w + 2 - 4 * x, z)
    y_dev = (w + 4 - 8 * y, z)
    up_dev = (w, z + 1)
    down_dev = (w, z - 1)

    ends = []

    def remote(src, dst, ssem, rsem, dev):
        return pltpu.make_async_remote_copy(
            src_ref=src, dst_ref=dst, send_sem=ssem, recv_sem=rsem, device_id=dev, device_id_type=MESH
        )

    def send(make, cond=None, track=True):
        if cond is None:
            make().start()
        else:
            pl.when(cond())(lambda: make().start())
        if track:
            ends.append((cond, make))

    def both(a, b):
        return jnp.logical_and(a, b)

    lane = lax.broadcasted_iota(jnp.int32, (1, dp), 1)
    live = lax.rem(lane, bp) < blk
    livef = live.astype(F32)

    barrier = pltpu.get_barrier_semaphore()
    others = [(w, lax.rem(z + k, NZ)) for k in range(1, NZ)]
    for dev in [core_dev, x_dev, y_dev] + others:
        pl.semaphore_signal(barrier, inc=1, device_id=dev, device_id_type=MESH)
    pl.semaphore_wait(barrier, 3 + len(others))

    def rows_of(s, yy, r0=0, nr=None):
        return pl.ds(pl.multiple_of(bp * s + hb * yy + r0, 16), hb if nr is None else nr)

    q_pieces = [(0, 80), (80, hb - 80)]
    gathers = {
        "q": (wq, 0, q_pieces),
        "f": (wf, 4 * len(q_pieces), [(0, hb)]),
        "p": (wp, 4 * len(q_pieces) + 4, [(0, hb)]),
        "o": (wo, 4 * len(q_pieces) + 8, [(0, hb)]),
    }

    def ag_view(name, s, yy, piece):
        ref, base, pieces = gathers[name]
        r0, nr = pieces[piece]
        if name == "o":
            return ref.at[rows_of(0, yy, r0, nr)]
        return ref.at[rows_of(s, yy, r0, nr)]

    def ag_id(name, s, piece):
        ref, base, pieces = gathers[name]
        return base if name == "o" else base + 4 * piece + s

    def ag_z(name, s, piece, up):
        v = ag_view(name, s, y, piece)
        i = ag_id(name, s, piece)
        return remote(v, v, ag_sem.at[i, 0 if up else 1], ag_sem.at[i, 2], up_dev if up else down_dev)

    def ag_y(name, s, yy, piece):
        v = ag_view(name, s, yy, piece)
        i = ag_id(name, s, piece)
        return remote(v, v, ag_sem.at[i, 3], ag_sem.at[i, 4], y_dev)

    def ag_start(name):
        for piece in range(len(gathers[name][2])):
            def own():
                return (t == z) if name == "o" else (z >= 0)

            send(lambda p=piece: ag_z(name, z, p, True), lambda: both(own(), z < NZ - 1))
            send(lambda p=piece: ag_z(name, z, p, False), lambda: both(own(), z > 0))

    def ag_forward(name, k):
        for piece in range(len(gathers[name][2])):
            for up in (True, False):
                s = z - k if up else z + k
                ok = (z >= k) if up else (z + k <= NZ - 1)
                if name == "o":
                    ok = t == s
                more = (z < NZ - 1) if up else (z > 0)
                pl.when(ok)(lambda s=s, p=piece, u=up: ag_z(name, s, p, u).wait_recv())
                send(lambda s=s, p=piece, u=up: ag_z(name, s, p, u), lambda ok=ok, more=more: both(ok, more))
                send(lambda s=s, p=piece: ag_y(name, s, y, p), lambda ok=ok: ok)

    def ag_finish(name):
        for piece in range(len(gathers[name][2])):
            if name == "o":
                pl.when(z != t)(lambda p=piece: ag_y(name, 0, 1 - y, p).wait_recv())
            else:
                for s in range(NZ):
                    pl.when(z != s)(lambda s=s, p=piece: ag_y(name, s, 1 - y, p).wait_recv())

    def blk_of(s, cc, xx):
        return s * NT + cc * 2 + xx

    def xg(ref, e, s, kind):
        i = 2 * e + s
        if kind == "x":
            v = ref.at[blk_of(s, c, x)]
            return remote(v, v, xs_sem.at[i, 0], xs_sem.at[i, 1], x_dev)
        if kind == "own":
            v = ref.at[blk_of(s, c, x)]
            return remote(v, v, xs_sem.at[i, 2], xs_sem.at[i, 3], core_dev)
        v = ref.at[blk_of(s, c, 1 - x)]
        return remote(v, v, xs_sem.at[i, 4], xs_sem.at[i, 5], core_dev)

    def xg_start(ref, e, s, track=True):
        send(lambda: xg(ref, e, s, "x"), track=track)
        send(lambda: xg(ref, e, s, "own"), track=track)

    def xg_forward(ref, e, s, track=True):
        xg(ref, e, s, "x").wait_recv()
        send(lambda: xg(ref, e, s, "fwd"), track=track)

    def xg_finish(ref, e, s):
        xg(ref, e, s, "own").wait_recv()
        xg(ref, e, s, "fwd").wait_recv()

    def xg_sent(ref, e, s):
        for kind in ("x", "own", "fwd"):
            xg(ref, e, s, kind).wait_send()

    def part_of(e):
        return part1 if e == 1 else part

    def ex_a(e, s):
        i = 2 * e + s
        return remote(
            part_of(e).at[pl.ds(s * NT + (1 - c) * 2, 2)], ra.at[int(e == 1), s],
            xa_sem.at[i, 0], xa_sem.at[i, 1], core_dev,
        )

    def ex_b(e, s):
        i = 2 * e + s
        return remote(sb.at[int(e == 1), s], rb.at[int(e == 1), s], xa_sem.at[i, 2], xa_sem.at[i, 3], x_dev)

    def ex_relay(e, s):
        ex_a(e, s).wait_recv()
        sb[int(e == 1), s] = (
            part_of(e)[blk_of(s, c, 1 - x)].astype(F32) + ra[int(e == 1), s, 1 - x].astype(F32)
        ).astype(BF)
        ex_b(e, s).start()

    def ex_sum(e, s):
        ex_b(e, s).wait_recv()
        return (
            part_of(e)[blk_of(s, c, x)].astype(F32)
            + ra[int(e == 1), s, x].astype(F32)
            + rb[int(e == 1), s].astype(F32)
        )

    base = pl.multiple_of(bp * z, 16)
    reduces = {"q": (gq, yq, zq, 0), "f": (gf, yf, zf, 1), "p": (gp, yp, zp, 2), "o": (go, yo, zo, 3)}

    def rs_y(name, d):
        g, yr, zr, i = reduces[name]
        if name == "o":
            return remote(g.at[rows_of(0, 1 - y)], yr.at[0], rs_sem.at[i, 0], rs_sem.at[i, 4], y_dev)
        if name in ZFIRST:
            return remote(g.at[rows_of(z, 1 - y)], yr.at[0], rs_sem.at[i, 0], rs_sem.at[i, 4], y_dev)
        return remote(g.at[rows_of(d, 1 - y)], yr.at[d], rs_sem.at[i, d], rs_sem.at[i, 4 + d], y_dev)

    def rs_z(name, d, slot, up):
        g, yr, zr, i = reduces[name]
        dd = 0 if name == "o" else d
        if name in ZFIRST:
            return remote(
                g.at[pl.ds(bp * d, bp)], zr.at[slot], rs_sem.at[i, 8 + d], rs_sem.at[i, 12 + slot], up_dev if up else down_dev
            )
        return remote(yr.at[dd], zr.at[slot], rs_sem.at[i, 8 + dd], rs_sem.at[i, 12 + slot], up_dev if up else down_dev)

    def add_up(dst, srcs):
        step = 48

        def body(j, carry):
            r = pl.ds(pl.multiple_of(j * step, step), step)
            total = srcs[0][r, :].astype(F32)
            for src in srcs[1:]:
                total = total + src[r, :].astype(F32)
            dst[r, :] = total.astype(BF)
            return carry

        lax.fori_loop(0, dst.shape[0] // step, body, 0)

    def rs_start(name, dests=(3, 0, 2, 1)):
        for d in (0,) if name == "o" else dests:
            send(lambda d=d: rs_y(name, d))

    def rs_stage(name, d, j):
        g, yr, zr, i = reduces[name]

        def side(pos, up):
            def run():
                if name in ZFIRST:
                    if j > 0:
                        own = g.at[pl.ds(bp * d, bp)]
                        rs_z(name, d, d, up).wait_recv()
                        add_up(own, [own, zr.at[d]])
                    return
                rs_y(name, d).wait_recv()
                own = g.at[rows_of(0 if name == "o" else d, y)]
                mine = yr.at[0 if name == "o" else d]
                srcs = [own, mine]
                slot = 0 if name == "o" else d
                if j > 0:
                    rs_z(name, d, slot, up).wait_recv()
                    srcs.append(zr.at[slot])
                add_up(mine, srcs)

            nxt = pos + 1 if up else pos - 1
            if name == "o":
                last = t == nxt
                cond = both(z == pos, (t > pos) if up else (t < pos))
                pl.when(cond)(run)
                if up:
                    send(lambda: rs_z(name, 0, 1, True), lambda: both(cond, last))
                    send(lambda: rs_z(name, 0, 0, True), lambda: both(cond, jnp.logical_not(last)))
                else:
                    send(lambda: rs_z(name, 0, 0, False), lambda: cond)
            else:
                cond = z == pos
                pl.when(cond)(run)
                slot = NZ if (up and nxt == d) else d
                send(lambda: rs_z(name, d, slot, up), lambda: cond)

        if name == "o":
            if j < NZ - 1:
                side(j, True)
                side(NZ - 1 - j, False)
            return
        if j < d:
            side(j, True)
        if NZ - 1 - j > d:
            side(NZ - 1 - j, False)

    def rs_line(name):
        g, yr, zr, i = reduces[name]
        own = g.at[pl.ds(base, bp)]

        def run(slots):
            def go_():
                for slot in slots:
                    rs_z(name, slot if slot < NZ else 0, slot, True).wait_recv()
                add_up(own, [own] + [zr.at[slot] for slot in slots])
            return go_

        for k in range(NZ):
            pl.when(z == k)(run(([k] if k < NZ - 1 else []) + ([NZ] if k > 0 else [])))
        send(lambda: rs_y(name, 0))

    def rs_final(name):
        g, yr, zr, i = reduces[name]
        if name in ZFIRST:
            rs_y(name, 0).wait_recv()
            add_up(yr.at[0], [g.at[rows_of(z, y)], yr.at[0]])
            return
        out = name == "o"
        me = 0 if out else z
        here = (t == z) if out else (z >= 0)
        above = 0 if out else z
        below = 1 if out else NZ

        def run(has_above, has_below):
            def go_():
                rs_y(name, me).wait_recv()
                srcs = [g.at[rows_of(me, y)], yr.at[me]]
                if has_above:
                    rs_z(name, me, above, True).wait_recv()
                    srcs.append(zr.at[above])
                if has_below:
                    rs_z(name, me, below, True).wait_recv()
                    srcs.append(zr.at[below])
                add_up(yr.at[me], srcs)
            return go_

        pl.when(both(here, z == 0))(run(True, False))
        pl.when(both(here, z == NZ - 1))(run(False, True))
        pl.when(both(here, both(z > 0, z < NZ - 1)))(run(True, True))

    outs = {"q": gq_o, "f": gf_o, "p": gp_o, "o": go_o}

    def fin_view(name, tt, yy):
        return outs[name].at[yy] if name == "o" else outs[name].at[tt * 2 + yy]

    def fin_copy(name, src, tt, yy, k, dev):
        i = reduces[name][3]
        slot = yy if name == "o" else tt * 2 + yy
        return remote(src, fin_view(name, tt, yy), fin_sem.at[i, k], fin_sem.at[i, 8 + slot], dev)

    def own_block(name):
        yr = reduces[name][1]
        return yr.at[0] if name == "o" or name in ZFIRST else yr.at[z]

    def keep_own(name):
        return pltpu.make_async_copy(own_block(name), fin_view(name, t, y), fin_sem.at[reduces[name][3], 7])

    tx = 2 * (1 - x) + c

    def fin_start(name):
        here = (lambda: t == z) if name == "o" else None
        if here is None:
            keep_own(name).start()
        else:
            pl.when(here())(lambda: keep_own(name).start())
        send(lambda: fin_copy(name, own_block(name), t, y, 0, y_dev), here)
        send(lambda: fin_copy(name, own_block(name), t, y, 1, x_dev), here)
        send(lambda: fin_copy(name, own_block(name), t, y, 2, core_dev), here)

    def fin_wait(name, tt, yy):
        fin_copy(name, fin_view(name, tt, yy), tt, yy, 0, core_dev).wait_recv()

    def fin_forward_y(name):
        here = (t == z) if name == "o" else (z >= 0)
        pl.when(here)(lambda: fin_wait(name, t, 1 - y))
        v = fin_view(name, t, 1 - y)
        send(lambda: fin_copy(name, v, t, 1 - y, 3, x_dev), lambda: here)
        send(lambda: fin_copy(name, v, t, 1 - y, 4, core_dev), lambda: here)

    def fin_forward_x(name, other):
        here = (tx == z) if name == "o" else (z >= 0)
        for k, yy in ((6, 1 - y) if other else (5, y),):
            pl.when(here)(lambda yy=yy: fin_wait(name, tx, yy))
            send(lambda k=k, yy=yy: fin_copy(name, fin_view(name, tx, yy), tx, yy, k, core_dev), lambda: here)

    def fin_finish(name):
        if name == "o":
            here = lax.rem(z, 2) != c
            for yy in range(2):
                pl.when(here)(lambda yy=yy: fin_wait(name, 0, yy))
            pl.when(t == z)(lambda: keep_own(name).wait())
        else:
            for xx in range(2):
                for yy in range(2):
                    fin_wait(name, 2 * xx + (1 - c), yy)
            keep_own(name).wait()

    def prepare(rq, rt, ro, rd, turned):
        loads = [
            pltpu.make_async_copy(wq_h, rq, raw_sem.at[0]),
            pltpu.make_async_copy(tok_h, rt, raw_sem.at[1]),
            pltpu.make_async_copy(wo_h, ro, raw_sem.at[2]),
            pltpu.make_async_copy(dy_h, rd, raw_sem.at[3]),
        ]
        for load in loads:
            load.start()
        lnv[...] = jnp.zeros_like(lnv)
        for k, ref in enumerate((g1_i, b1_i, g2_i, b2_i)):
            lnv[k : k + 1, 0:blk] = ref[...].astype(F32).reshape(1, blk)
        lnr[z] = lnv[...]
        for k in range(1, NZ):
            send(lambda k=k: remote(lnv, lnr.at[z], ln_sem.at[k - 1], ln_sem.at[2 + k], others[k - 1]))

        loads[0].wait()
        wq[pl.ds(base, bp), :] = jnp.zeros((bp, nq), BF)
        for k in range(NT):
            @pl.when(t == k)
            def _(k=k):
                for j in range(3):
                    wq[pl.ds(base, blk), blk * j : blk * (j + 1)] = rq[:, dim * j + blk * k : dim * j + blk * (k + 1)]
        ag_start("q")

        turned[...] = jnp.zeros_like(turned)

        def spread(dst, src):
            for j in range(NZ):
                turned[bp * j : bp * j + blk, :] = src[blk * j : blk * (j + 1), :]
            dst[...] = turned[...].T

        loads[1].wait()
        for s in range(WAVES):
            spread(xown.at[s], rt.at[s])
            sent = jnp.where(lane == blk, len_s[s].astype(F32), xown[s].astype(F32))
            tok[blk_of(s, c, x)] = sent.astype(BF)
            xg_start(tok, 0, s, track=False)
        loads[2].wait()

        @pl.when(t == z)
        def _():
            wo[...] = jnp.zeros_like(wo)
            for j in range(NZ):
                wo[0:blk, bp * j : bp * j + blk] = ro[:, blk * j : blk * (j + 1)]
        ag_start("o")
        loads[3].wait()
        for s in range(WAVES):
            spread(dys.at[blk_of(s, c, x)], rd.at[s])
            xg_start(dys, 1, s)

    def prepare_mlp(rf, rp):
        loads = [
            pltpu.make_async_copy(wf_h, rf, raw_sem.at[4]),
            pltpu.make_async_copy(wp_h.at[pl.ds(pl.multiple_of(blk * t, 8), blk)], rp, raw_sem.at[5]),
        ]
        for load in loads:
            load.start()
        loads[0].wait()
        wf[pl.ds(base, bp), :] = jnp.zeros((bp, dp), BF)
        for k in range(NT):
            @pl.when(t == k)
            def _(k=k):
                for j in range(NZ):
                    lo = (ff // NZ) * j + blk * k
                    wf[pl.ds(base, blk), bp * j : bp * j + blk] = rf[:, lo : lo + blk]
        loads[1].wait()
        wp[pl.ds(base, bp), :] = jnp.zeros((bp, dp), BF)
        for j in range(NZ):
            wp[pl.ds(base, blk), bp * j : bp * j + blk] = rp[:, blk * j : blk * (j + 1)]

    pl.run_scoped(
        prepare,
        pltpu.VMEM((blk, 3 * dim), BF),
        pltpu.VMEM((WAVES, dim, SEQ), BF),
        pltpu.VMEM((blk, dim), BF),
        pltpu.VMEM((WAVES, dim, SEQ), BF),
        pltpu.VMEM((dp, SEQ), BF),
    )
    pl.run_scoped(prepare_mlp, pltpu.VMEM((blk, ff), BF), pltpu.VMEM((blk, dim), BF))

    def main(first, pm):
        for k in range(1, NZ):
            remote(lnv, lnr.at[lax.rem(z + NZ - k, NZ)], ln_sem.at[k - 1], ln_sem.at[2 + k], others[k - 1]).wait_recv()
        vec[...] = jnp.zeros_like(vec)
        for j in range(NZ):
            vec[:, bp * j : bp * j + blk] = lnr[j, :, 0:blk]
        lg[...] = jnp.zeros_like(lg)
        dqkv[...] = jnp.zeros_like(dqkv)

        def stats(rows):
            mean = jnp.sum(rows, axis=-1, keepdims=True) * inv_dim
            cen = (rows - mean) * livef
            inv = lax.rsqrt(jnp.sum(cen * cen, axis=-1, keepdims=True) * inv_dim + EPS)
            return cen * inv, inv

        def norm_back(e, n, inv):
            me = jnp.sum(e, axis=-1, keepdims=True) * inv_dim
            mn = jnp.sum(e * n, axis=-1, keepdims=True) * inv_dim
            return inv * (e - me - n * mn) * livef

        def ln_first(s):
            def body(i, carry):
                b = s * NT + i
                raw = tok[b].astype(F32)
                lens[b] = jnp.broadcast_to(raw[0:8, blk : blk + 1], (8, SEQ))
                n, inv = stats(raw * livef)
                first[b] = (n * vec[0:1, :] + vec[1:2, :]).astype(BF)
                return carry
            lax.fori_loop(0, NT, body, 0)

        lane_h = lax.broadcasted_iota(jnp.int32, (1, bp), 1)
        head_masks = [(lane_h >= head * h) & (lane_h < head * (h + 1)) for h in range(nh)]

        def stack_heads(v):
            zero = jnp.zeros_like(v)
            return jnp.concatenate([jnp.where(m, v, zero) for m in head_masks], axis=0)

        def side_by_side(v):
            return jnp.concatenate([v[SEQ * h : SEQ * (h + 1)] for h in range(nh)], axis=1)

        def project(s):
            def body(i, carry):
                b = s * NT + i * 2
                rows = first[pl.ds(b, 2)].reshape(2 * SEQ, dp)
                out = nn(rows, wq[...])
                for j, ref in enumerate((qs, ks, vs)):
                    ref[pl.ds(b, 2)] = out[:, blk * j : blk * j + bp].astype(BF).reshape(2, SEQ, bp)
                return carry
            lax.fori_loop(0, 2, body, 0)

        def attend(s):
            q_pos = lax.broadcasted_iota(jnp.int32, (SEQ, SEQ), 0)
            k_pos = lax.broadcasted_iota(jnp.int32, (SEQ, SEQ), 1)

            def body(i, carry):
                b = s * NT + i
                scores = nt(stack_heads(qs[b]), ks[b]) * scale
                ok = (k_pos <= q_pos) & (k_pos.astype(F32) < lens[b, 0:1, :])
                bias = jnp.concatenate([ok.astype(F32)] * nh, axis=0) > 0.5
                scores = jnp.where(bias, scores, MASKED)
                top = jnp.max(scores, axis=-1, keepdims=True)
                ex = jnp.exp(scores - top)
                prob = ex / jnp.sum(ex, axis=-1, keepdims=True)
                pm[b] = prob
                out = nn(side_by_side(prob.astype(BF)), stack_heads(vs[b]))
                att[b] = out.astype(BF)
                return carry
            lax.fori_loop(0, NT, body, 0)

        def matmul_part(src, weight, s, transposed, e):
            width = src.shape[2]
            dst = part_of(e)

            def body(i, carry):
                b = s * NT + i * 2
                rows = src[pl.ds(b, 2)].reshape(2 * SEQ, width)
                out = nt(rows, weight[...]) if transposed else nn(rows, weight[...])
                dst[pl.ds(b, 2)] = out.astype(BF).reshape(2, SEQ, dp)
                return carry
            lax.fori_loop(0, 2, body, 0)

        def mid(s):
            rows = xown[s].astype(F32) + ex_sum(0, s)
            mix[s] = rows
            n, inv = stats(rows)
            sec[blk_of(s, c, x)] = (n * vec[2:3, :] + vec[3:4, :]).astype(BF)
            xg_start(sec, 2, s)

        def expand(s):
            def body(i, carry):
                b = s * NT + i * 2
                rows = sec[pl.ds(b, 2)].reshape(2 * SEQ, dp)
                pre = nn(rows, wf[...])
                sq = pre * pre
                th = jnp.tanh(GELU_C * (pre + GELU_A * (pre * sq)))
                half = 0.5 * (1.0 + th)
                act[pl.ds(b, 2)] = (pre * half).astype(BF).reshape(2, SEQ, dp)
                slope = half + (0.5 * GELU_C) * pre * (1.0 - th * th) * (1.0 + (3.0 * GELU_A) * sq)
                gel[pl.ds(b, 2)] = slope.astype(BF).reshape(2, SEQ, dp)
                return carry
            lax.fori_loop(0, 2, body, 0)

        def grad_of(dst, left, right):
            step = 384
            rows = NB * SEQ

            def body(j, carry):
                cols = pl.ds(pl.multiple_of(j * step, step), step)
                out = tn(left[:, :, cols].reshape(rows, step), right[...].reshape(rows, right.shape[2]))
                dst[cols, :] = out.astype(BF)
                return carry
            lax.fori_loop(0, dp // step, body, 0)

        def back_act(s):
            def body(i, carry):
                b = s * NT + i * 2
                d_act = nt(dys[pl.ds(b, 2)].reshape(2 * SEQ, dp), wp[...])
                slope = gel[pl.ds(b, 2)].reshape(2 * SEQ, dp).astype(F32)
                gel[pl.ds(b, 2)] = (d_act * slope).astype(BF).reshape(2, SEQ, dp)
                return carry
            lax.fori_loop(0, 2, body, 0)

        def back_mid(s):
            d2 = ex_sum(2, s)
            n, inv = stats(mix[s])
            lg[2:3, :] = lg[2:3, :] + jnp.sum(d2 * n, axis=0, keepdims=True)
            lg[3:4, :] = lg[3:4, :] + jnp.sum(d2, axis=0, keepdims=True)
            rows = dys[blk_of(s, c, x)].astype(F32) + norm_back(d2 * vec[2:3, :], n, inv)
            dmix[s] = rows
            tok[blk_of(s, c, x)] = rows.astype(BF)
            xg_start(tok, 3, s)

        def back_attend(s):
            def proj(i, carry):
                b = s * NT + i * 2
                out = nt(tok[pl.ds(b, 2)].reshape(2 * SEQ, dp), wo[...])
                datt[pl.ds(b, 2)] = out.astype(BF).reshape(2, SEQ, bp)
                return carry
            lax.fori_loop(0, 2, proj, 0)

            def body(i, carry):
                b = s * NT + i
                d_out = stack_heads(datt[b])
                prob = pm[b]
                d_prob = nt(d_out, vs[b])
                total = jnp.sum(prob * d_prob, axis=-1, keepdims=True)
                d_scores = (prob * (d_prob - total)).astype(BF)
                dqkv[b, :, 0:bp] = (nn(side_by_side(d_scores), stack_heads(ks[b])) * scale).astype(BF)
                dqkv[b, :, blk : blk + bp] = (tn(d_scores, stack_heads(qs[b])) * scale).astype(BF)
                dqkv[b, :, 2 * blk : 2 * blk + bp] = tn(prob.astype(BF), d_out).astype(BF)
                return carry
            lax.fori_loop(0, NT, body, 0)

        def back_first(s):
            d1 = ex_sum(3, s)
            n, inv = stats(xown[s].astype(F32))
            lg[0:1, :] = lg[0:1, :] + jnp.sum(d1 * n, axis=0, keepdims=True)
            lg[1:2, :] = lg[1:2, :] + jnp.sum(d1, axis=0, keepdims=True)
            gtok_o[s] = (dmix[s] + norm_back(d1 * vec[0:1, :], n, inv)).astype(BF)

        def grad_out():
            rows_all = NB * SEQ
            go[...] = tn(att[...].reshape(rows_all, bp), tok[...].reshape(rows_all, dp)).astype(BF)

        def finish_rows(s):
            res_o[s] = (mix[s] + ex_sum(1, s)).astype(BF)

        hops = [
            remote(lg, lr.at[k], ln_sem.at[6 + 2 * k], ln_sem.at[7 + 2 * k], dev)
            for k, dev in enumerate((core_dev, x_dev, y_dev))
        ]

        def ln_add(k):
            hops[k].wait()
            lg[...] = lg[...] + lr[k]

        def ln_line(k):
            return remote(lg, lz.at[k - 1], ln_sem.at[11 + k], ln_sem.at[14 + k], others[k - 1])

        def ln_send():
            for k in range(1, NZ):
                send(lambda k=k: ln_line(k))

        def ln_total():
            for k in range(1, NZ):
                ln_line(k).wait_recv()
            total = lg[...] + lz[0] + lz[1] + lz[2]
            for j in range(NZ):
                @pl.when(z == j)
                def _(j=j):
                    gln_o[:, 0:blk] = total[:, bp * j : bp * j + blk]

        ag_forward("q", 1)
        xg_forward(tok, 0, 0, track=False)
        ag_start("f")
        xg_finish(tok, 0, 0)
        ag_forward("q", 2)
        xg_forward(tok, 0, 1, track=False)
        xg_finish(tok, 0, 1)
        ag_forward("o", 1)
        ag_forward("q", 3)
        ln_first(0)
        ln_first(1)
        ag_forward("o", 2)
        ag_start("p")
        ag_forward("o", 3)
        ag_finish("q")
        project(1)
        ag_forward("f", 1)
        project(0)
        attend(0)
        ag_finish("o")
        matmul_part(att, wo, 0, False, 0)
        ex_a(0, 0).start()
        attend(1)
        matmul_part(att, wo, 1, False, 0)
        ex_a(0, 1).start()
        ag_forward("f", 2)
        xg_forward(dys, 1, 1)
        ex_relay(0, 0)
        ex_a(0, 1).wait_send()
        ex_relay(0, 1)
        mid(0)
        xg_forward(dys, 1, 0)
        xg_sent(tok, 0, 1)
        ag_forward("f", 3)
        ag_forward("p", 1)
        ag_forward("p", 2)
        xg_finish(dys, 1, 1)
        mid(1)
        xg_forward(sec, 2, 0)
        xg_forward(sec, 2, 1)
        xg_sent(tok, 0, 0)
        ag_finish("f")
        xg_finish(dys, 1, 0)
        xg_finish(sec, 2, 1)
        xg_finish(sec, 2, 0)
        expand(1)
        expand(0)
        ag_forward("p", 3)
        grad_of(gp, act, dys)
        rs_stage("p", 3, 0)
        ag_finish("p")
        rs_stage("p", 0, 0)
        rs_stage("p", 2, 0)
        rs_stage("p", 1, 0)
        back_act(0)
        ex_a(0, 0).wait_send()
        matmul_part(gel, wf, 0, True, 2)
        ex_a(2, 0).start()
        back_act(1)
        ex_b(0, 0).wait_send()
        ex_relay(2, 0)
        matmul_part(gel, wf, 1, True, 2)
        ex_a(2, 1).start()
        ex_b(0, 1).wait_send()
        ex_relay(2, 1)
        grad_of(gf, sec, gel)
        rs_start("f")
        rs_stage("p", 3, 1)
        back_mid(0)
        back_mid(1)
        xg_forward(tok, 3, 0)
        rs_stage("p", 0, 1)
        xg_finish(tok, 3, 0)
        back_attend(0)
        xg_forward(tok, 3, 1)
        xg_finish(tok, 3, 1)
        back_attend(1)
        grad_of(gq, first, dqkv)
        rs_start("q")
        grad_out()
        rs_start("o")
        rs_stage("p", 1, 1)
        rs_stage("p", 2, 1)
        matmul_part(act, wp, 0, False, 1)
        ex_a(1, 0).start()
        matmul_part(act, wp, 1, False, 1)
        ex_a(1, 1).start()
        rs_stage("p", 3, 2)
        rs_stage("p", 0, 2)
        rs_stage("f", 3, 0)
        ex_relay(1, 0)
        ex_relay(1, 1)
        ex_a(2, 0).wait_send()
        matmul_part(dqkv, wq, 0, True, 3)
        ex_a(3, 0).start()
        ex_a(2, 1).wait_send()
        matmul_part(dqkv, wq, 1, True, 3)
        ex_a(3, 1).start()
        rs_stage("f", 0, 0)
        rs_stage("f", 2, 0)
        rs_stage("f", 1, 0)
        ex_b(2, 0).wait_send()
        ex_relay(3, 0)
        ex_b(2, 1).wait_send()
        ex_relay(3, 1)
        rs_stage("q", 3, 0)
        rs_line("p")
        rs_stage("q", 0, 0)
        rs_stage("f", 3, 1)
        rs_stage("f", 0, 1)
        rs_stage("q", 2, 0)
        rs_stage("f", 2, 1)
        rs_stage("q", 1, 0)
        rs_stage("q", 3, 1)
        rs_stage("q", 0, 1)
        rs_stage("f", 1, 1)
        rs_stage("f", 3, 2)
        rs_stage("f", 0, 2)
        rs_stage("q", 2, 1)
        rs_stage("q", 1, 1)
        rs_final("p")
        fin_start("p")
        rs_stage("q", 3, 2)
        rs_stage("q", 0, 2)
        back_first(0)
        back_first(1)
        hops[0].start()
        rs_final("f")
        fin_start("f")
        rs_final("q")
        fin_start("q")
        rs_stage("o", 0, 0)
        ln_add(0)
        hops[1].start()
        fin_forward_y("p")
        fin_forward_x("p", False)
        finish_rows(0)
        finish_rows(1)
        rs_stage("o", 0, 1)
        ln_add(1)
        hops[2].start()
        fin_forward_x("p", True)
        rs_stage("o", 0, 2)
        rs_final("o")
        fin_start("o")
        fin_forward_y("f")
        fin_forward_x("f", False)
        ln_add(2)
        ln_send()
        fin_forward_y("q")
        fin_forward_x("q", False)
        fin_forward_y("o")
        fin_forward_x("o", False)
        fin_forward_x("f", True)
        fin_forward_x("q", True)
        fin_forward_x("o", True)
        ln_total()
        for name in ("p", "f", "o", "q"):
            fin_finish(name)
        for s in range(WAVES):
            for e in (1, 3):
                ex_a(e, s).wait_send()
                ex_b(e, s).wait_send()
        for cond, make in ends:
            if cond is None:
                make().wait_send()
            else:
                pl.when(cond())(lambda make=make: make().wait_send())

    pl.run_scoped(main, pltpu.VMEM((NB, SEQ, dp), BF), pltpu.VMEM((NB, nh * SEQ, SEQ), F32))


def layer_call(dim, ff, tokens, cot, w_qkv, w_out, w_fc, w_proj, lengths, norms):
    blk = dim // NZ
    bp = up16(blk)
    hb = bp // 2
    dp = NZ * bp
    nq = up128(3 * blk)
    vm, dma = pltpu.VMEM, pltpu.SemaphoreType.DMA
    big = (NB, SEQ, dp)
    half = lambda k: (1 if k in ZFIRST else NZ, hb, nq if k == "q" else dp)
    line = lambda k: (NZ + 1, bp if k in ZFIRST else hb, nq if k == "q" else dp)
    scratch = [
        vm(big, BF), vm(big, BF), vm((WAVES, SEQ, dp), BF),
        vm((dp, nq), BF), vm((bp, dp), BF), vm((dp, dp), BF), vm((dp, dp), BF),
        vm((NB, SEQ, bp), BF), vm((NB, SEQ, bp), BF), vm((NB, SEQ, bp), BF),
        vm((NB, SEQ, bp), BF),
        vm(big, BF), vm(big, BF),
        vm((2, WAVES, 2, SEQ, dp), BF), vm((2, WAVES, SEQ, dp), BF), vm((2, WAVES, SEQ, dp), BF),
        vm((WAVES, SEQ, dp), F32), vm((WAVES, SEQ, dp), F32),
        vm(big, BF), vm(big, BF), vm(big, BF),
        vm((NB, SEQ, bp), BF), vm((NB, SEQ, nq), BF),
        vm((dp, nq), BF), vm((bp, dp), BF), vm((dp, dp), BF), vm((dp, dp), BF),
        vm(half("q"), BF), vm((1, hb, dp), BF), vm(half("f"), BF), vm(half("p"), BF),
        vm(line("q"), BF), vm((2, hb, dp), BF), vm(line("f"), BF), vm(line("p"), BF),
        vm((8, up128(blk)), F32), vm((NZ, 8, up128(blk)), F32), vm((8, dp), F32), vm((NB, 8, SEQ), F32),
        vm((8, dp), F32), vm((3, 8, dp), F32), vm((3, 8, dp), F32),
        dma((6,)), dma((17, 5)), dma((4, 17)), dma((4, 16)), dma((8, 6)), dma((8, 4)), dma((18,)),
    ]
    hbm = pl.BlockSpec(memory_space=pl.ANY)
    inv = pl.BlockSpec(memory_space=pltpu.VMEM)
    shape = jax.ShapeDtypeStruct

    def body(*refs):
        layer_kernel(dim, ff, *refs)

    return pl.pallas_call(
        body,
        out_shape=(
            shape((WAVES, SEQ, dp), BF), shape((WAVES, SEQ, dp), BF),
            shape((8, hb, nq), BF), shape((2, hb, dp), BF), shape((8, hb, dp), BF), shape((8, hb, dp), BF),
            shape((8, up128(blk)), F32),
        ),
        in_specs=[hbm] * 6 + [pl.BlockSpec(memory_space=pltpu.SMEM)] + [inv] * 4,
        out_specs=(inv, inv, hbm, hbm, hbm, hbm, inv),
        scratch_shapes=scratch,
        compiler_params=pltpu.CompilerParams(
            collective_id=0, has_side_effects=True, vmem_limit_bytes=67043328
        ),
    )(tokens, cot, w_qkv, w_out, w_fc, w_proj, lengths, *norms)


def finish_kernel(dim, ff, res, gtok, gq, go, gf, gp, gln, res_o, gtok_o, gq_o, go_o, gf_o, gp_o, *norms_o):
    blk = dim // NZ
    bp = up16(blk)
    for j in range(NZ):
        there = slice(bp * j, bp * j + blk)
        go_o[:, blk * j : blk * (j + 1)] = go[:, there].astype(F32)
        for t in range(NT):
            gp_o[t, :, blk * j : blk * (j + 1)] = gp[t, :, there].astype(F32)
            lo = (ff // NZ) * j + blk * t
            gf_o[:, lo : lo + blk] = gf[t, :, there].astype(F32)
    for j in range(3):
        for t in range(NT):
            lo = dim * j + blk * t
            gq_o[:, lo : lo + blk] = gq[t, :, blk * j : blk * (j + 1)].astype(F32)

    @pl.when(pl.program_id(0) == 0)
    def _():
        for k, ref in enumerate(norms_o):
            ref[...] = gln[k : k + 1, 0:blk].reshape(blk)
        for src, dst in ((res, res_o), (gtok, gtok_o)):
            for s in range(WAVES):
                turned = src[s].T
                for j in range(NZ):
                    dst[s, blk * j : blk * (j + 1), :] = turned[bp * j : bp * j + blk, :]


def finish_call(dim, ff, res, gtok, gq, go, gf, gp, gln):
    blk = dim // NZ
    bp = up16(blk)
    dp = NZ * bp
    nq = gq.shape[2]
    step = 56
    shape, spec = jax.ShapeDtypeStruct, pl.BlockSpec
    whole = spec(memory_space=pltpu.VMEM)
    quarters = lambda n: spec((NT, step, n), lambda i: (0, i, 0))
    lines = lambda n: spec((step, n), lambda i: (i, 0))
    return pl.pallas_call(
        lambda *refs: finish_kernel(dim, ff, *refs),
        grid=(blk // step,),
        in_specs=[whole, whole, quarters(nq), lines(dp), quarters(dp), quarters(dp), whole],
        out_specs=[whole, whole, lines(3 * dim), lines(dim), lines(ff), quarters(dim)] + [whole] * 4,
        out_shape=[
            shape((WAVES, dim, SEQ), BF), shape((WAVES, dim, SEQ), BF),
            shape((blk, 3 * dim), F32), shape((blk, dim), F32), shape((blk, ff), F32), shape((NT, blk, dim), F32),
        ] + [shape((blk,), F32)] * 4,
        compiler_params=pltpu.CompilerParams(vmem_limit_bytes=67043328),
    )(
        res, gtok, gq.reshape(NT, bp, nq), go.reshape(bp, dp), gf.reshape(NT, bp, dp), gp.reshape(NT, bp, dp), gln
    )


def sum_boxes(value, wide):
    total = value
    for k in range(1, wide // 8):
        total = total + lax.ppermute(value, "wide", [(i, (i + 8 * k) % wide) for i in range(wide)])
    return total


def solution(mesh):
    wide, narrow = mesh.shape["wide"], mesh.shape["narrow"]
    assert narrow == NZ and wide % 8 == 0

    def shards(tokens, lengths, ln1_gain, ln1_bias, w_qkv, w_out, ln2_gain, ln2_bias, w_fc, w_proj, cotangent):
        cells, seq, dim = tokens.shape
        assert cells == WAVES and seq == SEQ
        ff = w_fc.shape[1]
        blk = dim // NZ
        bp = up16(blk)
        res, gtok, gq, go, gf, gp, gln = layer_call(
            dim, ff, tokens.transpose(0, 2, 1), cotangent.transpose(0, 2, 1),
            w_qkv, w_out, w_fc, w_proj, lengths, (ln1_gain, ln1_bias, ln2_gain, ln2_bias),
        )
        res, gtok, *grads = finish_call(dim, ff, res, gtok, gq, go, gf, gp, gln)
        gq, go, gf, gp, g1, b1, g2, b2 = [sum_boxes(g, wide) for g in grads]
        return (
            res.transpose(0, 2, 1), gtok.transpose(0, 2, 1), g1, b1, gq, go, g2, b2, gf, gp.reshape(ff // NZ, dim)
        )

    rows = P(("wide", "narrow"), None, None)
    vec, mat = P("narrow"), P("narrow", None)
    return jax.shard_map(
        shards,
        mesh=mesh,
        in_specs=(rows, P(("wide", "narrow")), vec, vec, mat, mat, vec, vec, mat, mat, rows),
        out_specs=(rows, rows, vec, vec, mat, mat, vec, vec, mat, mat),
        check_vma=False,
    )
```

```python
import math

import jax
import jax.numpy as jnp
from jax import lax
from jax.experimental import pallas as pl
from jax.experimental.pallas import tpu as pltpu
from jax.sharding import PartitionSpec as P

HEADS = 20
EPS = 1e-05
MASKED = -1e30
BF, F32 = jnp.bfloat16, jnp.float32
MESH = pl.DeviceIdType.MESH

NZ = 4
NT = 4
WAVES = 2
SEQ = 128
NB = NT * WAVES
GELU_C = math.sqrt(2.0 / math.pi)
GELU_A = 0.044715
YWAY = ("f",)
ZFIRST = ("p",)


def up16(n):
    return -(-n // 16) * 16


def up128(n):
    return -(-n // 128) * 128


def nn(a, b):
    return lax.dot_general(a, b, (((1,), (0,)), ((), ())), preferred_element_type=F32)


def nt(a, b):
    return lax.dot_general(a, b, (((1,), (1,)), ((), ())), preferred_element_type=F32)


def tn(a, b):
    return lax.dot_general(a, b, (((0,), (0,)), ((), ())), preferred_element_type=F32)


def layer_kernel(
    dim, ff,
    tok_h, dy_h, wq_h, wo_h, wf_h, wp_h, len_s, g1_i, b1_i, g2_i, b2_i,
    res_o, gtok_o, gq_o, go_o, gf_o, gp_o, gln_o,
    tok, dys, xown, wq, wo, wf, wp, qs, ks, vs, att, part, part1, ra, sb, rb, mix, dmix,
    sec, act, gel, datt, dqkv, gq, go, gf, gp, yq, yo, yf, yp, zq, zo, zf, zp,
    lnv, lnr, vec, lens, lg, lr, lz,
    raw_sem, ag_sem, rs_sem, fin_sem, xs_sem, xa_sem, ln_sem,
):
    blk = dim // NZ
    bp = up16(blk)
    hb = bp // 2
    dp = NZ * bp
    nq = wq.shape[1]
    head = dim // HEADS
    nh = HEADS // NT
    inv_dim = 1.0 / dim
    scale = head ** (-0.5)

    w = lax.axis_index("wide")
    z = lax.axis_index("narrow")
    c = lax.rem(w, 2)
    x = lax.rem(w // 2, 2)
    y = lax.rem(w // 4, 2)
    t = 2 * x + c
    core_dev = (w + 1 - 2 * c, z)
    x_dev = (w + 2 - 4 * x, z)
    y_dev = (w + 4 - 8 * y, z)
    up_dev = (w, z + 1)
    down_dev = (w, z - 1)

    ends = []

    def remote(src, dst, ssem, rsem, dev):
        return pltpu.make_async_remote_copy(
            src_ref=src, dst_ref=dst, send_sem=ssem, recv_sem=rsem, device_id=dev, device_id_type=MESH
        )

    def send(make, cond=None, track=True):
        if cond is None:
            make().start()
        else:
            pl.when(cond())(lambda: make().start())
        if track:
            ends.append((cond, make))

    def both(a, b):
        return jnp.logical_and(a, b)

    lane = lax.broadcasted_iota(jnp.int32, (1, dp), 1)
    live = lax.rem(lane, bp) < blk
    livef = live.astype(F32)

    barrier = pltpu.get_barrier_semaphore()
    others = [(w, lax.rem(z + k, NZ)) for k in range(1, NZ)]
    for dev in [core_dev, x_dev, y_dev] + others:
        pl.semaphore_signal(barrier, inc=1, device_id=dev, device_id_type=MESH)
    pl.semaphore_wait(barrier, 3 + len(others))

    def rows_of(s, yy, r0=0, nr=None):
        return pl.ds(pl.multiple_of(bp * s + hb * yy + r0, 16), hb if nr is None else nr)

    q_pieces = [(0, 80), (80, hb - 80)]
    o_pieces = [(0, 48), (48, 48), (96, hb - 96)]
    gathers = {
        "q": (wq, 0, q_pieces),
        "f": (wf, 4 * len(q_pieces), [(0, hb)]),
        "p": (wp, 4 * len(q_pieces) + 4, [(0, hb)]),
        "o": (wo, 4 * len(q_pieces) + 8, o_pieces),
    }

    def ag_view(name, s, yy, piece):
        ref, base, pieces = gathers[name]
        r0, nr = pieces[piece]
        if name == "o":
            return ref.at[rows_of(0, yy, r0, nr)]
        return ref.at[rows_of(s, yy, r0, nr)]

    def ag_id(name, s, piece):
        ref, base, pieces = gathers[name]
        return base + piece if name == "o" else base + 4 * piece + s

    def ag_z(name, s, piece, up):
        v = ag_view(name, s, y, piece)
        i = ag_id(name, s, piece)
        return remote(v, v, ag_sem.at[i, 0 if up else 1], ag_sem.at[i, 2], up_dev if up else down_dev)

    def ag_y(name, s, yy, piece):
        v = ag_view(name, s, yy, piece)
        i = ag_id(name, s, piece)
        return remote(v, v, ag_sem.at[i, 3], ag_sem.at[i, 4], y_dev)

    def ag_start(name):
        for piece in range(len(gathers[name][2])):
            def own():
                return (t == z) if name == "o" else (z >= 0)

            send(lambda p=piece: ag_z(name, z, p, True), lambda: both(own(), z < NZ - 1))
            send(lambda p=piece: ag_z(name, z, p, False), lambda: both(own(), z > 0))

    def ag_forward(name, k):
        for piece in range(len(gathers[name][2])):
            for up in (True, False):
                s = z - k if up else z + k
                ok = (z >= k) if up else (z + k <= NZ - 1)
                if name == "o":
                    ok = t == s
                more = (z < NZ - 1) if up else (z > 0)
                pl.when(ok)(lambda s=s, p=piece, u=up: ag_z(name, s, p, u).wait_recv())
                send(lambda s=s, p=piece, u=up: ag_z(name, s, p, u), lambda ok=ok, more=more: both(ok, more))
                send(lambda s=s, p=piece: ag_y(name, s, y, p), lambda ok=ok: ok)

    def ag_finish(name):
        for piece in range(len(gathers[name][2])):
            if name == "o":
                pl.when(z != t)(lambda p=piece: ag_y(name, 0, 1 - y, p).wait_recv())
            else:
                for s in range(NZ):
                    pl.when(z != s)(lambda s=s, p=piece: ag_y(name, s, 1 - y, p).wait_recv())

    def blk_of(s, cc, xx):
        return s * NT + cc * 2 + xx

    def xg(ref, e, s, kind):
        i = 2 * e + s
        if kind == "x":
            v = ref.at[blk_of(s, c, x)]
            return remote(v, v, xs_sem.at[i, 0], xs_sem.at[i, 1], x_dev)
        if kind == "own":
            v = ref.at[blk_of(s, c, x)]
            return remote(v, v, xs_sem.at[i, 2], xs_sem.at[i, 3], core_dev)
        v = ref.at[blk_of(s, c, 1 - x)]
        return remote(v, v, xs_sem.at[i, 4], xs_sem.at[i, 5], core_dev)

    def xg_start(ref, e, s, track=True):
        send(lambda: xg(ref, e, s, "x"), track=track)
        send(lambda: xg(ref, e, s, "own"), track=track)

    def xg_forward(ref, e, s, track=True):
        xg(ref, e, s, "x").wait_recv()
        send(lambda: xg(ref, e, s, "fwd"), track=track)

    def xg_finish(ref, e, s):
        xg(ref, e, s, "own").wait_recv()
        xg(ref, e, s, "fwd").wait_recv()

    def xg_sent(ref, e, s):
        for kind in ("x", "own", "fwd"):
            xg(ref, e, s, kind).wait_send()

    def part_of(e):
        return part1 if e == 1 else part

    def ex_a(e, s):
        i = 2 * e + s
        return remote(
            part_of(e).at[pl.ds(s * NT + (1 - c) * 2, 2)], ra.at[int(e == 1), s],
            xa_sem.at[i, 0], xa_sem.at[i, 1], core_dev,
        )

    def ex_b(e, s):
        i = 2 * e + s
        return remote(sb.at[int(e == 1), s], rb.at[int(e == 1), s], xa_sem.at[i, 2], xa_sem.at[i, 3], x_dev)

    def ex_relay(e, s):
        ex_a(e, s).wait_recv()
        sb[int(e == 1), s] = (
            part_of(e)[blk_of(s, c, 1 - x)].astype(F32) + ra[int(e == 1), s, 1 - x].astype(F32)
        ).astype(BF)
        ex_b(e, s).start()

    def ex_sum(e, s):
        ex_b(e, s).wait_recv()
        return (
            part_of(e)[blk_of(s, c, x)].astype(F32)
            + ra[int(e == 1), s, x].astype(F32)
            + rb[int(e == 1), s].astype(F32)
        )

    base = pl.multiple_of(bp * z, 16)
    reduces = {"q": (gq, yq, zq, 0), "f": (gf, yf, zf, 1), "p": (gp, yp, zp, 2), "o": (go, yo, zo, 3)}

    def rs_y(name, d):
        g, yr, zr, i = reduces[name]
        if name == "o":
            r0, nr = o_pieces[d]
            return remote(
                g.at[rows_of(0, 1 - y, r0, nr)], yr.at[0, pl.ds(r0, nr)], rs_sem.at[i, d], rs_sem.at[i, 4 + d], y_dev
            )
        if name in ZFIRST:
            return remote(g.at[rows_of(z, 1 - y)], yr.at[0], rs_sem.at[i, 0], rs_sem.at[i, 4], y_dev)
        return remote(g.at[rows_of(d, 1 - y)], yr.at[d], rs_sem.at[i, d], rs_sem.at[i, 4 + d], y_dev)

    def rs_z(name, d, slot, up):
        g, yr, zr, i = reduces[name]
        if name == "o":
            rows = pl.ds(*o_pieces[d])
            return remote(
                yr.at[0, rows], zr.at[slot, rows], rs_sem.at[i, 8 + d], rs_sem.at[i, 12 + 2 * d + slot], up_dev if up else down_dev
            )
        if name in ZFIRST:
            return remote(
                g.at[pl.ds(bp * d, bp)], zr.at[slot], rs_sem.at[i, 8 + d], rs_sem.at[i, 12 + slot], up_dev if up else down_dev
            )
        return remote(yr.at[d], zr.at[slot], rs_sem.at[i, 8 + d], rs_sem.at[i, 12 + slot], up_dev if up else down_dev)

    def add_up(dst, srcs):
        step = 48

        def body(j, carry):
            r = pl.ds(pl.multiple_of(j * step, step), step)
            total = srcs[0][r, :].astype(F32)
            for src in srcs[1:]:
                total = total + src[r, :].astype(F32)
            dst[r, :] = total.astype(BF)
            return carry

        lax.fori_loop(0, dst.shape[0] // step, body, 0)

    def rs_start(name, dests=(3, 0, 2, 1)):
        for d in range(len(o_pieces)) if name == "o" else dests:
            send(lambda d=d: rs_y(name, d))

    def rs_stage(name, d, j):
        g, yr, zr, i = reduces[name]

        def side(pos, up):
            def run():
                if name in ZFIRST:
                    if j > 0:
                        own = g.at[pl.ds(bp * d, bp)]
                        rs_z(name, d, d, up).wait_recv()
                        add_up(own, [own, zr.at[d]])
                    return
                rs_y(name, d).wait_recv()
                if name == "o":
                    r0, nr = o_pieces[d]
                    own, mine, past = g.at[rows_of(0, y, r0, nr)], yr.at[0, pl.ds(r0, nr)], zr.at[0, pl.ds(r0, nr)]
                else:
                    own, mine, past = g.at[rows_of(d, y)], yr.at[d], zr.at[d]
                srcs = [own, mine]
                if j > 0:
                    rs_z(name, d, 0 if name == "o" else d, up).wait_recv()
                    srcs.append(past)
                add_up(mine, srcs)

            nxt = pos + 1 if up else pos - 1
            if name == "o":
                last = t == nxt
                cond = both(z == pos, (t > pos) if up else (t < pos))
                pl.when(cond)(run)
                if up:
                    send(lambda: rs_z(name, d, 1, True), lambda: both(cond, last))
                    send(lambda: rs_z(name, d, 0, True), lambda: both(cond, jnp.logical_not(last)))
                else:
                    send(lambda: rs_z(name, d, 0, False), lambda: cond)
            else:
                cond = z == pos
                pl.when(cond)(run)
                slot = NZ if (up and nxt == d) else d
                send(lambda: rs_z(name, d, slot, up), lambda: cond)

        if name == "o":
            if j < NZ - 1:
                side(j, True)
                side(NZ - 1 - j, False)
            return
        if j < d:
            side(j, True)
        if NZ - 1 - j > d:
            side(NZ - 1 - j, False)

    def rs_line(name):
        g, yr, zr, i = reduces[name]
        own = g.at[pl.ds(base, bp)]

        def run(slots):
            def go_():
                for slot in slots:
                    rs_z(name, slot if slot < NZ else 0, slot, True).wait_recv()
                add_up(own, [own] + [zr.at[slot] for slot in slots])
            return go_

        for k in range(NZ):
            pl.when(z == k)(run(([k] if k < NZ - 1 else []) + ([NZ] if k > 0 else [])))
        send(lambda: rs_y(name, 0))

    def rs_final(name):
        g, yr, zr, i = reduces[name]
        if name in ZFIRST:
            rs_y(name, 0).wait_recv()
            add_up(yr.at[0], [g.at[rows_of(z, y)], yr.at[0]])
            return
        out = name == "o"
        me = 0 if out else z
        here = (t == z) if out else (z >= 0)
        above = 0 if out else z
        below = 1 if out else NZ

        def run(has_above, has_below):
            def go_():
                parts = range(len(o_pieces)) if out else [me]
                for d in parts:
                    rs_y(name, d).wait_recv()
                srcs = [g.at[rows_of(me, y)], yr.at[me]]
                if has_above:
                    for d in parts:
                        rs_z(name, d, above, True).wait_recv()
                    srcs.append(zr.at[above])
                if has_below:
                    for d in parts:
                        rs_z(name, d, below, True).wait_recv()
                    srcs.append(zr.at[below])
                add_up(yr.at[me], srcs)
            return go_

        pl.when(both(here, z == 0))(run(True, False))
        pl.when(both(here, z == NZ - 1))(run(False, True))
        pl.when(both(here, both(z > 0, z < NZ - 1)))(run(True, True))

    outs = {"q": gq_o, "f": gf_o, "p": gp_o, "o": go_o}

    def fin_view(name, tt, yy):
        return outs[name].at[yy] if name == "o" else outs[name].at[tt * 2 + yy]

    def fin_copy(name, src, tt, yy, k, dev):
        i = reduces[name][3]
        slot = yy if name == "o" else tt * 2 + yy
        return remote(src, fin_view(name, tt, yy), fin_sem.at[i, k], fin_sem.at[i, 8 + slot], dev)

    def own_block(name):
        yr = reduces[name][1]
        return yr.at[0] if name == "o" or name in ZFIRST else yr.at[z]

    def keep_own(name):
        return pltpu.make_async_copy(own_block(name), fin_view(name, t, y), fin_sem.at[reduces[name][3], 7])

    tx = 2 * (1 - x) + c

    def fin_start(name):
        here = (lambda: t == z) if name == "o" else None
        if here is None:
            keep_own(name).start()
        else:
            pl.when(here())(lambda: keep_own(name).start())
        send(lambda: fin_copy(name, own_block(name), t, y, 0, y_dev), here)
        send(lambda: fin_copy(name, own_block(name), t, y, 1, x_dev), here)
        send(lambda: fin_copy(name, own_block(name), t, y, 2, core_dev), here)

    def fin_wait(name, tt, yy):
        fin_copy(name, fin_view(name, tt, yy), tt, yy, 0, core_dev).wait_recv()

    def fin_forward(name, turn):
        steps = [(t, 1 - y, x_dev), (tx, y, None), (tx, 1 - y, None)]
        if name in YWAY:
            steps = [(tx, y, y_dev), (t, 1 - y, None), (tx, 1 - y, None)]
        tt, yy, dev = steps[turn]
        here = (tt == z) if name == "o" else (z >= 0)
        v = fin_view(name, tt, yy)
        pl.when(here)(lambda: fin_wait(name, tt, yy))
        if dev is not None:
            send(lambda: fin_copy(name, v, tt, yy, 3, dev), lambda: here)
        send(lambda: fin_copy(name, v, tt, yy, 4 + turn, core_dev), lambda: here)

    def fin_finish(name):
        if name == "o":
            here = lax.rem(z, 2) != c
            for yy in range(2):
                pl.when(here)(lambda yy=yy: fin_wait(name, 0, yy))
            pl.when(t == z)(lambda: keep_own(name).wait())
        else:
            for xx in range(2):
                for yy in range(2):
                    fin_wait(name, 2 * xx + (1 - c), yy)
            keep_own(name).wait()

    def prepare(rq, rt, ro, rd, turned):
        loads = [
            pltpu.make_async_copy(wq_h, rq, raw_sem.at[0]),
            pltpu.make_async_copy(tok_h, rt, raw_sem.at[1]),
            pltpu.make_async_copy(wo_h, ro, raw_sem.at[2]),
            pltpu.make_async_copy(dy_h, rd, raw_sem.at[3]),
        ]
        for load in loads:
            load.start()
        lnv[...] = jnp.zeros_like(lnv)
        for k, ref in enumerate((g1_i, b1_i, g2_i, b2_i)):
            lnv[k : k + 1, 0:blk] = ref[...].astype(F32).reshape(1, blk)
        lnr[z] = lnv[...]
        for k in range(1, NZ):
            send(lambda k=k: remote(lnv, lnr.at[z], ln_sem.at[k - 1], ln_sem.at[2 + k], others[k - 1]))

        loads[0].wait()
        wq[pl.ds(base, bp), :] = jnp.zeros((bp, nq), BF)
        for k in range(NT):
            @pl.when(t == k)
            def _(k=k):
                for j in range(3):
                    wq[pl.ds(base, blk), blk * j : blk * (j + 1)] = rq[:, dim * j + blk * k : dim * j + blk * (k + 1)]
        ag_start("q")

        turned[...] = jnp.zeros_like(turned)

        def spread(dst, src):
            for j in range(NZ):
                turned[bp * j : bp * j + blk, :] = src[blk * j : blk * (j + 1), :]
            dst[...] = turned[...].T

        loads[1].wait()
        for s in range(WAVES):
            spread(xown.at[s], rt.at[s])
            sent = jnp.where(lane == blk, len_s[s].astype(F32), xown[s].astype(F32))
            tok[blk_of(s, c, x)] = sent.astype(BF)
            xg_start(tok, 0, s, track=False)
        loads[2].wait()

        @pl.when(t == z)
        def _():
            wo[...] = jnp.zeros_like(wo)
            for j in range(NZ):
                wo[0:blk, bp * j : bp * j + blk] = ro[:, blk * j : blk * (j + 1)]
        ag_start("o")
        loads[3].wait()
        for s in range(WAVES):
            spread(dys.at[blk_of(s, c, x)], rd.at[s])
            xg_start(dys, 1, s)

    def prepare_mlp(rf, rp):
        loads = [
            pltpu.make_async_copy(wf_h, rf, raw_sem.at[4]),
            pltpu.make_async_copy(wp_h.at[pl.ds(pl.multiple_of(blk * t, 8), blk)], rp, raw_sem.at[5]),
        ]
        for load in loads:
            load.start()
        loads[0].wait()
        wf[pl.ds(base, bp), :] = jnp.zeros((bp, dp), BF)
        for k in range(NT):
            @pl.when(t == k)
            def _(k=k):
                for j in range(NZ):
                    lo = (ff // NZ) * j + blk * k
                    wf[pl.ds(base, blk), bp * j : bp * j + blk] = rf[:, lo : lo + blk]
        loads[1].wait()
        wp[pl.ds(base, bp), :] = jnp.zeros((bp, dp), BF)
        for j in range(NZ):
            wp[pl.ds(base, blk), bp * j : bp * j + blk] = rp[:, blk * j : blk * (j + 1)]

    pl.run_scoped(
        prepare,
        pltpu.VMEM((blk, 3 * dim), BF),
        pltpu.VMEM((WAVES, dim, SEQ), BF),
        pltpu.VMEM((blk, dim), BF),
        pltpu.VMEM((WAVES, dim, SEQ), BF),
        pltpu.VMEM((dp, SEQ), BF),
    )
    pl.run_scoped(prepare_mlp, pltpu.VMEM((blk, ff), BF), pltpu.VMEM((blk, dim), BF))

    def main(first, pm):
        for k in range(1, NZ):
            remote(lnv, lnr.at[lax.rem(z + NZ - k, NZ)], ln_sem.at[k - 1], ln_sem.at[2 + k], others[k - 1]).wait_recv()
        vec[...] = jnp.zeros_like(vec)
        for j in range(NZ):
            vec[:, bp * j : bp * j + blk] = lnr[j, :, 0:blk]
        lg[...] = jnp.zeros_like(lg)
        dqkv[...] = jnp.zeros_like(dqkv)

        def stats(rows):
            mean = jnp.sum(rows, axis=-1, keepdims=True) * inv_dim
            cen = (rows - mean) * livef
            inv = lax.rsqrt(jnp.sum(cen * cen, axis=-1, keepdims=True) * inv_dim + EPS)
            return cen * inv, inv

        def norm_back(e, n, inv):
            me = jnp.sum(e, axis=-1, keepdims=True) * inv_dim
            mn = jnp.sum(e * n, axis=-1, keepdims=True) * inv_dim
            return inv * (e - me - n * mn) * livef

        def ln_first(s):
            def body(i, carry):
                b = s * NT + i
                raw = tok[b].astype(F32)
                lens[b] = jnp.broadcast_to(raw[0:8, blk : blk + 1], (8, SEQ))
                n, inv = stats(raw * livef)
                first[b] = (n * vec[0:1, :] + vec[1:2, :]).astype(BF)
                return carry
            lax.fori_loop(0, NT, body, 0)

        lane_h = lax.broadcasted_iota(jnp.int32, (1, bp), 1)
        head_masks = [(lane_h >= head * h) & (lane_h < head * (h + 1)) for h in range(nh)]

        def stack_heads(v):
            zero = jnp.zeros_like(v)
            return jnp.concatenate([jnp.where(m, v, zero) for m in head_masks], axis=0)

        def side_by_side(v):
            return jnp.concatenate([v[SEQ * h : SEQ * (h + 1)] for h in range(nh)], axis=1)

        def project(s):
            def body(i, carry):
                b = s * NT + i * 2
                rows = first[pl.ds(b, 2)].reshape(2 * SEQ, dp)
                out = nn(rows, wq[...])
                for j, ref in enumerate((qs, ks, vs)):
                    ref[pl.ds(b, 2)] = out[:, blk * j : blk * j + bp].astype(BF).reshape(2, SEQ, bp)
                return carry
            lax.fori_loop(0, 2, body, 0)

        def attend(s):
            q_pos = lax.broadcasted_iota(jnp.int32, (SEQ, SEQ), 0)
            k_pos = lax.broadcasted_iota(jnp.int32, (SEQ, SEQ), 1)

            def body(i, carry):
                b = s * NT + i
                scores = nt(stack_heads(qs[b]), ks[b]) * scale
                ok = (k_pos <= q_pos) & (k_pos.astype(F32) < lens[b, 0:1, :])
                bias = jnp.concatenate([ok.astype(F32)] * nh, axis=0) > 0.5
                scores = jnp.where(bias, scores, MASKED)
                top = jnp.max(scores, axis=-1, keepdims=True)
                ex = jnp.exp(scores - top)
                prob = ex / jnp.sum(ex, axis=-1, keepdims=True)
                pm[b] = prob
                out = nn(side_by_side(prob.astype(BF)), stack_heads(vs[b]))
                att[b] = out.astype(BF)
                return carry
            lax.fori_loop(0, NT, body, 0)

        def matmul_part(src, weight, s, transposed, e):
            width = src.shape[2]
            dst = part_of(e)

            def body(i, carry):
                b = s * NT + i * 2
                rows = src[pl.ds(b, 2)].reshape(2 * SEQ, width)
                out = nt(rows, weight[...]) if transposed else nn(rows, weight[...])
                dst[pl.ds(b, 2)] = out.astype(BF).reshape(2, SEQ, dp)
                return carry
            lax.fori_loop(0, 2, body, 0)

        def mid(s):
            rows = xown[s].astype(F32) + ex_sum(0, s)
            mix[s] = rows
            n, inv = stats(rows)
            sec[blk_of(s, c, x)] = (n * vec[2:3, :] + vec[3:4, :]).astype(BF)
            xg_start(sec, 2, s)

        def expand(s):
            def body(i, carry):
                b = s * NT + i * 2
                rows = sec[pl.ds(b, 2)].reshape(2 * SEQ, dp)
                pre = nn(rows, wf[...])
                sq = pre * pre
                th = jnp.tanh(GELU_C * (pre + GELU_A * (pre * sq)))
                half = 0.5 * (1.0 + th)
                act[pl.ds(b, 2)] = (pre * half).astype(BF).reshape(2, SEQ, dp)
                slope = half + (0.5 * GELU_C) * pre * (1.0 - th * th) * (1.0 + (3.0 * GELU_A) * sq)
                gel[pl.ds(b, 2)] = slope.astype(BF).reshape(2, SEQ, dp)
                return carry
            lax.fori_loop(0, 2, body, 0)

        def grad_of(dst, left, right):
            step = 384
            rows = NB * SEQ

            def body(j, carry):
                cols = pl.ds(pl.multiple_of(j * step, step), step)
                out = tn(left[:, :, cols].reshape(rows, step), right[...].reshape(rows, right.shape[2]))
                dst[cols, :] = out.astype(BF)
                return carry
            lax.fori_loop(0, dp // step, body, 0)

        def back_act(s):
            def body(i, carry):
                b = s * NT + i * 2
                d_act = nt(dys[pl.ds(b, 2)].reshape(2 * SEQ, dp), wp[...])
                slope = gel[pl.ds(b, 2)].reshape(2 * SEQ, dp).astype(F32)
                gel[pl.ds(b, 2)] = (d_act * slope).astype(BF).reshape(2, SEQ, dp)
                return carry
            lax.fori_loop(0, 2, body, 0)

        def back_mid(s):
            d2 = ex_sum(2, s)
            n, inv = stats(mix[s])
            lg[2:3, :] = lg[2:3, :] + jnp.sum(d2 * n, axis=0, keepdims=True)
            lg[3:4, :] = lg[3:4, :] + jnp.sum(d2, axis=0, keepdims=True)
            rows = dys[blk_of(s, c, x)].astype(F32) + norm_back(d2 * vec[2:3, :], n, inv)
            dmix[s] = rows
            tok[blk_of(s, c, x)] = rows.astype(BF)
            xg_start(tok, 3, s)

        def back_attend(s):
            def proj(i, carry):
                b = s * NT + i * 2
                out = nt(tok[pl.ds(b, 2)].reshape(2 * SEQ, dp), wo[...])
                datt[pl.ds(b, 2)] = out.astype(BF).reshape(2, SEQ, bp)
                return carry
            lax.fori_loop(0, 2, proj, 0)

            def body(i, carry):
                b = s * NT + i
                d_out = stack_heads(datt[b])
                prob = pm[b]
                d_prob = nt(d_out, vs[b])
                total = jnp.sum(prob * d_prob, axis=-1, keepdims=True)
                d_scores = (prob * (d_prob - total)).astype(BF)
                dqkv[b, :, 0:bp] = (nn(side_by_side(d_scores), stack_heads(ks[b])) * scale).astype(BF)
                dqkv[b, :, blk : blk + bp] = (tn(d_scores, stack_heads(qs[b])) * scale).astype(BF)
                dqkv[b, :, 2 * blk : 2 * blk + bp] = tn(prob.astype(BF), d_out).astype(BF)
                return carry
            lax.fori_loop(0, NT, body, 0)

        def back_first(s):
            d1 = ex_sum(3, s)
            n, inv = stats(xown[s].astype(F32))
            lg[0:1, :] = lg[0:1, :] + jnp.sum(d1 * n, axis=0, keepdims=True)
            lg[1:2, :] = lg[1:2, :] + jnp.sum(d1, axis=0, keepdims=True)
            gtok_o[s] = (dmix[s] + norm_back(d1 * vec[0:1, :], n, inv)).astype(BF)

        def grad_out():
            rows_all = NB * SEQ
            go[...] = tn(att[...].reshape(rows_all, bp), tok[...].reshape(rows_all, dp)).astype(BF)

        def finish_rows(s):
            res_o[s] = (mix[s] + ex_sum(1, s)).astype(BF)

        hops = [
            remote(lg, lr.at[k], ln_sem.at[6 + 2 * k], ln_sem.at[7 + 2 * k], dev)
            for k, dev in enumerate((core_dev, x_dev, y_dev))
        ]

        def ln_add(k):
            hops[k].wait()
            lg[...] = lg[...] + lr[k]

        def ln_line(k):
            return remote(lg, lz.at[k - 1], ln_sem.at[11 + k], ln_sem.at[14 + k], others[k - 1])

        def ln_send():
            for k in range(1, NZ):
                send(lambda k=k: ln_line(k))

        def ln_total():
            for k in range(1, NZ):
                ln_line(k).wait_recv()
            total = lg[...] + lz[0] + lz[1] + lz[2]
            for j in range(NZ):
                @pl.when(z == j)
                def _(j=j):
                    gln_o[:, 0:blk] = total[:, bp * j : bp * j + blk]

        ag_forward("q", 1)
        ag_forward("q", 2)
        ag_forward("q", 3)
        ag_forward("o", 1)
        ag_start("f")
        xg_forward(tok, 0, 0, track=False)
        xg_finish(tok, 0, 0)
        ln_first(0)
        ag_forward("o", 2)
        xg_forward(tok, 0, 1, track=False)
        xg_sent(tok, 0, 0)
        xg_finish(tok, 0, 1)
        xg_forward(dys, 1, 0)
        ln_first(1)
        ag_forward("o", 3)
        xg_finish(dys, 1, 0)
        ag_forward("f", 1)
        xg_sent(tok, 0, 1)
        ag_start("p")
        xg_forward(dys, 1, 1)
        ag_finish("q")
        project(0)
        attend(0)
        project(1)
        ag_finish("o")
        attend(1)
        matmul_part(att, wo, 0, False, 0)
        ex_a(0, 0).start()
        ag_forward("f", 2)
        ex_relay(0, 0)
        ag_forward("p", 1)
        matmul_part(att, wo, 1, False, 0)
        ex_a(0, 1).start()
        ex_relay(0, 1)
        ag_forward("f", 3)
        mid(0)
        ex_b(0, 1).wait_send()
        xg_forward(sec, 2, 0)
        ag_forward("p", 2)
        xg_finish(dys, 1, 1)
        ex_b(0, 0).wait_send()
        mid(1)
        ex_a(0, 1).wait_send()
        ex_a(0, 0).wait_send()
        ag_finish("f")
        xg_finish(sec, 2, 0)
        expand(0)
        ag_forward("p", 3)
        xg_forward(sec, 2, 1)
        xg_finish(sec, 2, 1)
        expand(1)
        grad_of(gp, act, dys)
        ag_finish("p")
        rs_stage("p", 3, 0)
        rs_stage("p", 0, 0)
        back_act(1)
        rs_stage("p", 1, 0)
        back_act(0)
        matmul_part(gel, wf, 0, True, 2)
        ex_a(2, 0).start()
        grad_of(gf, sec, gel)
        rs_start("f")
        ex_relay(2, 0)
        matmul_part(act, wp, 1, False, 1)
        ex_a(1, 1).start()
        matmul_part(gel, wf, 1, True, 2)
        ex_a(2, 1).start()
        back_mid(0)
        ex_relay(2, 1)
        matmul_part(act, wp, 0, False, 1)
        ex_a(1, 0).start()
        rs_stage("p", 2, 0)
        rs_stage("f", 0, 0)
        ex_a(2, 1).wait_send()
        xg_forward(tok, 3, 0)
        rs_stage("p", 0, 1)
        back_mid(1)
        ex_a(2, 0).wait_send()
        ex_relay(1, 0)
        rs_stage("f", 3, 0)
        xg_finish(tok, 3, 0)
        back_attend(0)
        rs_stage("p", 3, 1)
        xg_forward(tok, 3, 1)
        xg_finish(tok, 3, 1)
        back_attend(1)
        grad_of(gq, first, dqkv)
        rs_stage("f", 2, 0)
        rs_start("q")
        rs_stage("p", 1, 1)
        rs_stage("p", 2, 1)
        ex_b(2, 0).wait_send()
        grad_out()
        rs_stage("f", 0, 1)
        ex_relay(1, 1)
        rs_stage("f", 3, 1)
        rs_stage("p", 0, 2)
        matmul_part(dqkv, wq, 1, True, 3)
        ex_a(3, 1).start()
        rs_stage("f", 1, 0)
        ex_b(2, 1).wait_send()
        rs_stage("p", 3, 2)
        matmul_part(dqkv, wq, 0, True, 3)
        ex_a(3, 0).start()
        rs_stage("f", 2, 1)
        rs_stage("q", 0, 0)
        ex_relay(3, 0)
        rs_stage("f", 0, 2)
        rs_stage("q", 3, 0)
        finish_rows(0)
        rs_line("p")
        ex_relay(3, 1)
        rs_stage("q", 2, 0)
        rs_stage("f", 3, 2)
        rs_start("o")
        back_first(0)
        rs_stage("q", 3, 1)
        rs_stage("q", 0, 1)
        rs_stage("q", 2, 1)
        finish_rows(1)
        rs_stage("f", 1, 1)
        back_first(1)
        rs_stage("q", 1, 0)
        rs_final("p")
        hops[0].start()
        fin_start("p")
        rs_stage("q", 3, 2)
        rs_final("f")
        rs_stage("o", 0, 0)
        rs_stage("q", 1, 1)
        rs_stage("o", 0, 1)
        rs_stage("o", 1, 0)
        rs_stage("o", 2, 0)
        ln_add(0)
        rs_stage("q", 0, 2)
        hops[1].start()
        fin_start("f")
        rs_final("q")
        fin_forward("p", 0)
        ln_add(1)
        rs_stage("o", 1, 1)
        fin_start("q")
        rs_final("o")
        fin_start("o")
        rs_stage("o", 2, 1)
        hops[2].start()
        rs_stage("o", 0, 2)
        rs_stage("o", 1, 2)
        fin_forward("o", 0)
        rs_stage("o", 2, 2)
        fin_forward("f", 0)
        fin_forward("f", 1)
        fin_forward("q", 0)
        fin_forward("p", 1)
        ln_add(2)
        ln_send()
        fin_forward("q", 1)
        fin_forward("p", 2)
        fin_forward("o", 2)
        fin_forward("f", 2)
        fin_forward("o", 1)
        fin_forward("q", 2)
        ln_total()
        for name in ("p", "f", "o", "q"):
            fin_finish(name)
        for s in range(WAVES):
            for e in (1, 3):
                ex_a(e, s).wait_send()
                ex_b(e, s).wait_send()
        for cond, make in ends:
            if cond is None:
                make().wait_send()
            else:
                pl.when(cond())(lambda make=make: make().wait_send())

    pl.run_scoped(main, pltpu.VMEM((NB, SEQ, dp), BF), pltpu.VMEM((NB, nh * SEQ, SEQ), F32))


def layer_call(dim, ff, tokens, cot, w_qkv, w_out, w_fc, w_proj, lengths, norms):
    blk = dim // NZ
    bp = up16(blk)
    hb = bp // 2
    dp = NZ * bp
    nq = up128(3 * blk)
    vm, dma = pltpu.VMEM, pltpu.SemaphoreType.DMA
    big = (NB, SEQ, dp)
    half = lambda k: (1 if k in ZFIRST else NZ, hb, nq if k == "q" else dp)
    line = lambda k: (NZ + 1, bp if k in ZFIRST else hb, nq if k == "q" else dp)
    scratch = [
        vm(big, BF), vm(big, BF), vm((WAVES, SEQ, dp), BF),
        vm((dp, nq), BF), vm((bp, dp), BF), vm((dp, dp), BF), vm((dp, dp), BF),
        vm((NB, SEQ, bp), BF), vm((NB, SEQ, bp), BF), vm((NB, SEQ, bp), BF),
        vm((NB, SEQ, bp), BF),
        vm(big, BF), vm(big, BF),
        vm((2, WAVES, 2, SEQ, dp), BF), vm((2, WAVES, SEQ, dp), BF), vm((2, WAVES, SEQ, dp), BF),
        vm((WAVES, SEQ, dp), F32), vm((WAVES, SEQ, dp), F32),
        vm(big, BF), vm(big, BF), vm(big, BF),
        vm((NB, SEQ, bp), BF), vm((NB, SEQ, nq), BF),
        vm((dp, nq), BF), vm((bp, dp), BF), vm((dp, dp), BF), vm((dp, dp), BF),
        vm(half("q"), BF), vm((1, hb, dp), BF), vm(half("f"), BF), vm(half("p"), BF),
        vm(line("q"), BF), vm((2, hb, dp), BF), vm(line("f"), BF), vm(line("p"), BF),
        vm((8, up128(blk)), F32), vm((NZ, 8, up128(blk)), F32), vm((8, dp), F32), vm((NB, 8, SEQ), F32),
        vm((8, dp), F32), vm((3, 8, dp), F32), vm((3, 8, dp), F32),
        dma((6,)), dma((19, 5)), dma((4, 18)), dma((4, 16)), dma((8, 6)), dma((8, 4)), dma((18,)),
    ]
    hbm = pl.BlockSpec(memory_space=pl.ANY)
    inv = pl.BlockSpec(memory_space=pltpu.VMEM)
    shape = jax.ShapeDtypeStruct

    def body(*refs):
        layer_kernel(dim, ff, *refs)

    return pl.pallas_call(
        body,
        out_shape=(
            shape((WAVES, SEQ, dp), BF), shape((WAVES, SEQ, dp), BF),
            shape((8, hb, nq), BF), shape((2, hb, dp), BF), shape((8, hb, dp), BF), shape((8, hb, dp), BF),
            shape((8, up128(blk)), F32),
        ),
        in_specs=[hbm] * 6 + [pl.BlockSpec(memory_space=pltpu.SMEM)] + [inv] * 4,
        out_specs=(inv, inv, hbm, hbm, hbm, hbm, inv),
        scratch_shapes=scratch,
        compiler_params=pltpu.CompilerParams(
            collective_id=0, has_side_effects=True, vmem_limit_bytes=67043328
        ),
    )(tokens, cot, w_qkv, w_out, w_fc, w_proj, lengths, *norms)


def finish_kernel(dim, ff, res, gtok, gq, go, gf, gp, gln, res_o, gtok_o, gq_o, go_o, gf_o, gp_o, *norms_o):
    blk = dim // NZ
    bp = up16(blk)
    for j in range(NZ):
        there = slice(bp * j, bp * j + blk)
        go_o[:, blk * j : blk * (j + 1)] = go[:, there].astype(F32)
        for t in range(NT):
            gp_o[t, :, blk * j : blk * (j + 1)] = gp[t, :, there].astype(F32)
            lo = (ff // NZ) * j + blk * t
            gf_o[:, lo : lo + blk] = gf[t, :, there].astype(F32)
    for j in range(3):
        for t in range(NT):
            lo = dim * j + blk * t
            gq_o[:, lo : lo + blk] = gq[t, :, blk * j : blk * (j + 1)].astype(F32)

    @pl.when(pl.program_id(0) == 0)
    def _():
        for k, ref in enumerate(norms_o):
            ref[...] = gln[k : k + 1, 0:blk].reshape(blk)
        for src, dst in ((res, res_o), (gtok, gtok_o)):
            for s in range(WAVES):
                turned = src[s].T
                for j in range(NZ):
                    dst[s, blk * j : blk * (j + 1), :] = turned[bp * j : bp * j + blk, :]


def finish_call(dim, ff, res, gtok, gq, go, gf, gp, gln):
    blk = dim // NZ
    bp = up16(blk)
    dp = NZ * bp
    nq = gq.shape[2]
    step = 56
    shape, spec = jax.ShapeDtypeStruct, pl.BlockSpec
    whole = spec(memory_space=pltpu.VMEM)
    quarters = lambda n: spec((NT, step, n), lambda i: (0, i, 0))
    lines = lambda n: spec((step, n), lambda i: (i, 0))
    return pl.pallas_call(
        lambda *refs: finish_kernel(dim, ff, *refs),
        grid=(blk // step,),
        in_specs=[whole, whole, quarters(nq), lines(dp), quarters(dp), quarters(dp), whole],
        out_specs=[whole, whole, lines(3 * dim), lines(dim), lines(ff), quarters(dim)] + [whole] * 4,
        out_shape=[
            shape((WAVES, dim, SEQ), BF), shape((WAVES, dim, SEQ), BF),
            shape((blk, 3 * dim), F32), shape((blk, dim), F32), shape((blk, ff), F32), shape((NT, blk, dim), F32),
        ] + [shape((blk,), F32)] * 4,
        compiler_params=pltpu.CompilerParams(vmem_limit_bytes=67043328),
    )(
        res, gtok, gq.reshape(NT, bp, nq), go.reshape(bp, dp), gf.reshape(NT, bp, dp), gp.reshape(NT, bp, dp), gln
    )


def sum_boxes(value, wide):
    total = value
    for k in range(1, wide // 8):
        total = total + lax.ppermute(value, "wide", [(i, (i + 8 * k) % wide) for i in range(wide)])
    return total


def solution(mesh):
    wide, narrow = mesh.shape["wide"], mesh.shape["narrow"]
    assert narrow == NZ and wide % 8 == 0

    def shards(tokens, lengths, ln1_gain, ln1_bias, w_qkv, w_out, ln2_gain, ln2_bias, w_fc, w_proj, cotangent):
        cells, seq, dim = tokens.shape
        assert cells == WAVES and seq == SEQ
        ff = w_fc.shape[1]
        blk = dim // NZ
        bp = up16(blk)
        res, gtok, gq, go, gf, gp, gln = layer_call(
            dim, ff, tokens.transpose(0, 2, 1), cotangent.transpose(0, 2, 1),
            w_qkv, w_out, w_fc, w_proj, lengths, (ln1_gain, ln1_bias, ln2_gain, ln2_bias),
        )
        res, gtok, *grads = finish_call(dim, ff, res, gtok, gq, go, gf, gp, gln)
        gq, go, gf, gp, g1, b1, g2, b2 = [sum_boxes(g, wide) for g in grads]
        return (
            res.transpose(0, 2, 1), gtok.transpose(0, 2, 1), g1, b1, gq, go, g2, b2, gf, gp.reshape(ff // NZ, dim)
        )

    rows = P(("wide", "narrow"), None, None)
    vec, mat = P("narrow"), P("narrow", None)
    return jax.shard_map(
        shards,
        mesh=mesh,
        in_specs=(rows, P(("wide", "narrow")), vec, vec, mat, mat, vec, vec, mat, mat, rows),
        out_specs=(rows, rows, vec, vec, mat, mat, vec, vec, mat, mat),
        check_vma=False,
    )
```

```python
import math

import jax
import jax.numpy as jnp
from jax import lax
from jax.experimental import pallas as pl
from jax.experimental.pallas import tpu as pltpu
from jax.sharding import PartitionSpec as P

HEADS = 20
EPS = 1e-05
MASKED = -1e30
BF, F32 = jnp.bfloat16, jnp.float32
MESH = pl.DeviceIdType.MESH

NZ = 4
NT = 4
WAVES = 2
SEQ = 128
NB = NT * WAVES
GELU_C = math.sqrt(2.0 / math.pi)
GELU_A = 0.044715
YWAY = ("f", "q",)
ZFIRST = ("p",)


def up16(n):
    return -(-n // 16) * 16


def up128(n):
    return -(-n // 128) * 128


def nn(a, b):
    return lax.dot_general(a, b, (((1,), (0,)), ((), ())), preferred_element_type=F32)


def nt(a, b):
    return lax.dot_general(a, b, (((1,), (1,)), ((), ())), preferred_element_type=F32)


def tn(a, b):
    return lax.dot_general(a, b, (((0,), (0,)), ((), ())), preferred_element_type=F32)


def layer_kernel(
    dim, ff,
    tok_h, dy_h, wq_h, wo_h, wf_h, wp_h, len_s, g1_i, b1_i, g2_i, b2_i,
    res_o, gtok_o, gq_o, go_o, gf_o, gp_o, gln_o,
    tok, dys, xown, wq, wo, wf, wp, qs, ks, vs, att, part, part1, ra, sb, rb, mix, dmix,
    sec, act, gel, datt, dqkv, gq, go, gf, gp, yq, yo, yf, yp, zq, zo, zf, zp,
    lnv, lnr, vec, lens, lg, lr, lz,
    raw_sem, ag_sem, rs_sem, fin_sem, xs_sem, xa_sem, ln_sem,
):
    blk = dim // NZ
    bp = up16(blk)
    hb = bp // 2
    dp = NZ * bp
    nq = wq.shape[1]
    head = dim // HEADS
    nh = HEADS // NT
    inv_dim = 1.0 / dim
    scale = head ** (-0.5)

    w = lax.axis_index("wide")
    z = lax.axis_index("narrow")
    c = lax.rem(w, 2)
    x = lax.rem(w // 2, 2)
    y = lax.rem(w // 4, 2)
    t = 2 * x + c
    core_dev = (w + 1 - 2 * c, z)
    x_dev = (w + 2 - 4 * x, z)
    y_dev = (w + 4 - 8 * y, z)
    up_dev = (w, z + 1)
    down_dev = (w, z - 1)

    ends = []

    def remote(src, dst, ssem, rsem, dev):
        return pltpu.make_async_remote_copy(
            src_ref=src, dst_ref=dst, send_sem=ssem, recv_sem=rsem, device_id=dev, device_id_type=MESH
        )

    def send(make, cond=None, track=True):
        if cond is None:
            make().start()
        else:
            pl.when(cond())(lambda: make().start())
        if track:
            ends.append((cond, make))

    def both(a, b):
        return jnp.logical_and(a, b)

    lane = lax.broadcasted_iota(jnp.int32, (1, dp), 1)
    live = lax.rem(lane, bp) < blk
    livef = live.astype(F32)

    barrier = pltpu.get_barrier_semaphore()
    others = [(w, lax.rem(z + k, NZ)) for k in range(1, NZ)]
    for dev in [core_dev, x_dev, y_dev] + others:
        pl.semaphore_signal(barrier, inc=1, device_id=dev, device_id_type=MESH)

    def rows_of(s, yy, r0=0, nr=None):
        return pl.ds(pl.multiple_of(bp * s + hb * yy + r0, 16), hb if nr is None else nr)

    q_pieces = [(0, 80), (80, hb - 80)]
    o_pieces = [(0, 48), (48, 48), (96, hb - 96)]
    gathers = {
        "q": (wq, 0, q_pieces),
        "f": (wf, 4 * len(q_pieces), [(0, hb)]),
        "p": (wp, 4 * len(q_pieces) + 4, [(0, hb)]),
        "o": (wo, 4 * len(q_pieces) + 8, o_pieces),
    }

    def ag_view(name, s, yy, piece):
        ref, base, pieces = gathers[name]
        r0, nr = pieces[piece]
        if name == "o":
            return ref.at[rows_of(0, yy, r0, nr)]
        return ref.at[rows_of(s, yy, r0, nr)]

    def ag_id(name, s, piece):
        ref, base, pieces = gathers[name]
        return base + piece if name == "o" else base + 4 * piece + s

    def ag_z(name, s, piece, up):
        v = ag_view(name, s, y, piece)
        i = ag_id(name, s, piece)
        return remote(v, v, ag_sem.at[i, 0 if up else 1], ag_sem.at[i, 2], up_dev if up else down_dev)

    def ag_y(name, s, yy, piece):
        v = ag_view(name, s, yy, piece)
        i = ag_id(name, s, piece)
        return remote(v, v, ag_sem.at[i, 3], ag_sem.at[i, 4], y_dev)

    def ag_start(name):
        for piece in range(len(gathers[name][2])):
            def own():
                return (t == z) if name == "o" else (z >= 0)

            send(lambda p=piece: ag_z(name, z, p, True), lambda: both(own(), z < NZ - 1))
            send(lambda p=piece: ag_z(name, z, p, False), lambda: both(own(), z > 0))

    def ag_forward(name, k):
        for piece in range(len(gathers[name][2])):
            for up in (True, False):
                s = z - k if up else z + k
                ok = (z >= k) if up else (z + k <= NZ - 1)
                if name == "o":
                    ok = t == s
                more = (z < NZ - 1) if up else (z > 0)
                pl.when(ok)(lambda s=s, p=piece, u=up: ag_z(name, s, p, u).wait_recv())
                send(lambda s=s, p=piece, u=up: ag_z(name, s, p, u), lambda ok=ok, more=more: both(ok, more))
                send(lambda s=s, p=piece: ag_y(name, s, y, p), lambda ok=ok: ok)

    def ag_finish(name):
        for piece in range(len(gathers[name][2])):
            if name == "o":
                pl.when(z != t)(lambda p=piece: ag_y(name, 0, 1 - y, p).wait_recv())
            else:
                for s in range(NZ):
                    pl.when(z != s)(lambda s=s, p=piece: ag_y(name, s, 1 - y, p).wait_recv())

    def blk_of(s, cc, xx):
        return s * NT + cc * 2 + xx

    def xg(ref, e, s, kind):
        i = 2 * e + s
        if kind == "x":
            v = ref.at[blk_of(s, c, x)]
            return remote(v, v, xs_sem.at[i, 0], xs_sem.at[i, 1], x_dev)
        if kind == "own":
            v = ref.at[blk_of(s, c, x)]
            return remote(v, v, xs_sem.at[i, 2], xs_sem.at[i, 3], core_dev)
        v = ref.at[blk_of(s, c, 1 - x)]
        return remote(v, v, xs_sem.at[i, 4], xs_sem.at[i, 5], core_dev)

    def xg_start(ref, e, s, track=True):
        send(lambda: xg(ref, e, s, "x"), track=track)
        send(lambda: xg(ref, e, s, "own"), track=track)

    def xg_forward(ref, e, s, track=True):
        xg(ref, e, s, "x").wait_recv()
        send(lambda: xg(ref, e, s, "fwd"), track=track)

    def xg_finish(ref, e, s):
        xg(ref, e, s, "own").wait_recv()
        xg(ref, e, s, "fwd").wait_recv()

    def xg_sent(ref, e, s):
        for kind in ("x", "own", "fwd"):
            xg(ref, e, s, kind).wait_send()

    def part_of(e):
        return part1 if e == 1 else part

    def ex_a(e, s):
        i = 2 * e + s
        return remote(
            part_of(e).at[pl.ds(s * NT + (1 - c) * 2, 2)], ra.at[int(e == 1), s],
            xa_sem.at[i, 0], xa_sem.at[i, 1], core_dev,
        )

    def ex_b(e, s):
        i = 2 * e + s
        return remote(sb.at[int(e == 1), s], rb.at[int(e == 1), s], xa_sem.at[i, 2], xa_sem.at[i, 3], x_dev)

    def ex_relay(e, s):
        ex_a(e, s).wait_recv()
        sb[int(e == 1), s] = (
            part_of(e)[blk_of(s, c, 1 - x)].astype(F32) + ra[int(e == 1), s, 1 - x].astype(F32)
        ).astype(BF)
        ex_b(e, s).start()

    def ex_sum(e, s):
        ex_b(e, s).wait_recv()
        return (
            part_of(e)[blk_of(s, c, x)].astype(F32)
            + ra[int(e == 1), s, x].astype(F32)
            + rb[int(e == 1), s].astype(F32)
        )

    base = pl.multiple_of(bp * z, 16)
    reduces = {"q": (gq, yq, zq, 0), "f": (gf, yf, zf, 1), "p": (gp, yp, zp, 2), "o": (go, yo, zo, 3)}

    def rs_y(name, d):
        g, yr, zr, i = reduces[name]
        if name == "o":
            r0, nr = o_pieces[d]
            return remote(
                g.at[rows_of(0, 1 - y, r0, nr)], yr.at[0, pl.ds(r0, nr)], rs_sem.at[i, d], rs_sem.at[i, 4 + d], y_dev
            )
        if name in ZFIRST:
            return remote(g.at[rows_of(z, 1 - y)], yr.at[0], rs_sem.at[i, 0], rs_sem.at[i, 4], y_dev)
        return remote(g.at[rows_of(d, 1 - y)], yr.at[d], rs_sem.at[i, d], rs_sem.at[i, 4 + d], y_dev)

    def rs_z(name, d, slot, up):
        g, yr, zr, i = reduces[name]
        if name == "o":
            rows = pl.ds(*o_pieces[d])
            return remote(
                yr.at[0, rows], zr.at[slot, rows], rs_sem.at[i, 8 + d], rs_sem.at[i, 12 + 2 * d + slot], up_dev if up else down_dev
            )
        if name in ZFIRST:
            return remote(
                g.at[pl.ds(bp * d, bp)], zr.at[slot], rs_sem.at[i, 8 + d], rs_sem.at[i, 12 + slot], up_dev if up else down_dev
            )
        return remote(yr.at[d], zr.at[slot], rs_sem.at[i, 8 + d], rs_sem.at[i, 12 + slot], up_dev if up else down_dev)

    def add_up(dst, srcs):
        step = 48

        def body(j, carry):
            r = pl.ds(pl.multiple_of(j * step, step), step)
            total = srcs[0][r, :].astype(F32)
            for src in srcs[1:]:
                total = total + src[r, :].astype(F32)
            dst[r, :] = total.astype(BF)
            return carry

        lax.fori_loop(0, dst.shape[0] // step, body, 0)

    def rs_start(name, dests=(3, 0, 2, 1)):
        for d in range(len(o_pieces)) if name == "o" else dests:
            send(lambda d=d: rs_y(name, d))

    def rs_stage(name, d, j):
        g, yr, zr, i = reduces[name]

        def side(pos, up):
            def run():
                if name in ZFIRST:
                    if j > 0:
                        own = g.at[pl.ds(bp * d, bp)]
                        rs_z(name, d, d, up).wait_recv()
                        add_up(own, [own, zr.at[d]])
                    return
                rs_y(name, d).wait_recv()
                if name == "o":
                    r0, nr = o_pieces[d]
                    own, mine, past = g.at[rows_of(0, y, r0, nr)], yr.at[0, pl.ds(r0, nr)], zr.at[0, pl.ds(r0, nr)]
                else:
                    own, mine, past = g.at[rows_of(d, y)], yr.at[d], zr.at[d]
                srcs = [own, mine]
                if j > 0:
                    rs_z(name, d, 0 if name == "o" else d, up).wait_recv()
                    srcs.append(past)
                add_up(mine, srcs)

            nxt = pos + 1 if up else pos - 1
            if name == "o":
                last = t == nxt
                cond = both(z == pos, (t > pos) if up else (t < pos))
                pl.when(cond)(run)
                if up:
                    send(lambda: rs_z(name, d, 1, True), lambda: both(cond, last))
                    send(lambda: rs_z(name, d, 0, True), lambda: both(cond, jnp.logical_not(last)))
                else:
                    send(lambda: rs_z(name, d, 0, False), lambda: cond)
            else:
                cond = z == pos
                pl.when(cond)(run)
                slot = NZ if (up and nxt == d) else d
                send(lambda: rs_z(name, d, slot, up), lambda: cond)

        if name == "o":
            if j < NZ - 1:
                side(j, True)
                side(NZ - 1 - j, False)
            return
        if j < d:
            side(j, True)
        if NZ - 1 - j > d:
            side(NZ - 1 - j, False)

    def rs_line(name):
        g, yr, zr, i = reduces[name]
        own = g.at[pl.ds(base, bp)]

        def run(slots):
            def go_():
                for slot in slots:
                    rs_z(name, slot if slot < NZ else 0, slot, True).wait_recv()
                add_up(own, [own] + [zr.at[slot] for slot in slots])
            return go_

        for k in range(NZ):
            pl.when(z == k)(run(([k] if k < NZ - 1 else []) + ([NZ] if k > 0 else [])))
        send(lambda: rs_y(name, 0))

    def rs_final(name):
        g, yr, zr, i = reduces[name]
        if name in ZFIRST:
            rs_y(name, 0).wait_recv()
            add_up(yr.at[0], [g.at[rows_of(z, y)], yr.at[0]])
            return
        out = name == "o"
        me = 0 if out else z
        here = (t == z) if out else (z >= 0)
        above = 0 if out else z
        below = 1 if out else NZ

        def run(has_above, has_below):
            def go_():
                parts = range(len(o_pieces)) if out else [me]
                for d in parts:
                    rs_y(name, d).wait_recv()
                srcs = [g.at[rows_of(me, y)], yr.at[me]]
                if has_above:
                    for d in parts:
                        rs_z(name, d, above, True).wait_recv()
                    srcs.append(zr.at[above])
                if has_below:
                    for d in parts:
                        rs_z(name, d, below, True).wait_recv()
                    srcs.append(zr.at[below])
                add_up(yr.at[me], srcs)
            return go_

        pl.when(both(here, z == 0))(run(True, False))
        pl.when(both(here, z == NZ - 1))(run(False, True))
        pl.when(both(here, both(z > 0, z < NZ - 1)))(run(True, True))

    outs = {"q": gq_o, "f": gf_o, "p": gp_o, "o": go_o}

    def fin_view(name, tt, yy):
        return outs[name].at[yy] if name == "o" else outs[name].at[tt * 2 + yy]

    def fin_copy(name, src, tt, yy, k, dev):
        i = reduces[name][3]
        slot = yy if name == "o" else tt * 2 + yy
        return remote(src, fin_view(name, tt, yy), fin_sem.at[i, k], fin_sem.at[i, 8 + slot], dev)

    def own_block(name):
        yr = reduces[name][1]
        return yr.at[0] if name == "o" or name in ZFIRST else yr.at[z]

    def keep_own(name):
        return pltpu.make_async_copy(own_block(name), fin_view(name, t, y), fin_sem.at[reduces[name][3], 7])

    tx = 2 * (1 - x) + c

    def fin_start(name):
        here = (lambda: t == z) if name == "o" else None
        if here is None:
            keep_own(name).start()
        else:
            pl.when(here())(lambda: keep_own(name).start())
        send(lambda: fin_copy(name, own_block(name), t, y, 0, y_dev), here)
        send(lambda: fin_copy(name, own_block(name), t, y, 1, x_dev), here)
        send(lambda: fin_copy(name, own_block(name), t, y, 2, core_dev), here)

    def fin_wait(name, tt, yy):
        fin_copy(name, fin_view(name, tt, yy), tt, yy, 0, core_dev).wait_recv()

    def fin_forward(name, turn):
        steps = [(t, 1 - y, x_dev), (tx, y, None), (tx, 1 - y, None)]
        if name in YWAY:
            steps = [(tx, y, y_dev), (t, 1 - y, None), (tx, 1 - y, None)]
        tt, yy, dev = steps[turn]
        here = (tt == z) if name == "o" else (z >= 0)
        v = fin_view(name, tt, yy)
        pl.when(here)(lambda: fin_wait(name, tt, yy))
        if dev is not None:
            send(lambda: fin_copy(name, v, tt, yy, 3, dev), lambda: here)
        send(lambda: fin_copy(name, v, tt, yy, 4 + turn, core_dev), lambda: here)

    def fin_finish(name):
        if name == "o":
            here = lax.rem(z, 2) != c
            for yy in range(2):
                pl.when(here)(lambda yy=yy: fin_wait(name, 0, yy))
            pl.when(t == z)(lambda: keep_own(name).wait())
        else:
            for xx in range(2):
                for yy in range(2):
                    fin_wait(name, 2 * xx + (1 - c), yy)
            keep_own(name).wait()

    def prepare(rq, rt, ro, rd, turned, rf, rp):
        loads = [
            pltpu.make_async_copy(wq_h, rq, raw_sem.at[0]),
            pltpu.make_async_copy(tok_h, rt, raw_sem.at[1]),
            pltpu.make_async_copy(wo_h, ro, raw_sem.at[2]),
            pltpu.make_async_copy(dy_h, rd, raw_sem.at[3]),
            pltpu.make_async_copy(wf_h, rf, raw_sem.at[4]),
            pltpu.make_async_copy(wp_h.at[pl.ds(pl.multiple_of(blk * t, 8), blk)], rp, raw_sem.at[5]),
        ]
        for load in loads:
            load.start()
        lnv[...] = jnp.zeros_like(lnv)
        for k, ref in enumerate((g1_i, b1_i, g2_i, b2_i)):
            lnv[k : k + 1, 0:blk] = ref[...].astype(F32).reshape(1, blk)
        lnr[z] = lnv[...]

        loads[0].wait()
        wq[pl.ds(base, bp), :] = jnp.zeros((bp, nq), BF)
        for k in range(NT):
            @pl.when(t == k)
            def _(k=k):
                for j in range(3):
                    wq[pl.ds(base, blk), blk * j : blk * (j + 1)] = rq[:, dim * j + blk * k : dim * j + blk * (k + 1)]
        pl.semaphore_wait(barrier, 3 + len(others))
        ag_start("q")
        for k in range(1, NZ):
            send(lambda k=k: remote(lnv, lnr.at[z], ln_sem.at[k - 1], ln_sem.at[2 + k], others[k - 1]))

        turned[...] = jnp.zeros_like(turned)

        def spread(dst, src):
            for j in range(NZ):
                turned[bp * j : bp * j + blk, :] = src[blk * j : blk * (j + 1), :]
            dst[...] = turned[...].T

        loads[1].wait()
        for s in range(WAVES):
            spread(xown.at[s], rt.at[s])
            sent = jnp.where(lane == blk, len_s[s].astype(F32), xown[s].astype(F32))
            tok[blk_of(s, c, x)] = sent.astype(BF)
            xg_start(tok, 0, s, track=False)
        loads[2].wait()

        @pl.when(t == z)
        def _():
            wo[...] = jnp.zeros_like(wo)
            for j in range(NZ):
                wo[0:blk, bp * j : bp * j + blk] = ro[:, blk * j : blk * (j + 1)]
        ag_start("o")
        loads[3].wait()
        for s in range(WAVES):
            spread(dys.at[blk_of(s, c, x)], rd.at[s])
            xg_start(dys, 1, s)

        def prepare_mlp():
            loads[4].wait()
            wf[pl.ds(base, bp), :] = jnp.zeros((bp, dp), BF)
            for k in range(NT):
                @pl.when(t == k)
                def _(k=k):
                    for j in range(NZ):
                        lo = (ff // NZ) * j + blk * k
                        wf[pl.ds(base, blk), bp * j : bp * j + blk] = rf[:, lo : lo + blk]
            loads[5].wait()
            wp[pl.ds(base, bp), :] = jnp.zeros((bp, dp), BF)
            for j in range(NZ):
                wp[pl.ds(base, blk), bp * j : bp * j + blk] = rp[:, blk * j : blk * (j + 1)]

        prepare_mlp()

    pl.run_scoped(
        prepare,
        pltpu.VMEM((blk, 3 * dim), BF),
        pltpu.VMEM((WAVES, dim, SEQ), BF),
        pltpu.VMEM((blk, dim), BF),
        pltpu.VMEM((WAVES, dim, SEQ), BF),
        pltpu.VMEM((dp, SEQ), BF),
        pltpu.VMEM((blk, ff), BF),
        pltpu.VMEM((blk, dim), BF),
    )

    def main(first, pm):
        for k in range(1, NZ):
            remote(lnv, lnr.at[lax.rem(z + NZ - k, NZ)], ln_sem.at[k - 1], ln_sem.at[2 + k], others[k - 1]).wait_recv()
        vec[...] = jnp.zeros_like(vec)
        for j in range(NZ):
            vec[:, bp * j : bp * j + blk] = lnr[j, :, 0:blk]
        lg[...] = jnp.zeros_like(lg)
        dqkv[...] = jnp.zeros_like(dqkv)

        def stats(rows):
            mean = jnp.sum(rows, axis=-1, keepdims=True) * inv_dim
            cen = (rows - mean) * livef
            inv = lax.rsqrt(jnp.sum(cen * cen, axis=-1, keepdims=True) * inv_dim + EPS)
            return cen * inv, inv

        def norm_back(e, n, inv):
            me = jnp.sum(e, axis=-1, keepdims=True) * inv_dim
            mn = jnp.sum(e * n, axis=-1, keepdims=True) * inv_dim
            return inv * (e - me - n * mn) * livef

        def ln_first(s):
            def body(i, carry):
                b = s * NT + i
                raw = tok[b].astype(F32)
                lens[b] = jnp.broadcast_to(raw[0:8, blk : blk + 1], (8, SEQ))
                n, inv = stats(raw * livef)
                first[b] = (n * vec[0:1, :] + vec[1:2, :]).astype(BF)
                return carry
            lax.fori_loop(0, NT, body, 0)

        lane_h = lax.broadcasted_iota(jnp.int32, (1, bp), 1)
        head_masks = [(lane_h >= head * h) & (lane_h < head * (h + 1)) for h in range(nh)]

        def stack_heads(v):
            zero = jnp.zeros_like(v)
            return jnp.concatenate([jnp.where(m, v, zero) for m in head_masks], axis=0)

        def side_by_side(v):
            return jnp.concatenate([v[SEQ * h : SEQ * (h + 1)] for h in range(nh)], axis=1)

        def project(s):
            def body(i, carry):
                b = s * NT + i * 2
                rows = first[pl.ds(b, 2)].reshape(2 * SEQ, dp)
                out = nn(rows, wq[...])
                for j, ref in enumerate((qs, ks, vs)):
                    ref[pl.ds(b, 2)] = out[:, blk * j : blk * j + bp].astype(BF).reshape(2, SEQ, bp)
                return carry
            lax.fori_loop(0, 2, body, 0)

        def attend(s):
            q_pos = lax.broadcasted_iota(jnp.int32, (SEQ, SEQ), 0)
            k_pos = lax.broadcasted_iota(jnp.int32, (SEQ, SEQ), 1)

            def body(i, carry):
                b = s * NT + i
                scores = nt(stack_heads(qs[b]), ks[b]) * scale
                ok = (k_pos <= q_pos) & (k_pos.astype(F32) < lens[b, 0:1, :])
                bias = jnp.concatenate([ok.astype(F32)] * nh, axis=0) > 0.5
                scores = jnp.where(bias, scores, MASKED)
                top = jnp.max(scores, axis=-1, keepdims=True)
                ex = jnp.exp(scores - top)
                prob = ex / jnp.sum(ex, axis=-1, keepdims=True)
                pm[b] = prob
                out = nn(side_by_side(prob.astype(BF)), stack_heads(vs[b]))
                att[b] = out.astype(BF)
                return carry
            lax.fori_loop(0, NT, body, 0)

        def matmul_part(src, weight, s, transposed, e):
            width = src.shape[2]
            dst = part_of(e)

            def body(i, carry):
                b = s * NT + i * 2
                rows = src[pl.ds(b, 2)].reshape(2 * SEQ, width)
                out = nt(rows, weight[...]) if transposed else nn(rows, weight[...])
                dst[pl.ds(b, 2)] = out.astype(BF).reshape(2, SEQ, dp)
                return carry
            lax.fori_loop(0, 2, body, 0)

        def mid(s):
            rows = xown[s].astype(F32) + ex_sum(0, s)
            mix[s] = rows
            n, inv = stats(rows)
            sec[blk_of(s, c, x)] = (n * vec[2:3, :] + vec[3:4, :]).astype(BF)
            xg_start(sec, 2, s)

        def expand(s):
            def body(i, carry):
                b = s * NT + i * 2
                rows = sec[pl.ds(b, 2)].reshape(2 * SEQ, dp)
                pre = nn(rows, wf[...])
                sq = pre * pre
                th = jnp.tanh(GELU_C * (pre + GELU_A * (pre * sq)))
                half = 0.5 * (1.0 + th)
                act[pl.ds(b, 2)] = (pre * half).astype(BF).reshape(2, SEQ, dp)
                slope = half + (0.5 * GELU_C) * pre * (1.0 - th * th) * (1.0 + (3.0 * GELU_A) * sq)
                gel[pl.ds(b, 2)] = slope.astype(BF).reshape(2, SEQ, dp)
                return carry
            lax.fori_loop(0, 2, body, 0)

        def grad_of(name, left, right):
            dst = reduces[name][0]
            step = 384
            rows = NB * SEQ
            leave = {} if name in ZFIRST else {0: (3,), 1: (0,), 2: (2, 1)}

            def depart(k):
                for d in leave.get(k, ()):
                    rs_y(name, d).start()

            def body(k, carry):
                cols = pl.ds(pl.multiple_of(lax.rem(k + 2, 3) * step, step), step)
                out = tn(left[:, :, cols].reshape(rows, step), right[...].reshape(rows, right.shape[2]))
                dst[cols, :] = out.astype(BF)
                for n in leave:
                    pl.when(k == n)(lambda n=n: depart(n))
                return carry

            lax.fori_loop(0, dp // step, body, 0)
            for ds in leave.values():
                ends.extend((None, lambda d=d: rs_y(name, d)) for d in ds)

        def back_act(s):
            def body(i, carry):
                b = s * NT + i * 2
                d_act = nt(dys[pl.ds(b, 2)].reshape(2 * SEQ, dp), wp[...])
                slope = gel[pl.ds(b, 2)].reshape(2 * SEQ, dp).astype(F32)
                gel[pl.ds(b, 2)] = (d_act * slope).astype(BF).reshape(2, SEQ, dp)
                return carry
            lax.fori_loop(0, 2, body, 0)

        def back_mid(s):
            d2 = ex_sum(2, s)
            n, inv = stats(mix[s])
            lg[2:3, :] = lg[2:3, :] + jnp.sum(d2 * n, axis=0, keepdims=True)
            lg[3:4, :] = lg[3:4, :] + jnp.sum(d2, axis=0, keepdims=True)
            rows = dys[blk_of(s, c, x)].astype(F32) + norm_back(d2 * vec[2:3, :], n, inv)
            dmix[s] = rows
            tok[blk_of(s, c, x)] = rows.astype(BF)
            xg_start(tok, 3, s)

        def back_attend(s):
            def proj(i, carry):
                b = s * NT + i * 2
                out = nt(tok[pl.ds(b, 2)].reshape(2 * SEQ, dp), wo[...])
                datt[pl.ds(b, 2)] = out.astype(BF).reshape(2, SEQ, bp)
                return carry
            lax.fori_loop(0, 2, proj, 0)

            def body(i, carry):
                b = s * NT + i
                d_out = stack_heads(datt[b])
                prob = pm[b]
                d_prob = nt(d_out, vs[b])
                total = jnp.sum(prob * d_prob, axis=-1, keepdims=True)
                d_scores = (prob * (d_prob - total)).astype(BF)
                dqkv[b, :, 0:bp] = (nn(side_by_side(d_scores), stack_heads(ks[b])) * scale).astype(BF)
                dqkv[b, :, blk : blk + bp] = (tn(d_scores, stack_heads(qs[b])) * scale).astype(BF)
                dqkv[b, :, 2 * blk : 2 * blk + bp] = tn(prob.astype(BF), d_out).astype(BF)
                return carry
            lax.fori_loop(0, NT, body, 0)

        def back_first(s):
            d1 = ex_sum(3, s)
            n, inv = stats(xown[s].astype(F32))
            lg[0:1, :] = lg[0:1, :] + jnp.sum(d1 * n, axis=0, keepdims=True)
            lg[1:2, :] = lg[1:2, :] + jnp.sum(d1, axis=0, keepdims=True)
            gtok_o[s] = (dmix[s] + norm_back(d1 * vec[0:1, :], n, inv)).astype(BF)

        def grad_out():
            rows_all = NB * SEQ
            go[...] = tn(att[...].reshape(rows_all, bp), tok[...].reshape(rows_all, dp)).astype(BF)

        def finish_rows(s):
            res_o[s] = (mix[s] + ex_sum(1, s)).astype(BF)

        hops = [
            remote(lg, lr.at[k], ln_sem.at[6 + 2 * k], ln_sem.at[7 + 2 * k], dev)
            for k, dev in enumerate((core_dev, x_dev, y_dev))
        ]

        def ln_add(k):
            hops[k].wait()
            lg[...] = lg[...] + lr[k]

        def ln_line(k):
            return remote(lg, lz.at[k - 1], ln_sem.at[11 + k], ln_sem.at[14 + k], others[k - 1])

        def ln_send():
            for k in range(1, NZ):
                send(lambda k=k: ln_line(k))

        def ln_total():
            for k in range(1, NZ):
                ln_line(k).wait_recv()
            total = lg[...] + lz[0] + lz[1] + lz[2]
            for j in range(NZ):
                @pl.when(z == j)
                def _(j=j):
                    gln_o[:, 0:blk] = total[:, bp * j : bp * j + blk]

        ag_forward("q", 1)
        ag_forward("o", 1)
        ag_forward("q", 2)
        ag_forward("o", 2)
        ag_start("f")
        ag_start("p")
        xg_forward(tok, 0, 0, track=False)
        ag_forward("q", 3)
        xg_finish(tok, 0, 0)
        xg_forward(tok, 0, 1, track=False)
        ln_first(0)
        xg_finish(tok, 0, 1)
        ln_first(1)
        xg_forward(dys, 1, 0)
        xg_finish(dys, 1, 0)
        ag_forward("o", 3)
        ag_finish("q")
        project(0)
        attend(0)
        project(1)
        ag_forward("f", 1)
        ag_finish("o")
        matmul_part(att, wo, 0, False, 0)
        ex_a(0, 0).start()
        ex_relay(0, 0)
        xg_sent(tok, 0, 0)
        attend(1)
        xg_forward(dys, 1, 1)
        matmul_part(att, wo, 1, False, 0)
        ex_a(0, 1).start()
        ag_forward("f", 2)
        ag_forward("p", 1)
        ex_relay(0, 1)
        mid(0)
        ag_forward("f", 3)
        mid(1)
        xg_finish(dys, 1, 1)
        ag_forward("p", 2)
        xg_sent(tok, 0, 1)
        ex_b(0, 1).wait_send()
        ex_a(0, 0).wait_send()
        xg_forward(sec, 2, 0)
        xg_forward(sec, 2, 1)
        ag_forward("p", 3)
        xg_finish(sec, 2, 0)
        ag_finish("f")
        expand(0)
        xg_finish(sec, 2, 1)
        expand(1)
        grad_of("p", act, dys)
        rs_stage("p", 2, 0)
        ex_a(0, 1).wait_send()
        rs_stage("p", 0, 0)
        ag_finish("p")
        back_act(1)
        matmul_part(gel, wf, 1, True, 2)
        ex_a(2, 1).start()
        back_act(0)
        ex_relay(2, 1)
        rs_stage("p", 3, 0)
        matmul_part(gel, wf, 0, True, 2)
        ex_a(2, 0).start()
        ex_b(0, 0).wait_send()
        ex_relay(2, 0)
        grad_of("f", sec, gel)
        matmul_part(act, wp, 0, False, 1)
        ex_a(1, 0).start()
        back_mid(0)
        rs_stage("p", 1, 0)
        matmul_part(act, wp, 1, False, 1)
        ex_a(1, 1).start()
        rs_stage("f", 3, 0)
        back_mid(1)
        rs_stage("p", 3, 1)
        xg_forward(tok, 3, 0)
        rs_stage("p", 0, 1)
        rs_stage("f", 0, 0)
        xg_finish(tok, 3, 0)
        back_attend(0)
        xg_forward(tok, 3, 1)
        xg_finish(tok, 3, 1)
        back_attend(1)
        grad_of("q", first, dqkv)
        ex_a(2, 1).wait_send()
        ex_b(2, 0).wait_send()
        rs_stage("f", 1, 0)
        rs_stage("p", 1, 1)
        rs_stage("f", 2, 0)
        rs_stage("p", 3, 2)
        rs_stage("p", 2, 1)
        ex_b(2, 1).wait_send()
        matmul_part(dqkv, wq, 1, True, 3)
        ex_a(3, 1).start()
        rs_stage("p", 0, 2)
        ex_relay(1, 0)
        ex_a(2, 0).wait_send()
        ex_relay(1, 1)
        rs_stage("f", 0, 1)
        matmul_part(dqkv, wq, 0, True, 3)
        ex_a(3, 0).start()
        ex_relay(3, 1)
        rs_stage("q", 3, 0)
        grad_out()
        rs_line("p")
        rs_stage("f", 3, 1)
        rs_start("o")
        ex_relay(3, 0)
        rs_stage("q", 0, 0)
        rs_stage("q", 2, 0)
        rs_stage("f", 1, 1)
        rs_stage("q", 1, 0)
        rs_stage("f", 2, 1)
        rs_final("p")
        fin_start("p")
        back_first(1)
        back_first(0)
        hops[0].start()
        rs_stage("q", 3, 1)
        rs_stage("f", 3, 2)
        rs_stage("o", 1, 0)
        rs_stage("f", 0, 2)
        rs_stage("q", 0, 1)
        finish_rows(1)
        ln_add(0)
        hops[1].start()
        rs_stage("o", 0, 0)
        rs_final("f")
        rs_stage("q", 2, 1)
        fin_start("f")
        rs_stage("q", 1, 1)
        rs_stage("q", 0, 2)
        rs_stage("o", 2, 0)
        ln_add(1)
        rs_stage("q", 3, 2)
        rs_stage("o", 0, 1)
        hops[2].start()
        rs_final("q")
        fin_start("q")
        rs_stage("o", 1, 1)
        fin_forward("p", 0)
        rs_final("o")
        fin_start("o")
        rs_stage("o", 2, 1)
        fin_forward("f", 0)
        finish_rows(0)
        rs_stage("o", 1, 2)
        ln_add(2)
        ln_send()
        rs_stage("o", 0, 2)
        fin_forward("o", 1)
        fin_forward("f", 1)
        rs_stage("o", 2, 2)
        fin_forward("q", 1)
        fin_forward("q", 0)
        fin_forward("p", 1)
        fin_forward("p", 2)
        fin_forward("o", 0)
        ln_total()
        fin_forward("f", 2)
        fin_forward("q", 2)
        fin_forward("o", 2)
        for name in ("p", "f", "o", "q"):
            fin_finish(name)
        for s in range(WAVES):
            for e in (1, 3):
                ex_a(e, s).wait_send()
                ex_b(e, s).wait_send()
        for cond, make in ends:
            if cond is None:
                make().wait_send()
            else:
                pl.when(cond())(lambda make=make: make().wait_send())

    pl.run_scoped(main, pltpu.VMEM((NB, SEQ, dp), BF), pltpu.VMEM((NB, nh * SEQ, SEQ), F32))


def layer_call(dim, ff, tokens, cot, w_qkv, w_out, w_fc, w_proj, lengths, norms):
    blk = dim // NZ
    bp = up16(blk)
    hb = bp // 2
    dp = NZ * bp
    nq = up128(3 * blk)
    vm, dma = pltpu.VMEM, pltpu.SemaphoreType.DMA
    big = (NB, SEQ, dp)
    half = lambda k: (1 if k in ZFIRST else NZ, hb, nq if k == "q" else dp)
    line = lambda k: (NZ + 1, bp if k in ZFIRST else hb, nq if k == "q" else dp)
    scratch = [
        vm(big, BF), vm(big, BF), vm((WAVES, SEQ, dp), BF),
        vm((dp, nq), BF), vm((bp, dp), BF), vm((dp, dp), BF), vm((dp, dp), BF),
        vm((NB, SEQ, bp), BF), vm((NB, SEQ, bp), BF), vm((NB, SEQ, bp), BF),
        vm((NB, SEQ, bp), BF),
        vm(big, BF), vm(big, BF),
        vm((2, WAVES, 2, SEQ, dp), BF), vm((2, WAVES, SEQ, dp), BF), vm((2, WAVES, SEQ, dp), BF),
        vm((WAVES, SEQ, dp), F32), vm((WAVES, SEQ, dp), F32),
        vm(big, BF), vm(big, BF), vm(big, BF),
        vm((NB, SEQ, bp), BF), vm((NB, SEQ, nq), BF),
        vm((dp, nq), BF), vm((bp, dp), BF), vm((dp, dp), BF), vm((dp, dp), BF),
        vm(half("q"), BF), vm((1, hb, dp), BF), vm(half("f"), BF), vm(half("p"), BF),
        vm(line("q"), BF), vm((2, hb, dp), BF), vm(line("f"), BF), vm(line("p"), BF),
        vm((8, up128(blk)), F32), vm((NZ, 8, up128(blk)), F32), vm((8, dp), F32), vm((NB, 8, SEQ), F32),
        vm((8, dp), F32), vm((3, 8, dp), F32), vm((3, 8, dp), F32),
        dma((6,)), dma((19, 5)), dma((4, 18)), dma((4, 16)), dma((8, 6)), dma((8, 4)), dma((18,)),
    ]
    hbm = pl.BlockSpec(memory_space=pl.ANY)
    inv = pl.BlockSpec(memory_space=pltpu.VMEM)
    shape = jax.ShapeDtypeStruct

    def body(*refs):
        layer_kernel(dim, ff, *refs)

    return pl.pallas_call(
        body,
        out_shape=(
            shape((WAVES, SEQ, dp), BF), shape((WAVES, SEQ, dp), BF),
            shape((8, hb, nq), BF), shape((2, hb, dp), BF), shape((8, hb, dp), BF), shape((8, hb, dp), BF),
            shape((8, up128(blk)), F32),
        ),
        in_specs=[hbm] * 6 + [pl.BlockSpec(memory_space=pltpu.SMEM)] + [inv] * 4,
        out_specs=(inv, inv, hbm, hbm, hbm, hbm, inv),
        scratch_shapes=scratch,
        compiler_params=pltpu.CompilerParams(
            collective_id=0, has_side_effects=True, vmem_limit_bytes=67043328
        ),
    )(tokens, cot, w_qkv, w_out, w_fc, w_proj, lengths, *norms)


def finish_kernel(dim, ff, res, gtok, gq, go, gf, gp, gln, res_o, gtok_o, gq_o, go_o, gf_o, gp_o, *norms_o):
    blk = dim // NZ
    bp = up16(blk)
    for j in range(NZ):
        there = slice(bp * j, bp * j + blk)
        go_o[:, blk * j : blk * (j + 1)] = go[:, there].astype(F32)
        for t in range(NT):
            gp_o[t, :, blk * j : blk * (j + 1)] = gp[t, :, there].astype(F32)
            lo = (ff // NZ) * j + blk * t
            gf_o[:, lo : lo + blk] = gf[t, :, there].astype(F32)
    for j in range(3):
        for t in range(NT):
            lo = dim * j + blk * t
            gq_o[:, lo : lo + blk] = gq[t, :, blk * j : blk * (j + 1)].astype(F32)

    @pl.when(pl.program_id(0) == 0)
    def _():
        for k, ref in enumerate(norms_o):
            ref[...] = gln[k : k + 1, 0:blk].reshape(blk)
        for src, dst in ((res, res_o), (gtok, gtok_o)):
            for s in range(WAVES):
                turned = src[s].T
                for j in range(NZ):
                    dst[s, blk * j : blk * (j + 1), :] = turned[bp * j : bp * j + blk, :]


def finish_call(dim, ff, res, gtok, gq, go, gf, gp, gln):
    blk = dim // NZ
    bp = up16(blk)
    dp = NZ * bp
    nq = gq.shape[2]
    step = 56
    shape, spec = jax.ShapeDtypeStruct, pl.BlockSpec
    whole = spec(memory_space=pltpu.VMEM)
    quarters = lambda n: spec((NT, step, n), lambda i: (0, i, 0))
    lines = lambda n: spec((step, n), lambda i: (i, 0))
    return pl.pallas_call(
        lambda *refs: finish_kernel(dim, ff, *refs),
        grid=(blk // step,),
        in_specs=[whole, whole, quarters(nq), lines(dp), quarters(dp), quarters(dp), whole],
        out_specs=[whole, whole, lines(3 * dim), lines(dim), lines(ff), quarters(dim)] + [whole] * 4,
        out_shape=[
            shape((WAVES, dim, SEQ), BF), shape((WAVES, dim, SEQ), BF),
            shape((blk, 3 * dim), F32), shape((blk, dim), F32), shape((blk, ff), F32), shape((NT, blk, dim), F32),
        ] + [shape((blk,), F32)] * 4,
        compiler_params=pltpu.CompilerParams(vmem_limit_bytes=67043328),
    )(
        res, gtok, gq.reshape(NT, bp, nq), go.reshape(bp, dp), gf.reshape(NT, bp, dp), gp.reshape(NT, bp, dp), gln
    )


def sum_boxes(value, wide):
    total = value
    for k in range(1, wide // 8):
        total = total + lax.ppermute(value, "wide", [(i, (i + 8 * k) % wide) for i in range(wide)])
    return total


def solution(mesh):
    wide, narrow = mesh.shape["wide"], mesh.shape["narrow"]
    assert narrow == NZ and wide % 8 == 0

    def shards(tokens, lengths, ln1_gain, ln1_bias, w_qkv, w_out, ln2_gain, ln2_bias, w_fc, w_proj, cotangent):
        cells, seq, dim = tokens.shape
        assert cells == WAVES and seq == SEQ
        ff = w_fc.shape[1]
        blk = dim // NZ
        bp = up16(blk)
        res, gtok, gq, go, gf, gp, gln = layer_call(
            dim, ff, tokens.transpose(0, 2, 1), cotangent.transpose(0, 2, 1),
            w_qkv, w_out, w_fc, w_proj, lengths, (ln1_gain, ln1_bias, ln2_gain, ln2_bias),
        )
        res, gtok, *grads = finish_call(dim, ff, res, gtok, gq, go, gf, gp, gln)
        gq, go, gf, gp, g1, b1, g2, b2 = [sum_boxes(g, wide) for g in grads]
        return (
            res.transpose(0, 2, 1), gtok.transpose(0, 2, 1), g1, b1, gq, go, g2, b2, gf, gp.reshape(ff // NZ, dim)
        )

    rows = P(("wide", "narrow"), None, None)
    vec, mat = P("narrow"), P("narrow", None)
    return jax.shard_map(
        shards,
        mesh=mesh,
        in_specs=(rows, P(("wide", "narrow")), vec, vec, mat, mat, vec, vec, mat, mat, rows),
        out_specs=(rows, rows, vec, vec, mat, mat, vec, vec, mat, mat),
        check_vma=False,
    )
```

```python
import math

import jax
import jax.numpy as jnp
from jax import lax
from jax.experimental import pallas as pl
from jax.experimental.pallas import tpu as pltpu
from jax.sharding import PartitionSpec as P

HEADS = 20
EPS = 1e-05
MASKED = -1e30
BF, F32 = jnp.bfloat16, jnp.float32
MESH = pl.DeviceIdType.MESH

NZ = 4
NT = 4
WAVES = 2
SEQ = 128
NB = NT * WAVES
GELU_C = math.sqrt(2.0 / math.pi)
GELU_A = 0.044715
YWAY = ("f", "q",)
ZFIRST = ("p",)


def up16(n):
    return -(-n // 16) * 16


def up128(n):
    return -(-n // 128) * 128


def nn(a, b):
    return lax.dot_general(a, b, (((1,), (0,)), ((), ())), preferred_element_type=F32)


def nt(a, b):
    return lax.dot_general(a, b, (((1,), (1,)), ((), ())), preferred_element_type=F32)


def tn(a, b):
    return lax.dot_general(a, b, (((0,), (0,)), ((), ())), preferred_element_type=F32)


def layer_kernel(
    dim, ff,
    tok_h, dy_h, wq_h, wo_h, wf_h, wp_h, len_s, g1_i, b1_i, g2_i, b2_i,
    res_o, gtok_o, gq_o, go_o, gf_o, gp_o, gln_o,
    tok, dys, xown, wq, wo, wf, wp, qs, ks, vs, att, part, part1, ra, sb, rb, mix, dmix,
    sec, act, gel, datt, dqkv, gq, go, gf, gp, yq, yo, yf, yp, zq, zo, zf, zp,
    lnv, lnr, vec, lens, lg, lr, lz,
    raw_sem, ag_sem, rs_sem, fin_sem, xs_sem, xa_sem, ln_sem,
):
    blk = dim // NZ
    bp = up16(blk)
    hb = bp // 2
    dp = NZ * bp
    nq = wq.shape[1]
    head = dim // HEADS
    nh = HEADS // NT
    inv_dim = 1.0 / dim
    scale = head ** (-0.5)

    w = lax.axis_index("wide")
    z = lax.axis_index("narrow")
    c = lax.rem(w, 2)
    x = lax.rem(w // 2, 2)
    y = lax.rem(w // 4, 2)
    t = 2 * x + c
    core_dev = (w + 1 - 2 * c, z)
    x_dev = (w + 2 - 4 * x, z)
    y_dev = (w + 4 - 8 * y, z)
    up_dev = (w, z + 1)
    down_dev = (w, z - 1)

    ends = []

    def remote(src, dst, ssem, rsem, dev):
        return pltpu.make_async_remote_copy(
            src_ref=src, dst_ref=dst, send_sem=ssem, recv_sem=rsem, device_id=dev, device_id_type=MESH
        )

    def send(make, cond=None, track=True):
        if cond is None:
            make().start()
        else:
            pl.when(cond())(lambda: make().start())
        if track:
            ends.append((cond, make))

    def both(a, b):
        return jnp.logical_and(a, b)

    lane = lax.broadcasted_iota(jnp.int32, (1, dp), 1)
    live = lax.rem(lane, bp) < blk
    livef = live.astype(F32)

    barrier = pltpu.get_barrier_semaphore()
    others = [(w, lax.rem(z + k, NZ)) for k in range(1, NZ)]
    for dev in [core_dev, x_dev, y_dev] + others:
        pl.semaphore_signal(barrier, inc=1, device_id=dev, device_id_type=MESH)

    def rows_of(s, yy, r0=0, nr=None):
        return pl.ds(pl.multiple_of(bp * s + hb * yy + r0, 16), hb if nr is None else nr)

    q_pieces = [(0, 80), (80, hb - 80)]
    o_pieces = [(0, 48), (48, 48), (96, hb - 96)]
    gathers = {
        "q": (wq, 0, q_pieces),
        "f": (wf, 8, q_pieces),
        "p": (wp, 16, q_pieces),
        "o": (wo, 24, o_pieces),
    }

    def ag_view(name, s, yy, piece):
        ref, base, pieces = gathers[name]
        r0, nr = pieces[piece]
        if name == "o":
            return ref.at[rows_of(0, yy, r0, nr)]
        return ref.at[rows_of(s, yy, r0, nr)]

    def ag_id(name, s, piece):
        ref, base, pieces = gathers[name]
        return base + piece if name == "o" else base + 4 * piece + s

    def ag_z(name, s, piece, up):
        v = ag_view(name, s, y, piece)
        i = ag_id(name, s, piece)
        return remote(v, v, ag_sem.at[i, 0 if up else 1], ag_sem.at[i, 2], up_dev if up else down_dev)

    def ag_y(name, s, yy, piece):
        v = ag_view(name, s, yy, piece)
        i = ag_id(name, s, piece)
        return remote(v, v, ag_sem.at[i, 3], ag_sem.at[i, 4], y_dev)

    def ag_start(name):
        for piece in range(len(gathers[name][2])):
            def own():
                return (t == z) if name == "o" else (z >= 0)

            send(lambda p=piece: ag_z(name, z, p, True), lambda: both(own(), z < NZ - 1))
            send(lambda p=piece: ag_z(name, z, p, False), lambda: both(own(), z > 0))

    def ag_forward(name, k):
        for piece in range(len(gathers[name][2])):
            for up in (True, False):
                s = z - k if up else z + k
                ok = (z >= k) if up else (z + k <= NZ - 1)
                if name == "o":
                    ok = t == s
                more = (z < NZ - 1) if up else (z > 0)
                pl.when(ok)(lambda s=s, p=piece, u=up: ag_z(name, s, p, u).wait_recv())
                send(lambda s=s, p=piece, u=up: ag_z(name, s, p, u), lambda ok=ok, more=more: both(ok, more))
                send(lambda s=s, p=piece: ag_y(name, s, y, p), lambda ok=ok: ok)

    def ag_finish(name):
        for piece in range(len(gathers[name][2])):
            if name == "o":
                pl.when(z != t)(lambda p=piece: ag_y(name, 0, 1 - y, p).wait_recv())
            else:
                for s in range(NZ):
                    pl.when(z != s)(lambda s=s, p=piece: ag_y(name, s, 1 - y, p).wait_recv())

    def blk_of(s, cc, xx):
        return s * NT + cc * 2 + xx

    def xg(ref, e, s, kind):
        i = 2 * e + s
        if kind == "x":
            v = ref.at[blk_of(s, c, x)]
            return remote(v, v, xs_sem.at[i, 0], xs_sem.at[i, 1], x_dev)
        if kind == "own":
            v = ref.at[blk_of(s, c, x)]
            return remote(v, v, xs_sem.at[i, 2], xs_sem.at[i, 3], core_dev)
        v = ref.at[blk_of(s, c, 1 - x)]
        return remote(v, v, xs_sem.at[i, 4], xs_sem.at[i, 5], core_dev)

    def xg_start(ref, e, s, track=True):
        send(lambda: xg(ref, e, s, "x"), track=track)
        send(lambda: xg(ref, e, s, "own"), track=track)

    def xg_forward(ref, e, s, track=True):
        xg(ref, e, s, "x").wait_recv()
        send(lambda: xg(ref, e, s, "fwd"), track=track)

    def xg_finish(ref, e, s):
        xg(ref, e, s, "own").wait_recv()
        xg(ref, e, s, "fwd").wait_recv()

    def xg_sent(ref, e, s):
        for kind in ("x", "own", "fwd"):
            xg(ref, e, s, kind).wait_send()

    def part_of(e):
        return part1 if e == 1 else part

    def ex_a(e, s):
        i = 2 * e + s
        return remote(
            part_of(e).at[pl.ds(s * NT + (1 - c) * 2, 2)], ra.at[int(e == 1), s],
            xa_sem.at[i, 0], xa_sem.at[i, 1], core_dev,
        )

    def ex_b(e, s):
        i = 2 * e + s
        return remote(sb.at[int(e == 1), s], rb.at[int(e == 1), s], xa_sem.at[i, 2], xa_sem.at[i, 3], x_dev)

    def ex_relay(e, s):
        ex_a(e, s).wait_recv()
        sb[int(e == 1), s] = (
            part_of(e)[blk_of(s, c, 1 - x)].astype(F32) + ra[int(e == 1), s, 1 - x].astype(F32)
        ).astype(BF)
        ex_b(e, s).start()

    def ex_sum(e, s):
        ex_b(e, s).wait_recv()
        return (
            part_of(e)[blk_of(s, c, x)].astype(F32)
            + ra[int(e == 1), s, x].astype(F32)
            + rb[int(e == 1), s].astype(F32)
        )

    base = pl.multiple_of(bp * z, 16)
    reduces = {"q": (gq, yq, zq, 0), "f": (gf, yf, zf, 1), "p": (gp, yp, zp, 2), "o": (go, yo, zo, 3)}

    def rs_y(name, d):
        g, yr, zr, i = reduces[name]
        if name == "o":
            r0, nr = o_pieces[d]
            return remote(
                g.at[rows_of(0, 1 - y, r0, nr)], yr.at[0, pl.ds(r0, nr)], rs_sem.at[i, d], rs_sem.at[i, 4 + d], y_dev
            )
        if name in ZFIRST:
            return remote(g.at[rows_of(z, 1 - y)], yr.at[0], rs_sem.at[i, 0], rs_sem.at[i, 4], y_dev)
        return remote(g.at[rows_of(d, 1 - y)], yr.at[d], rs_sem.at[i, d], rs_sem.at[i, 4 + d], y_dev)

    def rs_z(name, d, slot, up):
        g, yr, zr, i = reduces[name]
        if name == "o":
            rows = pl.ds(*o_pieces[d])
            return remote(
                yr.at[0, rows], zr.at[slot, rows], rs_sem.at[i, 8 + d], rs_sem.at[i, 12 + 2 * d + slot], up_dev if up else down_dev
            )
        if name in ZFIRST:
            return remote(
                g.at[pl.ds(bp * d, bp)], zr.at[slot], rs_sem.at[i, 8 + d], rs_sem.at[i, 12 + slot], up_dev if up else down_dev
            )
        return remote(yr.at[d], zr.at[slot], rs_sem.at[i, 8 + d], rs_sem.at[i, 12 + slot], up_dev if up else down_dev)

    def add_up(dst, srcs):
        step = 48

        def body(j, carry):
            r = pl.ds(pl.multiple_of(j * step, step), step)
            total = srcs[0][r, :].astype(F32)
            for src in srcs[1:]:
                total = total + src[r, :].astype(F32)
            dst[r, :] = total.astype(BF)
            return carry

        lax.fori_loop(0, dst.shape[0] // step, body, 0)

    def rs_start(name, dests=(3, 0, 2, 1)):
        for d in range(len(o_pieces)) if name == "o" else dests:
            send(lambda d=d: rs_y(name, d))

    def rs_stage(name, d, j):
        g, yr, zr, i = reduces[name]

        def side(pos, up):
            def run():
                if name in ZFIRST:
                    if j > 0:
                        own = g.at[pl.ds(bp * d, bp)]
                        rs_z(name, d, d, up).wait_recv()
                        add_up(own, [own, zr.at[d]])
                    return
                rs_y(name, d).wait_recv()
                if name == "o":
                    r0, nr = o_pieces[d]
                    own, mine, past = g.at[rows_of(0, y, r0, nr)], yr.at[0, pl.ds(r0, nr)], zr.at[0, pl.ds(r0, nr)]
                else:
                    own, mine, past = g.at[rows_of(d, y)], yr.at[d], zr.at[d]
                srcs = [own, mine]
                if j > 0:
                    rs_z(name, d, 0 if name == "o" else d, up).wait_recv()
                    srcs.append(past)
                add_up(mine, srcs)

            nxt = pos + 1 if up else pos - 1
            if name == "o":
                last = t == nxt
                cond = both(z == pos, (t > pos) if up else (t < pos))
                pl.when(cond)(run)
                if up:
                    send(lambda: rs_z(name, d, 1, True), lambda: both(cond, last))
                    send(lambda: rs_z(name, d, 0, True), lambda: both(cond, jnp.logical_not(last)))
                else:
                    send(lambda: rs_z(name, d, 0, False), lambda: cond)
            else:
                cond = z == pos
                pl.when(cond)(run)
                slot = NZ if (up and nxt == d) else d
                send(lambda: rs_z(name, d, slot, up), lambda: cond)

        if name == "o":
            if j < NZ - 1:
                side(j, True)
                side(NZ - 1 - j, False)
            return
        if j < d:
            side(j, True)
        if NZ - 1 - j > d:
            side(NZ - 1 - j, False)

    def rs_line(name):
        g, yr, zr, i = reduces[name]
        own = g.at[pl.ds(base, bp)]

        def run(slots):
            def go_():
                for slot in slots:
                    rs_z(name, slot if slot < NZ else 0, slot, True).wait_recv()
                add_up(own, [own] + [zr.at[slot] for slot in slots])
            return go_

        for k in range(NZ):
            pl.when(z == k)(run(([k] if k < NZ - 1 else []) + ([NZ] if k > 0 else [])))
        send(lambda: rs_y(name, 0))

    def rs_final(name):
        g, yr, zr, i = reduces[name]
        if name in ZFIRST:
            rs_y(name, 0).wait_recv()
            add_up(yr.at[0], [g.at[rows_of(z, y)], yr.at[0]])
            return
        out = name == "o"
        me = 0 if out else z
        here = (t == z) if out else (z >= 0)
        above = 0 if out else z
        below = 1 if out else NZ

        def run(has_above, has_below):
            def go_():
                parts = range(len(o_pieces)) if out else [me]
                for d in parts:
                    rs_y(name, d).wait_recv()
                srcs = [g.at[rows_of(me, y)], yr.at[me]]
                if has_above:
                    for d in parts:
                        rs_z(name, d, above, True).wait_recv()
                    srcs.append(zr.at[above])
                if has_below:
                    for d in parts:
                        rs_z(name, d, below, True).wait_recv()
                    srcs.append(zr.at[below])
                add_up(yr.at[me], srcs)
            return go_

        pl.when(both(here, z == 0))(run(True, False))
        pl.when(both(here, z == NZ - 1))(run(False, True))
        pl.when(both(here, both(z > 0, z < NZ - 1)))(run(True, True))

    outs = {"q": gq_o, "f": gf_o, "p": gp_o, "o": go_o}

    def fin_view(name, tt, yy):
        return outs[name].at[yy] if name == "o" else outs[name].at[tt * 2 + yy]

    def fin_copy(name, src, tt, yy, k, dev):
        i = reduces[name][3]
        slot = yy if name == "o" else tt * 2 + yy
        return remote(src, fin_view(name, tt, yy), fin_sem.at[i, k], fin_sem.at[i, 8 + slot], dev)

    def own_block(name):
        yr = reduces[name][1]
        return yr.at[0] if name == "o" or name in ZFIRST else yr.at[z]

    def keep_own(name):
        return pltpu.make_async_copy(own_block(name), fin_view(name, t, y), fin_sem.at[reduces[name][3], 7])

    tx = 2 * (1 - x) + c

    def fin_start(name):
        here = (lambda: t == z) if name == "o" else None
        if here is None:
            keep_own(name).start()
        else:
            pl.when(here())(lambda: keep_own(name).start())
        send(lambda: fin_copy(name, own_block(name), t, y, 0, y_dev), here)
        send(lambda: fin_copy(name, own_block(name), t, y, 1, x_dev), here)
        send(lambda: fin_copy(name, own_block(name), t, y, 2, core_dev), here)

    def fin_wait(name, tt, yy):
        fin_copy(name, fin_view(name, tt, yy), tt, yy, 0, core_dev).wait_recv()

    def fin_forward(name, turn):
        steps = [(t, 1 - y, x_dev), (tx, y, None), (tx, 1 - y, None)]
        if name in YWAY:
            steps = [(tx, y, y_dev), (t, 1 - y, None), (tx, 1 - y, None)]
        tt, yy, dev = steps[turn]
        here = (tt == z) if name == "o" else (z >= 0)
        v = fin_view(name, tt, yy)
        pl.when(here)(lambda: fin_wait(name, tt, yy))
        if dev is not None:
            send(lambda: fin_copy(name, v, tt, yy, 3, dev), lambda: here)
        send(lambda: fin_copy(name, v, tt, yy, 4 + turn, core_dev), lambda: here)

    def fin_finish(name):
        if name == "o":
            here = lax.rem(z, 2) != c
            for yy in range(2):
                pl.when(here)(lambda yy=yy: fin_wait(name, 0, yy))
            pl.when(t == z)(lambda: keep_own(name).wait())
        else:
            for xx in range(2):
                for yy in range(2):
                    fin_wait(name, 2 * xx + (1 - c), yy)
            keep_own(name).wait()

    def prepare(rq, rt, ro, rd, turned, rf, rp):
        loads = [
            pltpu.make_async_copy(wq_h, rq, raw_sem.at[0]),
            pltpu.make_async_copy(tok_h, rt, raw_sem.at[1]),
            pltpu.make_async_copy(wo_h, ro, raw_sem.at[2]),
            pltpu.make_async_copy(dy_h, rd, raw_sem.at[3]),
            pltpu.make_async_copy(wf_h, rf, raw_sem.at[4]),
            pltpu.make_async_copy(wp_h.at[pl.ds(pl.multiple_of(blk * t, 8), blk)], rp, raw_sem.at[5]),
        ]
        for load in loads:
            load.start()
        lnv[...] = jnp.zeros_like(lnv)
        for k, ref in enumerate((g1_i, b1_i, g2_i, b2_i)):
            lnv[k : k + 1, 0:blk] = ref[...].astype(F32).reshape(1, blk)
        lnr[z] = lnv[...]

        loads[0].wait()
        wq[pl.ds(base, bp), :] = jnp.zeros((bp, nq), BF)
        for k in range(NT):
            @pl.when(t == k)
            def _(k=k):
                for j in range(3):
                    wq[pl.ds(base, blk), blk * j : blk * (j + 1)] = rq[:, dim * j + blk * k : dim * j + blk * (k + 1)]
        pl.semaphore_wait(barrier, 3 + len(others))
        for k in range(1, NZ):
            send(lambda k=k: remote(lnv, lnr.at[z], ln_sem.at[k - 1], ln_sem.at[2 + k], others[k - 1]))
        ag_start("q")

        turned[...] = jnp.zeros_like(turned)

        def spread(dst, src):
            for j in range(NZ):
                turned[bp * j : bp * j + blk, :] = src[blk * j : blk * (j + 1), :]
            dst[...] = turned[...].T

        loads[1].wait()
        for s in range(WAVES):
            spread(xown.at[s], rt.at[s])
            sent = jnp.where(lane == blk, len_s[s].astype(F32), xown[s].astype(F32))
            tok[blk_of(s, c, x)] = sent.astype(BF)
            xg_start(tok, 0, s, track=False)
        loads[2].wait()

        @pl.when(t == z)
        def _():
            wo[...] = jnp.zeros_like(wo)
            for j in range(NZ):
                wo[0:blk, bp * j : bp * j + blk] = ro[:, blk * j : blk * (j + 1)]
        ag_start("o")
        loads[3].wait()
        for s in range(WAVES):
            spread(dys.at[blk_of(s, c, x)], rd.at[s])
            xg_start(dys, 1, s)

        def prepare_mlp():
            loads[4].wait()
            wf[pl.ds(base, bp), :] = jnp.zeros((bp, dp), BF)
            for k in range(NT):
                @pl.when(t == k)
                def _(k=k):
                    for j in range(NZ):
                        lo = (ff // NZ) * j + blk * k
                        wf[pl.ds(base, blk), bp * j : bp * j + blk] = rf[:, lo : lo + blk]
            loads[5].wait()
            wp[pl.ds(base, bp), :] = jnp.zeros((bp, dp), BF)
            for j in range(NZ):
                wp[pl.ds(base, blk), bp * j : bp * j + blk] = rp[:, blk * j : blk * (j + 1)]

        prepare_mlp()

    pl.run_scoped(
        prepare,
        pltpu.VMEM((blk, 3 * dim), BF),
        pltpu.VMEM((WAVES, dim, SEQ), BF),
        pltpu.VMEM((blk, dim), BF),
        pltpu.VMEM((WAVES, dim, SEQ), BF),
        pltpu.VMEM((dp, SEQ), BF),
        pltpu.VMEM((blk, ff), BF),
        pltpu.VMEM((blk, dim), BF),
    )

    def main(first, pm):
        def vectors():
            for k in range(1, NZ):
                remote(lnv, lnr.at[lax.rem(z + NZ - k, NZ)], ln_sem.at[k - 1], ln_sem.at[2 + k], others[k - 1]).wait_recv()
            vec[...] = jnp.zeros_like(vec)
            for j in range(NZ):
                vec[:, bp * j : bp * j + blk] = lnr[j, :, 0:blk]

        lg[...] = jnp.zeros_like(lg)
        dqkv[...] = jnp.zeros_like(dqkv)

        def stats(rows):
            mean = jnp.sum(rows, axis=-1, keepdims=True) * inv_dim
            cen = (rows - mean) * livef
            inv = lax.rsqrt(jnp.sum(cen * cen, axis=-1, keepdims=True) * inv_dim + EPS)
            return cen * inv, inv

        def norm_back(e, n, inv):
            me = jnp.sum(e, axis=-1, keepdims=True) * inv_dim
            mn = jnp.sum(e * n, axis=-1, keepdims=True) * inv_dim
            return inv * (e - me - n * mn) * livef

        def ln_first(s):
            def body(i, carry):
                b = s * NT + i
                raw = tok[b].astype(F32)
                lens[b] = jnp.broadcast_to(raw[0:8, blk : blk + 1], (8, SEQ))
                n, inv = stats(raw * livef)
                first[b] = (n * vec[0:1, :] + vec[1:2, :]).astype(BF)
                return carry
            lax.fori_loop(0, NT, body, 0)

        lane_h = lax.broadcasted_iota(jnp.int32, (1, bp), 1)
        head_masks = [(lane_h >= head * h) & (lane_h < head * (h + 1)) for h in range(nh)]

        def stack_heads(v):
            zero = jnp.zeros_like(v)
            return jnp.concatenate([jnp.where(m, v, zero) for m in head_masks], axis=0)

        def side_by_side(v):
            return jnp.concatenate([v[SEQ * h : SEQ * (h + 1)] for h in range(nh)], axis=1)

        def project(s):
            def body(i, carry):
                b = s * NT + i * 2
                rows = first[pl.ds(b, 2)].reshape(2 * SEQ, dp)
                out = nn(rows, wq[...])
                for j, ref in enumerate((qs, ks, vs)):
                    ref[pl.ds(b, 2)] = out[:, blk * j : blk * j + bp].astype(BF).reshape(2, SEQ, bp)
                return carry
            lax.fori_loop(0, 2, body, 0)

        def attend(s):
            q_pos = lax.broadcasted_iota(jnp.int32, (SEQ, SEQ), 0)
            k_pos = lax.broadcasted_iota(jnp.int32, (SEQ, SEQ), 1)

            def body(i, carry):
                b = s * NT + i
                scores = nt(stack_heads(qs[b]), ks[b]) * scale
                ok = (k_pos <= q_pos) & (k_pos.astype(F32) < lens[b, 0:1, :])
                bias = jnp.concatenate([ok.astype(F32)] * nh, axis=0) > 0.5
                scores = jnp.where(bias, scores, MASKED)
                top = jnp.max(scores, axis=-1, keepdims=True)
                ex = jnp.exp(scores - top)
                prob = ex / jnp.sum(ex, axis=-1, keepdims=True)
                pm[b] = prob
                out = nn(side_by_side(prob.astype(BF)), stack_heads(vs[b]))
                att[b] = out.astype(BF)
                return carry
            lax.fori_loop(0, NT, body, 0)

        def matmul_part(src, weight, s, transposed, e):
            width = src.shape[2]
            dst = part_of(e)

            def body(i, carry):
                b = s * NT + i * 2
                rows = src[pl.ds(b, 2)].reshape(2 * SEQ, width)
                out = nt(rows, weight[...]) if transposed else nn(rows, weight[...])
                dst[pl.ds(b, 2)] = out.astype(BF).reshape(2, SEQ, dp)
                return carry
            lax.fori_loop(0, 2, body, 0)

        def mid(s):
            rows = xown[s].astype(F32) + ex_sum(0, s)
            mix[s] = rows
            n, inv = stats(rows)
            sec[blk_of(s, c, x)] = (n * vec[2:3, :] + vec[3:4, :]).astype(BF)
            xg_start(sec, 2, s)

        def expand(s):
            def body(i, carry):
                b = s * NT + i * 2
                rows = sec[pl.ds(b, 2)].reshape(2 * SEQ, dp)
                pre = nn(rows, wf[...])
                sq = pre * pre
                th = jnp.tanh(GELU_C * (pre + GELU_A * (pre * sq)))
                half = 0.5 * (1.0 + th)
                act[pl.ds(b, 2)] = (pre * half).astype(BF).reshape(2, SEQ, dp)
                slope = half + (0.5 * GELU_C) * pre * (1.0 - th * th) * (1.0 + (3.0 * GELU_A) * sq)
                gel[pl.ds(b, 2)] = slope.astype(BF).reshape(2, SEQ, dp)
                return carry
            lax.fori_loop(0, 2, body, 0)

        def grad_of(name, left, right):
            dst = reduces[name][0]
            step = 384
            rows = NB * SEQ
            leave = {} if name in ZFIRST else {0: (3,), 1: (0,), 2: (2, 1)}

            def depart(k):
                for d in leave.get(k, ()):
                    rs_y(name, d).start()

            def body(k, carry):
                cols = pl.ds(pl.multiple_of(lax.rem(k + 2, 3) * step, step), step)
                out = tn(left[:, :, cols].reshape(rows, step), right[...].reshape(rows, right.shape[2]))
                dst[cols, :] = out.astype(BF)
                for n in leave:
                    pl.when(k == n)(lambda n=n: depart(n))
                return carry

            lax.fori_loop(0, dp // step, body, 0)
            for ds in leave.values():
                ends.extend((None, lambda d=d: rs_y(name, d)) for d in ds)

        def back_act(s):
            def body(i, carry):
                b = s * NT + i * 2
                d_act = nt(dys[pl.ds(b, 2)].reshape(2 * SEQ, dp), wp[...])
                slope = gel[pl.ds(b, 2)].reshape(2 * SEQ, dp).astype(F32)
                gel[pl.ds(b, 2)] = (d_act * slope).astype(BF).reshape(2, SEQ, dp)
                return carry
            lax.fori_loop(0, 2, body, 0)

        def back_mid(s):
            d2 = ex_sum(2, s)
            n, inv = stats(mix[s])
            lg[2:3, :] = lg[2:3, :] + jnp.sum(d2 * n, axis=0, keepdims=True)
            lg[3:4, :] = lg[3:4, :] + jnp.sum(d2, axis=0, keepdims=True)
            rows = dys[blk_of(s, c, x)].astype(F32) + norm_back(d2 * vec[2:3, :], n, inv)
            dmix[s] = rows
            tok[blk_of(s, c, x)] = rows.astype(BF)
            xg_start(tok, 3, s)

        def back_attend(s):
            def proj(i, carry):
                b = s * NT + i * 2
                out = nt(tok[pl.ds(b, 2)].reshape(2 * SEQ, dp), wo[...])
                datt[pl.ds(b, 2)] = out.astype(BF).reshape(2, SEQ, bp)
                return carry
            lax.fori_loop(0, 2, proj, 0)

            def body(i, carry):
                b = s * NT + i
                d_out = stack_heads(datt[b])
                prob = pm[b]
                d_prob = nt(d_out, vs[b])
                total = jnp.sum(prob * d_prob, axis=-1, keepdims=True)
                d_scores = (prob * (d_prob - total)).astype(BF)
                dqkv[b, :, 0:bp] = (nn(side_by_side(d_scores), stack_heads(ks[b])) * scale).astype(BF)
                dqkv[b, :, blk : blk + bp] = (tn(d_scores, stack_heads(qs[b])) * scale).astype(BF)
                dqkv[b, :, 2 * blk : 2 * blk + bp] = tn(prob.astype(BF), d_out).astype(BF)
                return carry
            lax.fori_loop(0, NT, body, 0)

        def back_first(s):
            d1 = ex_sum(3, s)
            n, inv = stats(xown[s].astype(F32))
            lg[0:1, :] = lg[0:1, :] + jnp.sum(d1 * n, axis=0, keepdims=True)
            lg[1:2, :] = lg[1:2, :] + jnp.sum(d1, axis=0, keepdims=True)
            gtok_o[s] = (dmix[s] + norm_back(d1 * vec[0:1, :], n, inv)).astype(BF)

        def grad_out():
            rows_all = NB * SEQ
            go[...] = tn(att[...].reshape(rows_all, bp), tok[...].reshape(rows_all, dp)).astype(BF)

        def finish_rows(s):
            res_o[s] = (mix[s] + ex_sum(1, s)).astype(BF)

        hops = [
            remote(lg, lr.at[k], ln_sem.at[6 + 2 * k], ln_sem.at[7 + 2 * k], dev)
            for k, dev in enumerate((core_dev, x_dev, y_dev))
        ]

        def ln_add(k):
            hops[k].wait()
            lg[...] = lg[...] + lr[k]

        def ln_line(k):
            return remote(lg, lz.at[k - 1], ln_sem.at[11 + k], ln_sem.at[14 + k], others[k - 1])

        def ln_send():
            for k in range(1, NZ):
                send(lambda k=k: ln_line(k))

        def ln_total():
            for k in range(1, NZ):
                ln_line(k).wait_recv()
            total = lg[...] + lz[0] + lz[1] + lz[2]
            for j in range(NZ):
                @pl.when(z == j)
                def _(j=j):
                    gln_o[:, 0:blk] = total[:, bp * j : bp * j + blk]

        ag_forward("q", 1)
        ag_forward("o", 1)
        ag_forward("q", 2)
        ag_forward("o", 2)
        ag_start("f")
        ag_start("p")
        xg_forward(tok, 0, 0, track=False)
        ag_forward("q", 3)
        xg_finish(tok, 0, 0)
        xg_forward(tok, 0, 1, track=False)
        vectors()
        ln_first(0)
        xg_finish(tok, 0, 1)
        ln_first(1)
        xg_forward(dys, 1, 0)
        xg_finish(dys, 1, 0)
        ag_forward("o", 3)
        ag_finish("q")
        project(0)
        project(1)
        attend(0)
        ag_forward("f", 1)
        ag_finish("o")
        matmul_part(att, wo, 0, False, 0)
        ex_a(0, 0).start()
        ex_relay(0, 0)
        xg_sent(tok, 0, 0)
        attend(1)
        xg_forward(dys, 1, 1)
        matmul_part(att, wo, 1, False, 0)
        ex_a(0, 1).start()
        ag_forward("f", 2)
        ag_forward("p", 1)
        ex_relay(0, 1)
        mid(0)
        ag_forward("f", 3)
        mid(1)
        xg_finish(dys, 1, 1)
        ag_forward("p", 2)
        xg_sent(tok, 0, 1)
        ex_b(0, 1).wait_send()
        ex_a(0, 0).wait_send()
        xg_forward(sec, 2, 0)
        xg_forward(sec, 2, 1)
        ag_forward("p", 3)
        xg_finish(sec, 2, 0)
        ag_finish("f")
        expand(0)
        xg_finish(sec, 2, 1)
        expand(1)
        grad_of("p", act, dys)
        rs_stage("p", 2, 0)
        ex_a(0, 1).wait_send()
        rs_stage("p", 0, 0)
        ag_finish("p")
        back_act(1)
        matmul_part(gel, wf, 1, True, 2)
        ex_a(2, 1).start()
        back_act(0)
        ex_relay(2, 1)
        rs_stage("p", 3, 0)
        matmul_part(gel, wf, 0, True, 2)
        ex_a(2, 0).start()
        ex_b(0, 0).wait_send()
        ex_relay(2, 0)
        grad_of("f", sec, gel)
        back_mid(0)
        rs_stage("p", 1, 0)
        matmul_part(act, wp, 0, False, 1)
        ex_a(1, 0).start()
        matmul_part(act, wp, 1, False, 1)
        ex_a(1, 1).start()
        rs_stage("f", 3, 0)
        back_mid(1)
        rs_stage("p", 3, 1)
        xg_forward(tok, 3, 0)
        rs_stage("p", 0, 1)
        rs_stage("f", 0, 0)
        xg_finish(tok, 3, 0)
        back_attend(0)
        xg_forward(tok, 3, 1)
        xg_finish(tok, 3, 1)
        back_attend(1)
        grad_of("q", first, dqkv)
        ex_a(2, 1).wait_send()
        ex_b(2, 0).wait_send()
        rs_stage("f", 1, 0)
        rs_stage("p", 1, 1)
        rs_stage("f", 2, 0)
        rs_stage("p", 3, 2)
        rs_stage("p", 2, 1)
        ex_b(2, 1).wait_send()
        matmul_part(dqkv, wq, 1, True, 3)
        ex_a(3, 1).start()
        rs_stage("p", 0, 2)
        ex_relay(1, 0)
        ex_a(2, 0).wait_send()
        ex_relay(1, 1)
        rs_stage("f", 0, 1)
        matmul_part(dqkv, wq, 0, True, 3)
        ex_a(3, 0).start()
        ex_relay(3, 1)
        rs_stage("q", 3, 0)
        grad_out()
        rs_line("p")
        rs_stage("f", 3, 1)
        rs_start("o")
        ex_relay(3, 0)
        rs_stage("q", 0, 0)
        rs_stage("q", 2, 0)
        rs_stage("f", 1, 1)
        rs_stage("q", 1, 0)
        rs_stage("f", 2, 1)
        rs_final("p")
        fin_start("p")
        back_first(1)
        back_first(0)
        hops[0].start()
        rs_stage("q", 3, 1)
        rs_stage("f", 3, 2)
        rs_stage("o", 1, 0)
        rs_stage("f", 0, 2)
        rs_stage("q", 0, 1)
        finish_rows(1)
        ln_add(0)
        hops[1].start()
        rs_stage("o", 0, 0)
        rs_final("f")
        rs_stage("q", 2, 1)
        fin_start("f")
        rs_stage("q", 1, 1)
        rs_stage("q", 0, 2)
        rs_stage("o", 2, 0)
        ln_add(1)
        rs_stage("q", 3, 2)
        rs_stage("o", 0, 1)
        hops[2].start()
        rs_final("q")
        fin_start("q")
        rs_stage("o", 1, 1)
        rs_final("o")
        fin_start("o")
        fin_forward("p", 0)
        rs_stage("o", 2, 1)
        fin_forward("f", 0)
        finish_rows(0)
        ln_add(2)
        ln_send()
        rs_stage("o", 1, 2)
        rs_stage("o", 0, 2)
        fin_forward("o", 1)
        fin_forward("f", 1)
        rs_stage("o", 2, 2)
        fin_forward("q", 1)
        fin_forward("q", 0)
        fin_forward("p", 1)
        fin_forward("p", 2)
        fin_forward("o", 0)
        ln_total()
        fin_forward("f", 2)
        fin_forward("q", 2)
        fin_forward("o", 2)
        for name in ("p", "f", "o", "q"):
            fin_finish(name)
        for s in range(WAVES):
            for e in (1, 3):
                ex_a(e, s).wait_send()
                ex_b(e, s).wait_send()
        for cond, make in ends:
            if cond is None:
                make().wait_send()
            else:
                pl.when(cond())(lambda make=make: make().wait_send())

    pl.run_scoped(main, pltpu.VMEM((NB, SEQ, dp), BF), pltpu.VMEM((NB, nh * SEQ, SEQ), F32))


def layer_call(dim, ff, tokens, cot, w_qkv, w_out, w_fc, w_proj, lengths, norms):
    blk = dim // NZ
    bp = up16(blk)
    hb = bp // 2
    dp = NZ * bp
    nq = up128(3 * blk)
    vm, dma = pltpu.VMEM, pltpu.SemaphoreType.DMA
    big = (NB, SEQ, dp)
    half = lambda k: (1 if k in ZFIRST else NZ, hb, nq if k == "q" else dp)
    line = lambda k: (NZ + 1, bp if k in ZFIRST else hb, nq if k == "q" else dp)
    scratch = [
        vm(big, BF), vm(big, BF), vm((WAVES, SEQ, dp), BF),
        vm((dp, nq), BF), vm((bp, dp), BF), vm((dp, dp), BF), vm((dp, dp), BF),
        vm((NB, SEQ, bp), BF), vm((NB, SEQ, bp), BF), vm((NB, SEQ, bp), BF),
        vm((NB, SEQ, bp), BF),
        vm(big, BF), vm(big, BF),
        vm((2, WAVES, 2, SEQ, dp), BF), vm((2, WAVES, SEQ, dp), BF), vm((2, WAVES, SEQ, dp), BF),
        vm((WAVES, SEQ, dp), F32), vm((WAVES, SEQ, dp), F32),
        vm(big, BF), vm(big, BF), vm(big, BF),
        vm((NB, SEQ, bp), BF), vm((NB, SEQ, nq), BF),
        vm((dp, nq), BF), vm((bp, dp), BF), vm((dp, dp), BF), vm((dp, dp), BF),
        vm(half("q"), BF), vm((1, hb, dp), BF), vm(half("f"), BF), vm(half("p"), BF),
        vm(line("q"), BF), vm((2, hb, dp), BF), vm(line("f"), BF), vm(line("p"), BF),
        vm((8, up128(blk)), F32), vm((NZ, 8, up128(blk)), F32), vm((8, dp), F32), vm((NB, 8, SEQ), F32),
        vm((8, dp), F32), vm((3, 8, dp), F32), vm((3, 8, dp), F32),
        dma((6,)), dma((27, 5)), dma((4, 18)), dma((4, 16)), dma((8, 6)), dma((8, 4)), dma((18,)),
    ]
    hbm = pl.BlockSpec(memory_space=pl.ANY)
    inv = pl.BlockSpec(memory_space=pltpu.VMEM)
    shape = jax.ShapeDtypeStruct

    def body(*refs):
        layer_kernel(dim, ff, *refs)

    return pl.pallas_call(
        body,
        out_shape=(
            shape((WAVES, SEQ, dp), BF), shape((WAVES, SEQ, dp), BF),
            shape((8, hb, nq), BF), shape((2, hb, dp), BF), shape((8, hb, dp), BF), shape((8, hb, dp), BF),
            shape((8, up128(blk)), F32),
        ),
        in_specs=[hbm] * 6 + [pl.BlockSpec(memory_space=pltpu.SMEM)] + [inv] * 4,
        out_specs=(inv, inv, hbm, hbm, hbm, hbm, inv),
        scratch_shapes=scratch,
        compiler_params=pltpu.CompilerParams(
            collective_id=0, has_side_effects=True, vmem_limit_bytes=67043328
        ),
    )(tokens, cot, w_qkv, w_out, w_fc, w_proj, lengths, *norms)


def finish_kernel(dim, ff, res, gtok, gq, go, gf, gp, gln, res_o, gtok_o, gq_o, go_o, gf_o, gp_o, *norms_o):
    blk = dim // NZ
    bp = up16(blk)
    for j in range(NZ):
        there = slice(bp * j, bp * j + blk)
        go_o[:, blk * j : blk * (j + 1)] = go[:, there].astype(F32)
        for t in range(NT):
            gp_o[t, :, blk * j : blk * (j + 1)] = gp[t, :, there].astype(F32)
            lo = (ff // NZ) * j + blk * t
            gf_o[:, lo : lo + blk] = gf[t, :, there].astype(F32)
    for j in range(3):
        for t in range(NT):
            lo = dim * j + blk * t
            gq_o[:, lo : lo + blk] = gq[t, :, blk * j : blk * (j + 1)].astype(F32)

    @pl.when(pl.program_id(0) == 0)
    def _():
        for k, ref in enumerate(norms_o):
            ref[...] = gln[k : k + 1, 0:blk].reshape(blk)
        for src, dst in ((res, res_o), (gtok, gtok_o)):
            for s in range(WAVES):
                turned = src[s].T
                for j in range(NZ):
                    dst[s, blk * j : blk * (j + 1), :] = turned[bp * j : bp * j + blk, :]


def finish_call(dim, ff, res, gtok, gq, go, gf, gp, gln):
    blk = dim // NZ
    bp = up16(blk)
    dp = NZ * bp
    nq = gq.shape[2]
    step = 56
    shape, spec = jax.ShapeDtypeStruct, pl.BlockSpec
    whole = spec(memory_space=pltpu.VMEM)
    quarters = lambda n: spec((NT, step, n), lambda i: (0, i, 0))
    lines = lambda n: spec((step, n), lambda i: (i, 0))
    return pl.pallas_call(
        lambda *refs: finish_kernel(dim, ff, *refs),
        grid=(blk // step,),
        in_specs=[whole, whole, quarters(nq), lines(dp), quarters(dp), quarters(dp), whole],
        out_specs=[whole, whole, lines(3 * dim), lines(dim), lines(ff), quarters(dim)] + [whole] * 4,
        out_shape=[
            shape((WAVES, dim, SEQ), BF), shape((WAVES, dim, SEQ), BF),
            shape((blk, 3 * dim), F32), shape((blk, dim), F32), shape((blk, ff), F32), shape((NT, blk, dim), F32),
        ] + [shape((blk,), F32)] * 4,
        compiler_params=pltpu.CompilerParams(vmem_limit_bytes=67043328),
    )(
        res, gtok, gq.reshape(NT, bp, nq), go.reshape(bp, dp), gf.reshape(NT, bp, dp), gp.reshape(NT, bp, dp), gln
    )


def sum_boxes(value, wide):
    total = value
    for k in range(1, wide // 8):
        total = total + lax.ppermute(value, "wide", [(i, (i + 8 * k) % wide) for i in range(wide)])
    return total


def solution(mesh):
    wide, narrow = mesh.shape["wide"], mesh.shape["narrow"]
    assert narrow == NZ and wide % 8 == 0

    def shards(tokens, lengths, ln1_gain, ln1_bias, w_qkv, w_out, ln2_gain, ln2_bias, w_fc, w_proj, cotangent):
        cells, seq, dim = tokens.shape
        assert cells == WAVES and seq == SEQ
        ff = w_fc.shape[1]
        blk = dim // NZ
        bp = up16(blk)
        res, gtok, gq, go, gf, gp, gln = layer_call(
            dim, ff, tokens.transpose(0, 2, 1), cotangent.transpose(0, 2, 1),
            w_qkv, w_out, w_fc, w_proj, lengths, (ln1_gain, ln1_bias, ln2_gain, ln2_bias),
        )
        res, gtok, *grads = finish_call(dim, ff, res, gtok, gq, go, gf, gp, gln)
        gq, go, gf, gp, g1, b1, g2, b2 = [sum_boxes(g, wide) for g in grads]
        return (
            res.transpose(0, 2, 1), gtok.transpose(0, 2, 1), g1, b1, gq, go, g2, b2, gf, gp.reshape(ff // NZ, dim)
        )

    rows = P(("wide", "narrow"), None, None)
    vec, mat = P("narrow"), P("narrow", None)
    return jax.shard_map(
        shards,
        mesh=mesh,
        in_specs=(rows, P(("wide", "narrow")), vec, vec, mat, mat, vec, vec, mat, mat, rows),
        out_specs=(rows, rows, vec, vec, mat, mat, vec, vec, mat, mat),
        check_vma=False,
    )
```

```python
import math

import jax
import jax.numpy as jnp
from jax import lax
from jax.experimental import pallas as pl
from jax.experimental.pallas import tpu as pltpu
from jax.sharding import PartitionSpec as P

HEADS = 20
EPS = 1e-05
MASKED = -1e30
BF, F32 = jnp.bfloat16, jnp.float32
MESH = pl.DeviceIdType.MESH

NZ = 4
NT = 4
WAVES = 2
SEQ = 128
NB = NT * WAVES
GELU_C = math.sqrt(2.0 / math.pi)
GELU_A = 0.044715
YWAY = ("f", "q",)
ZFIRST = ("p",)


def up16(n):
    return -(-n // 16) * 16


def up128(n):
    return -(-n // 128) * 128


def nn(a, b):
    return lax.dot_general(a, b, (((1,), (0,)), ((), ())), preferred_element_type=F32)


def nt(a, b):
    return lax.dot_general(a, b, (((1,), (1,)), ((), ())), preferred_element_type=F32)


def tn(a, b):
    return lax.dot_general(a, b, (((0,), (0,)), ((), ())), preferred_element_type=F32)


def layer_kernel(
    dim, ff,
    tok_h, dy_h, wq_h, wo_h, wf_h, wp_h, len_s, g1_i, b1_i, g2_i, b2_i,
    res_o, gtok_o, gq_o, go_o, gf_o, gp_o, gln_o,
    tok, dys, xown, wq, wo, wf, wp, qs, ks, vs, att, part, part1, ra, sb, rb, mix, dmix,
    sec, act, gel, datt, dqkv, gq, go, gf, gp, yq, yo, yf, yp, zq, zo, zf, zp,
    lnv, lnr, vec, lens, lg, lr, lz,
    raw_sem, ag_sem, rs_sem, fin_sem, xs_sem, xa_sem, ln_sem,
):
    blk = dim // NZ
    bp = up16(blk)
    hb = bp // 2
    dp = NZ * bp
    nq = wq.shape[1]
    head = dim // HEADS
    nh = HEADS // NT
    inv_dim = 1.0 / dim
    scale = head ** (-0.5)

    w = lax.axis_index("wide")
    z = lax.axis_index("narrow")
    c = lax.rem(w, 2)
    x = lax.rem(w // 2, 2)
    y = lax.rem(w // 4, 2)
    t = 2 * x + c
    core_dev = (w + 1 - 2 * c, z)
    x_dev = (w + 2 - 4 * x, z)
    y_dev = (w + 4 - 8 * y, z)
    up_dev = (w, z + 1)
    down_dev = (w, z - 1)

    ends = []

    def remote(src, dst, ssem, rsem, dev):
        return pltpu.make_async_remote_copy(
            src_ref=src, dst_ref=dst, send_sem=ssem, recv_sem=rsem, device_id=dev, device_id_type=MESH
        )

    def send(make, cond=None, track=True):
        if cond is None:
            make().start()
        else:
            pl.when(cond())(lambda: make().start())
        if track:
            ends.append((cond, make))

    def both(a, b):
        return jnp.logical_and(a, b)

    lane = lax.broadcasted_iota(jnp.int32, (1, dp), 1)
    live = lax.rem(lane, bp) < blk
    livef = live.astype(F32)

    barrier = pltpu.get_barrier_semaphore()
    others = [(w, lax.rem(z + k, NZ)) for k in range(1, NZ)]
    for dev in [core_dev, x_dev, y_dev] + others:
        pl.semaphore_signal(barrier, inc=1, device_id=dev, device_id_type=MESH)

    def rows_of(s, yy, r0=0, nr=None):
        return pl.ds(pl.multiple_of(bp * s + hb * yy + r0, 16), hb if nr is None else nr)

    q_pieces = [(0, 80), (80, hb - 80)]
    o_pieces = [(0, 48), (48, 48), (96, hb - 96)]
    gathers = {
        "q": (wq, 0, q_pieces),
        "f": (wf, 8, q_pieces),
        "p": (wp, 16, q_pieces),
        "o": (wo, 24, o_pieces),
    }

    def ag_view(name, s, yy, piece):
        ref, base, pieces = gathers[name]
        r0, nr = pieces[piece]
        if name == "o":
            return ref.at[rows_of(0, yy, r0, nr)]
        return ref.at[rows_of(s, yy, r0, nr)]

    def ag_id(name, s, piece):
        ref, base, pieces = gathers[name]
        return base + piece if name == "o" else base + 4 * piece + s

    def ag_z(name, s, piece, up):
        v = ag_view(name, s, y, piece)
        i = ag_id(name, s, piece)
        return remote(v, v, ag_sem.at[i, 0 if up else 1], ag_sem.at[i, 2], up_dev if up else down_dev)

    def ag_y(name, s, yy, piece):
        v = ag_view(name, s, yy, piece)
        i = ag_id(name, s, piece)
        return remote(v, v, ag_sem.at[i, 3], ag_sem.at[i, 4], y_dev)

    def ag_start(name):
        for piece in range(len(gathers[name][2])):
            def own():
                return (t == z) if name == "o" else (z >= 0)

            send(lambda p=piece: ag_z(name, z, p, True), lambda: both(own(), z < NZ - 1))
            send(lambda p=piece: ag_z(name, z, p, False), lambda: both(own(), z > 0))

    def ag_forward(name, k):
        for piece in range(len(gathers[name][2])):
            for up in (True, False):
                s = z - k if up else z + k
                ok = (z >= k) if up else (z + k <= NZ - 1)
                if name == "o":
                    ok = t == s
                more = (z < NZ - 1) if up else (z > 0)
                pl.when(ok)(lambda s=s, p=piece, u=up: ag_z(name, s, p, u).wait_recv())
                send(lambda s=s, p=piece, u=up: ag_z(name, s, p, u), lambda ok=ok, more=more: both(ok, more))
                send(lambda s=s, p=piece: ag_y(name, s, y, p), lambda ok=ok: ok)

    def ag_finish(name):
        for piece in range(len(gathers[name][2])):
            if name == "o":
                pl.when(z != t)(lambda p=piece: ag_y(name, 0, 1 - y, p).wait_recv())
            else:
                for s in range(NZ):
                    pl.when(z != s)(lambda s=s, p=piece: ag_y(name, s, 1 - y, p).wait_recv())

    def blk_of(s, cc, xx):
        return s * NT + cc * 2 + xx

    def xg(ref, e, s, kind):
        i = 2 * e + s
        if kind == "x":
            v = ref.at[blk_of(s, c, x)]
            return remote(v, v, xs_sem.at[i, 0], xs_sem.at[i, 1], x_dev)
        if kind == "own":
            v = ref.at[blk_of(s, c, x)]
            return remote(v, v, xs_sem.at[i, 2], xs_sem.at[i, 3], core_dev)
        v = ref.at[blk_of(s, c, 1 - x)]
        return remote(v, v, xs_sem.at[i, 4], xs_sem.at[i, 5], core_dev)

    def xg_start(ref, e, s, track=True):
        send(lambda: xg(ref, e, s, "x"), track=track)
        send(lambda: xg(ref, e, s, "own"), track=track)

    def xg_forward(ref, e, s, track=True):
        xg(ref, e, s, "x").wait_recv()
        send(lambda: xg(ref, e, s, "fwd"), track=track)

    def xg_finish(ref, e, s):
        xg(ref, e, s, "own").wait_recv()
        xg(ref, e, s, "fwd").wait_recv()

    def xg_sent(ref, e, s):
        for kind in ("x", "own", "fwd"):
            xg(ref, e, s, kind).wait_send()

    def part_of(e):
        return part1 if e == 1 else part

    def ex_a(e, s):
        i = 2 * e + s
        return remote(
            part_of(e).at[pl.ds(s * NT + (1 - c) * 2, 2)], ra.at[int(e == 1), s],
            xa_sem.at[i, 0], xa_sem.at[i, 1], core_dev,
        )

    def ex_b(e, s):
        i = 2 * e + s
        return remote(sb.at[int(e == 1), s], rb.at[int(e == 1), s], xa_sem.at[i, 2], xa_sem.at[i, 3], x_dev)

    def ex_relay(e, s):
        ex_a(e, s).wait_recv()
        sb[int(e == 1), s] = (
            part_of(e)[blk_of(s, c, 1 - x)].astype(F32) + ra[int(e == 1), s, 1 - x].astype(F32)
        ).astype(BF)
        ex_b(e, s).start()

    def ex_sum(e, s):
        ex_b(e, s).wait_recv()
        return (
            part_of(e)[blk_of(s, c, x)].astype(F32)
            + ra[int(e == 1), s, x].astype(F32)
            + rb[int(e == 1), s].astype(F32)
        )

    base = pl.multiple_of(bp * z, 16)
    reduces = {"q": (gq, yq, zq, 0), "f": (gf, yf, zf, 1), "p": (gp, yp, zp, 2), "o": (go, yo, zo, 3)}

    def rs_y(name, d):
        g, yr, zr, i = reduces[name]
        if name == "o":
            r0, nr = o_pieces[d]
            return remote(
                g.at[rows_of(0, 1 - y, r0, nr)], yr.at[0, pl.ds(r0, nr)], rs_sem.at[i, d], rs_sem.at[i, 4 + d], y_dev
            )
        if name in ZFIRST:
            return remote(g.at[rows_of(z, 1 - y)], yr.at[0], rs_sem.at[i, 0], rs_sem.at[i, 4], y_dev)
        return remote(g.at[rows_of(d, 1 - y)], yr.at[d], rs_sem.at[i, d], rs_sem.at[i, 4 + d], y_dev)

    def rs_z(name, d, slot, up):
        g, yr, zr, i = reduces[name]
        if name == "o":
            rows = pl.ds(*o_pieces[d])
            return remote(
                yr.at[0, rows], zr.at[slot, rows], rs_sem.at[i, 8 + d], rs_sem.at[i, 12 + 2 * d + slot], up_dev if up else down_dev
            )
        if name in ZFIRST:
            return remote(
                g.at[pl.ds(bp * d, bp)], zr.at[slot], rs_sem.at[i, 8 + d], rs_sem.at[i, 12 + slot], up_dev if up else down_dev
            )
        return remote(yr.at[d], zr.at[slot], rs_sem.at[i, 8 + d], rs_sem.at[i, 12 + slot], up_dev if up else down_dev)

    def add_up(dst, srcs):
        step = 48

        def body(j, carry):
            r = pl.ds(pl.multiple_of(j * step, step), step)
            total = srcs[0][r, :].astype(F32)
            for src in srcs[1:]:
                total = total + src[r, :].astype(F32)
            dst[r, :] = total.astype(BF)
            return carry

        lax.fori_loop(0, dst.shape[0] // step, body, 0)

    def rs_start(name, dests=(3, 0, 2, 1)):
        for d in range(len(o_pieces)) if name == "o" else dests:
            send(lambda d=d: rs_y(name, d))

    def rs_stage(name, d, j):
        g, yr, zr, i = reduces[name]

        def side(pos, up):
            def run():
                if name in ZFIRST:
                    if j > 0:
                        own = g.at[pl.ds(bp * d, bp)]
                        rs_z(name, d, d, up).wait_recv()
                        add_up(own, [own, zr.at[d]])
                    return
                rs_y(name, d).wait_recv()
                if name == "o":
                    r0, nr = o_pieces[d]
                    own, mine, past = g.at[rows_of(0, y, r0, nr)], yr.at[0, pl.ds(r0, nr)], zr.at[0, pl.ds(r0, nr)]
                else:
                    own, mine, past = g.at[rows_of(d, y)], yr.at[d], zr.at[d]
                srcs = [own, mine]
                if j > 0:
                    rs_z(name, d, 0 if name == "o" else d, up).wait_recv()
                    srcs.append(past)
                add_up(mine, srcs)

            nxt = pos + 1 if up else pos - 1
            if name == "o":
                last = t == nxt
                cond = both(z == pos, (t > pos) if up else (t < pos))
                pl.when(cond)(run)
                if up:
                    send(lambda: rs_z(name, d, 1, True), lambda: both(cond, last))
                    send(lambda: rs_z(name, d, 0, True), lambda: both(cond, jnp.logical_not(last)))
                else:
                    send(lambda: rs_z(name, d, 0, False), lambda: cond)
            else:
                cond = z == pos
                pl.when(cond)(run)
                slot = NZ if (up and nxt == d) else d
                send(lambda: rs_z(name, d, slot, up), lambda: cond)

        if name == "o":
            if j < NZ - 1:
                side(j, True)
                side(NZ - 1 - j, False)
            return
        if j < d:
            side(j, True)
        if NZ - 1 - j > d:
            side(NZ - 1 - j, False)

    def rs_line(name):
        g, yr, zr, i = reduces[name]
        own = g.at[pl.ds(base, bp)]

        def run(slots):
            def go_():
                for slot in slots:
                    rs_z(name, slot if slot < NZ else 0, slot, True).wait_recv()
                add_up(own, [own] + [zr.at[slot] for slot in slots])
            return go_

        for k in range(NZ):
            pl.when(z == k)(run(([k] if k < NZ - 1 else []) + ([NZ] if k > 0 else [])))
        send(lambda: rs_y(name, 0))

    def rs_final(name):
        g, yr, zr, i = reduces[name]
        if name in ZFIRST:
            rs_y(name, 0).wait_recv()
            add_up(yr.at[0], [g.at[rows_of(z, y)], yr.at[0]])
            return
        out = name == "o"
        me = 0 if out else z
        here = (t == z) if out else (z >= 0)
        above = 0 if out else z
        below = 1 if out else NZ

        def run(has_above, has_below):
            def go_():
                parts = range(len(o_pieces)) if out else [me]
                for d in parts:
                    rs_y(name, d).wait_recv()
                srcs = [g.at[rows_of(me, y)], yr.at[me]]
                if has_above:
                    for d in parts:
                        rs_z(name, d, above, True).wait_recv()
                    srcs.append(zr.at[above])
                if has_below:
                    for d in parts:
                        rs_z(name, d, below, True).wait_recv()
                    srcs.append(zr.at[below])
                add_up(yr.at[me], srcs)
            return go_

        pl.when(both(here, z == 0))(run(True, False))
        pl.when(both(here, z == NZ - 1))(run(False, True))
        pl.when(both(here, both(z > 0, z < NZ - 1)))(run(True, True))

    outs = {"q": gq_o, "f": gf_o, "p": gp_o, "o": go_o}

    def fin_view(name, tt, yy):
        return outs[name].at[yy] if name == "o" else outs[name].at[tt * 2 + yy]

    def fin_copy(name, src, tt, yy, k, dev):
        i = reduces[name][3]
        slot = yy if name == "o" else tt * 2 + yy
        return remote(src, fin_view(name, tt, yy), fin_sem.at[i, k], fin_sem.at[i, 8 + slot], dev)

    def own_block(name):
        yr = reduces[name][1]
        return yr.at[0] if name == "o" or name in ZFIRST else yr.at[z]

    def keep_own(name):
        return pltpu.make_async_copy(own_block(name), fin_view(name, t, y), fin_sem.at[reduces[name][3], 7])

    tx = 2 * (1 - x) + c

    def fin_start(name):
        here = (lambda: t == z) if name == "o" else None
        if here is None:
            keep_own(name).start()
        else:
            pl.when(here())(lambda: keep_own(name).start())
        send(lambda: fin_copy(name, own_block(name), t, y, 0, y_dev), here)
        send(lambda: fin_copy(name, own_block(name), t, y, 1, x_dev), here)
        send(lambda: fin_copy(name, own_block(name), t, y, 2, core_dev), here)

    def fin_wait(name, tt, yy):
        fin_copy(name, fin_view(name, tt, yy), tt, yy, 0, core_dev).wait_recv()

    def fin_forward(name, turn):
        steps = [(t, 1 - y, x_dev), (tx, y, None), (tx, 1 - y, None)]
        if name in YWAY:
            steps = [(tx, y, y_dev), (t, 1 - y, None), (tx, 1 - y, None)]
        tt, yy, dev = steps[turn]
        here = (tt == z) if name == "o" else (z >= 0)
        v = fin_view(name, tt, yy)
        pl.when(here)(lambda: fin_wait(name, tt, yy))
        if dev is not None:
            send(lambda: fin_copy(name, v, tt, yy, 3, dev), lambda: here)
        send(lambda: fin_copy(name, v, tt, yy, 4 + turn, core_dev), lambda: here)

    def fin_finish(name):
        if name == "o":
            here = lax.rem(z, 2) != c
            for yy in range(2):
                pl.when(here)(lambda yy=yy: fin_wait(name, 0, yy))
            pl.when(t == z)(lambda: keep_own(name).wait())
        else:
            for xx in range(2):
                for yy in range(2):
                    fin_wait(name, 2 * xx + (1 - c), yy)
            keep_own(name).wait()

    def prepare(rq, rt, ro, rd, turned, rf, rp):
        loads = [
            pltpu.make_async_copy(wq_h, rq, raw_sem.at[0]),
            pltpu.make_async_copy(tok_h, rt, raw_sem.at[1]),
            pltpu.make_async_copy(wo_h, ro, raw_sem.at[2]),
            pltpu.make_async_copy(dy_h, rd, raw_sem.at[3]),
            pltpu.make_async_copy(wf_h, rf, raw_sem.at[4]),
            pltpu.make_async_copy(wp_h.at[pl.ds(pl.multiple_of(blk * t, 8), blk)], rp, raw_sem.at[5]),
        ]
        for load in loads:
            load.start()
        lnv[...] = jnp.zeros_like(lnv)
        for k, ref in enumerate((g1_i, b1_i, g2_i, b2_i)):
            lnv[k : k + 1, 0:blk] = ref[...].astype(F32).reshape(1, blk)
        lnr[z] = lnv[...]

        loads[0].wait()
        wq[pl.ds(base, bp), :] = jnp.zeros((bp, nq), BF)
        for k in range(NT):
            @pl.when(t == k)
            def _(k=k):
                for j in range(3):
                    wq[pl.ds(base, blk), blk * j : blk * (j + 1)] = rq[:, dim * j + blk * k : dim * j + blk * (k + 1)]
        pl.semaphore_wait(barrier, 3 + len(others))
        for k in range(1, NZ):
            send(lambda k=k: remote(lnv, lnr.at[z], ln_sem.at[k - 1], ln_sem.at[2 + k], others[k - 1]))
        ag_start("q")

        turned[...] = jnp.zeros_like(turned)

        def spread(dst, src):
            for j in range(NZ):
                turned[bp * j : bp * j + blk, :] = src[blk * j : blk * (j + 1), :]
            dst[...] = turned[...].T

        loads[1].wait()
        for s in range(WAVES):
            spread(xown.at[s], rt.at[s])
            sent = jnp.where(lane == blk, len_s[s].astype(F32), xown[s].astype(F32))
            tok[blk_of(s, c, x)] = sent.astype(BF)
            xg_start(tok, 0, s, track=False)
        loads[2].wait()

        @pl.when(t == z)
        def _():
            wo[...] = jnp.zeros_like(wo)
            for j in range(NZ):
                wo[0:blk, bp * j : bp * j + blk] = ro[:, blk * j : blk * (j + 1)]
        ag_start("o")
        loads[3].wait()
        for s in range(WAVES):
            spread(dys.at[blk_of(s, c, x)], rd.at[s])
            xg_start(dys, 1, s)

        def prepare_mlp():
            loads[4].wait()
            wf[pl.ds(base, bp), :] = jnp.zeros((bp, dp), BF)
            for k in range(NT):
                @pl.when(t == k)
                def _(k=k):
                    for j in range(NZ):
                        lo = (ff // NZ) * j + blk * k
                        wf[pl.ds(base, blk), bp * j : bp * j + blk] = rf[:, lo : lo + blk]
            loads[5].wait()
            wp[pl.ds(base, bp), :] = jnp.zeros((bp, dp), BF)
            for j in range(NZ):
                wp[pl.ds(base, blk), bp * j : bp * j + blk] = rp[:, blk * j : blk * (j + 1)]

        prepare_mlp()

    pl.run_scoped(
        prepare,
        pltpu.VMEM((blk, 3 * dim), BF),
        pltpu.VMEM((WAVES, dim, SEQ), BF),
        pltpu.VMEM((blk, dim), BF),
        pltpu.VMEM((WAVES, dim, SEQ), BF),
        pltpu.VMEM((dp, SEQ), BF),
        pltpu.VMEM((blk, ff), BF),
        pltpu.VMEM((blk, dim), BF),
    )

    def main(first, pm):
        def vectors():
            for k in range(1, NZ):
                remote(lnv, lnr.at[lax.rem(z + NZ - k, NZ)], ln_sem.at[k - 1], ln_sem.at[2 + k], others[k - 1]).wait_recv()
            vec[...] = jnp.zeros_like(vec)
            for j in range(NZ):
                vec[:, bp * j : bp * j + blk] = lnr[j, :, 0:blk]

        lg[...] = jnp.zeros_like(lg)
        dqkv[...] = jnp.zeros_like(dqkv)

        def stats(rows):
            mean = jnp.sum(rows, axis=-1, keepdims=True) * inv_dim
            cen = (rows - mean) * livef
            inv = lax.rsqrt(jnp.sum(cen * cen, axis=-1, keepdims=True) * inv_dim + EPS)
            return cen * inv, inv

        def norm_back(e, n, inv):
            me = jnp.sum(e, axis=-1, keepdims=True) * inv_dim
            mn = jnp.sum(e * n, axis=-1, keepdims=True) * inv_dim
            return inv * (e - me - n * mn) * livef

        def ln_first(s):
            def body(i, carry):
                b = s * NT + i
                raw = tok[b].astype(F32)
                lens[b] = jnp.broadcast_to(raw[0:8, blk : blk + 1], (8, SEQ))
                n, inv = stats(raw * livef)
                first[b] = (n * vec[0:1, :] + vec[1:2, :]).astype(BF)
                return carry
            lax.fori_loop(0, NT, body, 0)

        lane_h = lax.broadcasted_iota(jnp.int32, (1, bp), 1)
        head_masks = [(lane_h >= head * h) & (lane_h < head * (h + 1)) for h in range(nh)]

        def stack_heads(v):
            zero = jnp.zeros_like(v)
            return jnp.concatenate([jnp.where(m, v, zero) for m in head_masks], axis=0)

        def side_by_side(v):
            return jnp.concatenate([v[SEQ * h : SEQ * (h + 1)] for h in range(nh)], axis=1)

        def project(s):
            def body(i, carry):
                b = s * NT + i * 2
                rows = first[pl.ds(b, 2)].reshape(2 * SEQ, dp)
                out = nn(rows, wq[...])
                for j, ref in enumerate((qs, ks, vs)):
                    ref[pl.ds(b, 2)] = out[:, blk * j : blk * j + bp].astype(BF).reshape(2, SEQ, bp)
                return carry
            lax.fori_loop(0, 2, body, 0)

        def attend(s):
            q_pos = lax.broadcasted_iota(jnp.int32, (SEQ, SEQ), 0)
            k_pos = lax.broadcasted_iota(jnp.int32, (SEQ, SEQ), 1)

            def body(i, carry):
                b = s * NT + i
                scores = nt(stack_heads(qs[b]), ks[b]) * scale
                ok = (k_pos <= q_pos) & (k_pos.astype(F32) < lens[b, 0:1, :])
                bias = jnp.concatenate([ok.astype(F32)] * nh, axis=0) > 0.5
                scores = jnp.where(bias, scores, MASKED)
                top = jnp.max(scores, axis=-1, keepdims=True)
                ex = jnp.exp(scores - top)
                prob = ex / jnp.sum(ex, axis=-1, keepdims=True)
                pm[b] = prob
                out = nn(side_by_side(prob.astype(BF)), stack_heads(vs[b]))
                att[b] = out.astype(BF)
                return carry
            lax.fori_loop(0, NT, body, 0)

        def matmul_part(src, weight, s, transposed, e):
            width = src.shape[2]
            dst = part_of(e)

            def body(i, carry):
                b = s * NT + i * 2
                rows = src[pl.ds(b, 2)].reshape(2 * SEQ, width)
                out = nt(rows, weight[...]) if transposed else nn(rows, weight[...])
                dst[pl.ds(b, 2)] = out.astype(BF).reshape(2, SEQ, dp)
                return carry
            lax.fori_loop(0, 2, body, 0)

        def mid(s):
            rows = xown[s].astype(F32) + ex_sum(0, s)
            mix[s] = rows
            n, inv = stats(rows)
            sec[blk_of(s, c, x)] = (n * vec[2:3, :] + vec[3:4, :]).astype(BF)
            xg_start(sec, 2, s)

        def expand(s):
            def body(i, carry):
                b = s * NT + i * 2
                rows = sec[pl.ds(b, 2)].reshape(2 * SEQ, dp)
                pre = nn(rows, wf[...])
                sq = pre * pre
                th = jnp.tanh(GELU_C * (pre + GELU_A * (pre * sq)))
                half = 0.5 * (1.0 + th)
                act[pl.ds(b, 2)] = (pre * half).astype(BF).reshape(2, SEQ, dp)
                slope = half + (0.5 * GELU_C) * pre * (1.0 - th * th) * (1.0 + (3.0 * GELU_A) * sq)
                gel[pl.ds(b, 2)] = slope.astype(BF).reshape(2, SEQ, dp)
                return carry
            lax.fori_loop(0, 2, body, 0)

        def grad_of(name, left, right):
            dst = reduces[name][0]
            step = 384
            rows = NB * SEQ
            leave = {} if name in ZFIRST else {0: (3,), 1: (0,), 2: (2, 1)}

            def depart(k):
                for d in leave.get(k, ()):
                    rs_y(name, d).start()

            def body(k, carry):
                cols = pl.ds(pl.multiple_of(lax.rem(k + 2, 3) * step, step), step)
                out = tn(left[:, :, cols].reshape(rows, step), right[...].reshape(rows, right.shape[2]))
                dst[cols, :] = out.astype(BF)
                for n in leave:
                    pl.when(k == n)(lambda n=n: depart(n))
                return carry

            lax.fori_loop(0, dp // step, body, 0)
            for ds in leave.values():
                ends.extend((None, lambda d=d: rs_y(name, d)) for d in ds)

        def back_act(s):
            def body(i, carry):
                b = s * NT + i * 2
                d_act = nt(dys[pl.ds(b, 2)].reshape(2 * SEQ, dp), wp[...])
                slope = gel[pl.ds(b, 2)].reshape(2 * SEQ, dp).astype(F32)
                gel[pl.ds(b, 2)] = (d_act * slope).astype(BF).reshape(2, SEQ, dp)
                return carry
            lax.fori_loop(0, 2, body, 0)

        def back_mid(s):
            d2 = ex_sum(2, s)
            n, inv = stats(mix[s])
            lg[2:3, :] = lg[2:3, :] + jnp.sum(d2 * n, axis=0, keepdims=True)
            lg[3:4, :] = lg[3:4, :] + jnp.sum(d2, axis=0, keepdims=True)
            rows = dys[blk_of(s, c, x)].astype(F32) + norm_back(d2 * vec[2:3, :], n, inv)
            dmix[s] = rows
            tok[blk_of(s, c, x)] = rows.astype(BF)
            xg_start(tok, 3, s)

        def back_attend(s):
            def proj(i, carry):
                b = s * NT + i * 2
                out = nt(tok[pl.ds(b, 2)].reshape(2 * SEQ, dp), wo[...])
                datt[pl.ds(b, 2)] = out.astype(BF).reshape(2, SEQ, bp)
                return carry
            lax.fori_loop(0, 2, proj, 0)

            def body(i, carry):
                b = s * NT + i
                d_out = stack_heads(datt[b])
                prob = pm[b]
                d_prob = nt(d_out, vs[b])
                total = jnp.sum(prob * d_prob, axis=-1, keepdims=True)
                d_scores = (prob * (d_prob - total)).astype(BF)
                dqkv[b, :, 0:bp] = (nn(side_by_side(d_scores), stack_heads(ks[b])) * scale).astype(BF)
                dqkv[b, :, blk : blk + bp] = (tn(d_scores, stack_heads(qs[b])) * scale).astype(BF)
                dqkv[b, :, 2 * blk : 2 * blk + bp] = tn(prob.astype(BF), d_out).astype(BF)
                return carry
            lax.fori_loop(0, NT, body, 0)

        def back_first(s):
            d1 = ex_sum(3, s)
            n, inv = stats(xown[s].astype(F32))
            lg[0:1, :] = lg[0:1, :] + jnp.sum(d1 * n, axis=0, keepdims=True)
            lg[1:2, :] = lg[1:2, :] + jnp.sum(d1, axis=0, keepdims=True)
            gtok_o[s] = (dmix[s] + norm_back(d1 * vec[0:1, :], n, inv)).astype(BF)

        def grad_out():
            rows_all = NB * SEQ
            go[...] = tn(att[...].reshape(rows_all, bp), tok[...].reshape(rows_all, dp)).astype(BF)

        def finish_rows(s):
            res_o[s] = (mix[s] + ex_sum(1, s)).astype(BF)

        hops = [
            remote(lg, lr.at[k], ln_sem.at[6 + 2 * k], ln_sem.at[7 + 2 * k], dev)
            for k, dev in enumerate((core_dev, x_dev, y_dev))
        ]

        def ln_add(k):
            hops[k].wait()
            lg[...] = lg[...] + lr[k]

        def ln_line(k):
            return remote(lg, lz.at[k - 1], ln_sem.at[11 + k], ln_sem.at[14 + k], others[k - 1])

        def ln_send():
            for k in range(1, NZ):
                send(lambda k=k: ln_line(k))

        def ln_total():
            for k in range(1, NZ):
                ln_line(k).wait_recv()
            total = lg[...] + lz[0] + lz[1] + lz[2]
            for j in range(NZ):
                @pl.when(z == j)
                def _(j=j):
                    gln_o[:, 0:blk] = total[:, bp * j : bp * j + blk]

        ag_forward("q", 1)
        ag_forward("o", 1)
        ag_forward("q", 2)
        ag_forward("o", 2)
        ag_start("f")
        ag_start("p")
        xg_forward(tok, 0, 0, track=False)
        ag_forward("q", 3)
        xg_finish(tok, 0, 0)
        xg_forward(tok, 0, 1, track=False)
        vectors()
        ln_first(0)
        xg_finish(tok, 0, 1)
        ln_first(1)
        xg_forward(dys, 1, 0)
        xg_finish(dys, 1, 0)
        ag_forward("o", 3)
        ag_finish("q")
        project(0)
        project(1)
        attend(0)
        ag_forward("f", 1)
        ag_finish("o")
        matmul_part(att, wo, 0, False, 0)
        ex_a(0, 0).start()
        ex_relay(0, 0)
        xg_sent(tok, 0, 0)
        attend(1)
        xg_forward(dys, 1, 1)
        matmul_part(att, wo, 1, False, 0)
        ex_a(0, 1).start()
        ag_forward("f", 2)
        ag_forward("p", 1)
        ex_relay(0, 1)
        mid(0)
        ag_forward("f", 3)
        mid(1)
        xg_finish(dys, 1, 1)
        ag_forward("p", 2)
        xg_sent(tok, 0, 1)
        ex_b(0, 1).wait_send()
        ex_a(0, 0).wait_send()
        xg_forward(sec, 2, 0)
        xg_forward(sec, 2, 1)
        ag_forward("p", 3)
        xg_finish(sec, 2, 0)
        ag_finish("f")
        expand(0)
        xg_finish(sec, 2, 1)
        expand(1)
        grad_of("p", act, dys)
        rs_stage("p", 3, 0)
        rs_stage("p", 2, 0)
        ex_a(0, 1).wait_send()
        rs_stage("p", 0, 0)
        ag_finish("p")
        back_act(1)
        matmul_part(gel, wf, 1, True, 2)
        ex_a(2, 1).start()
        back_act(0)
        ex_relay(2, 1)
        ex_b(0, 0).wait_send()
        matmul_part(gel, wf, 0, True, 2)
        ex_a(2, 0).start()
        ex_relay(2, 0)
        grad_of("f", sec, gel)
        back_mid(0)
        rs_stage("p", 1, 0)
        matmul_part(act, wp, 0, False, 1)
        ex_a(1, 0).start()
        matmul_part(act, wp, 1, False, 1)
        ex_a(1, 1).start()
        rs_stage("f", 3, 0)
        back_mid(1)
        rs_stage("p", 3, 1)
        xg_forward(tok, 3, 0)
        rs_stage("p", 0, 1)
        rs_stage("f", 0, 0)
        xg_finish(tok, 3, 0)
        back_attend(0)
        xg_forward(tok, 3, 1)
        xg_finish(tok, 3, 1)
        back_attend(1)
        grad_of("q", first, dqkv)
        ex_a(2, 1).wait_send()
        ex_b(2, 0).wait_send()
        rs_stage("f", 1, 0)
        rs_stage("p", 1, 1)
        rs_stage("f", 2, 0)
        rs_stage("p", 3, 2)
        rs_stage("p", 2, 1)
        ex_b(2, 1).wait_send()
        matmul_part(dqkv, wq, 1, True, 3)
        ex_a(3, 1).start()
        rs_stage("p", 0, 2)
        ex_relay(1, 0)
        ex_a(2, 0).wait_send()
        ex_relay(1, 1)
        rs_stage("f", 0, 1)
        matmul_part(dqkv, wq, 0, True, 3)
        ex_a(3, 0).start()
        rs_line("p")
        ex_relay(3, 1)
        rs_stage("q", 3, 0)
        grad_out()
        rs_stage("f", 3, 1)
        rs_start("o")
        ex_relay(3, 0)
        rs_stage("q", 0, 0)
        rs_stage("q", 2, 0)
        rs_stage("f", 1, 1)
        rs_stage("q", 1, 0)
        rs_stage("f", 2, 1)
        rs_final("p")
        fin_start("p")
        back_first(1)
        back_first(0)
        hops[0].start()
        rs_stage("q", 3, 1)
        rs_stage("f", 3, 2)
        rs_stage("o", 1, 0)
        rs_stage("f", 0, 2)
        rs_stage("q", 0, 1)
        finish_rows(1)
        ln_add(0)
        hops[1].start()
        rs_stage("o", 0, 0)
        rs_final("f")
        rs_stage("q", 2, 1)
        fin_start("f")
        rs_stage("q", 1, 1)
        rs_stage("q", 0, 2)
        rs_stage("o", 2, 0)
        ln_add(1)
        rs_stage("q", 3, 2)
        rs_stage("o", 0, 1)
        hops[2].start()
        rs_final("q")
        fin_start("q")
        rs_stage("o", 1, 1)
        rs_final("o")
        fin_start("o")
        fin_forward("p", 0)
        rs_stage("o", 2, 1)
        fin_forward("f", 0)
        finish_rows(0)
        ln_add(2)
        ln_send()
        rs_stage("o", 1, 2)
        rs_stage("o", 0, 2)
        fin_forward("o", 1)
        fin_forward("f", 1)
        rs_stage("o", 2, 2)
        fin_forward("q", 1)
        fin_forward("q", 0)
        fin_forward("p", 1)
        fin_forward("p", 2)
        fin_forward("o", 0)
        ln_total()
        fin_forward("f", 2)
        fin_forward("q", 2)
        fin_forward("o", 2)
        for name in ("p", "f", "o", "q"):
            fin_finish(name)
        for s in range(WAVES):
            for e in (1, 3):
                ex_a(e, s).wait_send()
                ex_b(e, s).wait_send()
        for cond, make in ends:
            if cond is None:
                make().wait_send()
            else:
                pl.when(cond())(lambda make=make: make().wait_send())

    pl.run_scoped(main, pltpu.VMEM((NB, SEQ, dp), BF), pltpu.VMEM((NB, nh * SEQ, SEQ), F32))


def layer_call(dim, ff, tokens, cot, w_qkv, w_out, w_fc, w_proj, lengths, norms):
    blk = dim // NZ
    bp = up16(blk)
    hb = bp // 2
    dp = NZ * bp
    nq = up128(3 * blk)
    vm, dma = pltpu.VMEM, pltpu.SemaphoreType.DMA
    big = (NB, SEQ, dp)
    half = lambda k: (1 if k in ZFIRST else NZ, hb, nq if k == "q" else dp)
    line = lambda k: (NZ + 1, bp if k in ZFIRST else hb, nq if k == "q" else dp)
    scratch = [
        vm(big, BF), vm(big, BF), vm((WAVES, SEQ, dp), BF),
        vm((dp, nq), BF), vm((bp, dp), BF), vm((dp, dp), BF), vm((dp, dp), BF),
        vm((NB, SEQ, bp), BF), vm((NB, SEQ, bp), BF), vm((NB, SEQ, bp), BF),
        vm((NB, SEQ, bp), BF),
        vm(big, BF), vm(big, BF),
        vm((2, WAVES, 2, SEQ, dp), BF), vm((2, WAVES, SEQ, dp), BF), vm((2, WAVES, SEQ, dp), BF),
        vm((WAVES, SEQ, dp), F32), vm((WAVES, SEQ, dp), F32),
        vm(big, BF), vm(big, BF), vm(big, BF),
        vm((NB, SEQ, bp), BF), vm((NB, SEQ, nq), BF),
        vm((dp, nq), BF), vm((bp, dp), BF), vm((dp, dp), BF), vm((dp, dp), BF),
        vm(half("q"), BF), vm((1, hb, dp), BF), vm(half("f"), BF), vm(half("p"), BF),
        vm(line("q"), BF), vm((2, hb, dp), BF), vm(line("f"), BF), vm(line("p"), BF),
        vm((8, up128(blk)), F32), vm((NZ, 8, up128(blk)), F32), vm((8, dp), F32), vm((NB, 8, SEQ), F32),
        vm((8, dp), F32), vm((3, 8, dp), F32), vm((3, 8, dp), F32),
        dma((6,)), dma((27, 5)), dma((4, 18)), dma((4, 16)), dma((8, 6)), dma((8, 4)), dma((18,)),
    ]
    hbm = pl.BlockSpec(memory_space=pl.ANY)
    inv = pl.BlockSpec(memory_space=pltpu.VMEM)
    shape = jax.ShapeDtypeStruct

    def body(*refs):
        layer_kernel(dim, ff, *refs)

    return pl.pallas_call(
        body,
        out_shape=(
            shape((WAVES, SEQ, dp), BF), shape((WAVES, SEQ, dp), BF),
            shape((8, hb, nq), BF), shape((2, hb, dp), BF), shape((8, hb, dp), BF), shape((8, hb, dp), BF),
            shape((8, up128(blk)), F32),
        ),
        in_specs=[hbm] * 6 + [pl.BlockSpec(memory_space=pltpu.SMEM)] + [inv] * 4,
        out_specs=(inv, inv, hbm, hbm, hbm, hbm, inv),
        scratch_shapes=scratch,
        compiler_params=pltpu.CompilerParams(
            collective_id=0, has_side_effects=True, vmem_limit_bytes=67043328
        ),
    )(tokens, cot, w_qkv, w_out, w_fc, w_proj, lengths, *norms)


def finish_kernel(dim, ff, res, gtok, gq, go, gf, gp, gln, res_o, gtok_o, gq_o, go_o, gf_o, gp_o, *norms_o):
    blk = dim // NZ
    bp = up16(blk)
    for j in range(NZ):
        there = slice(bp * j, bp * j + blk)
        go_o[:, blk * j : blk * (j + 1)] = go[:, there].astype(F32)
        for t in range(NT):
            gp_o[t, :, blk * j : blk * (j + 1)] = gp[t, :, there].astype(F32)
            lo = (ff // NZ) * j + blk * t
            gf_o[:, lo : lo + blk] = gf[t, :, there].astype(F32)
    for j in range(3):
        for t in range(NT):
            lo = dim * j + blk * t
            gq_o[:, lo : lo + blk] = gq[t, :, blk * j : blk * (j + 1)].astype(F32)

    @pl.when(pl.program_id(0) == 0)
    def _():
        for k, ref in enumerate(norms_o):
            ref[...] = gln[k : k + 1, 0:blk].reshape(blk)
        for src, dst in ((res, res_o), (gtok, gtok_o)):
            for s in range(WAVES):
                turned = src[s].T
                for j in range(NZ):
                    dst[s, blk * j : blk * (j + 1), :] = turned[bp * j : bp * j + blk, :]


def finish_call(dim, ff, res, gtok, gq, go, gf, gp, gln):
    blk = dim // NZ
    bp = up16(blk)
    dp = NZ * bp
    nq = gq.shape[2]
    step = 56
    shape, spec = jax.ShapeDtypeStruct, pl.BlockSpec
    whole = spec(memory_space=pltpu.VMEM)
    quarters = lambda n: spec((NT, step, n), lambda i: (0, i, 0))
    lines = lambda n: spec((step, n), lambda i: (i, 0))
    return pl.pallas_call(
        lambda *refs: finish_kernel(dim, ff, *refs),
        grid=(blk // step,),
        in_specs=[whole, whole, quarters(nq), lines(dp), quarters(dp), quarters(dp), whole],
        out_specs=[whole, whole, lines(3 * dim), lines(dim), lines(ff), quarters(dim)] + [whole] * 4,
        out_shape=[
            shape((WAVES, dim, SEQ), BF), shape((WAVES, dim, SEQ), BF),
            shape((blk, 3 * dim), F32), shape((blk, dim), F32), shape((blk, ff), F32), shape((NT, blk, dim), F32),
        ] + [shape((blk,), F32)] * 4,
        compiler_params=pltpu.CompilerParams(vmem_limit_bytes=67043328),
    )(
        res, gtok, gq.reshape(NT, bp, nq), go.reshape(bp, dp), gf.reshape(NT, bp, dp), gp.reshape(NT, bp, dp), gln
    )


def sum_boxes(value, wide):
    total = value
    for k in range(1, wide // 8):
        total = total + lax.ppermute(value, "wide", [(i, (i + 8 * k) % wide) for i in range(wide)])
    return total


def solution(mesh):
    wide, narrow = mesh.shape["wide"], mesh.shape["narrow"]
    assert narrow == NZ and wide % 8 == 0

    def shards(tokens, lengths, ln1_gain, ln1_bias, w_qkv, w_out, ln2_gain, ln2_bias, w_fc, w_proj, cotangent):
        cells, seq, dim = tokens.shape
        assert cells == WAVES and seq == SEQ
        ff = w_fc.shape[1]
        blk = dim // NZ
        bp = up16(blk)
        res, gtok, gq, go, gf, gp, gln = layer_call(
            dim, ff, tokens.transpose(0, 2, 1), cotangent.transpose(0, 2, 1),
            w_qkv, w_out, w_fc, w_proj, lengths, (ln1_gain, ln1_bias, ln2_gain, ln2_bias),
        )
        res, gtok, *grads = finish_call(dim, ff, res, gtok, gq, go, gf, gp, gln)
        gq, go, gf, gp, g1, b1, g2, b2 = [sum_boxes(g, wide) for g in grads]
        return (
            res.transpose(0, 2, 1), gtok.transpose(0, 2, 1), g1, b1, gq, go, g2, b2, gf, gp.reshape(ff // NZ, dim)
        )

    rows = P(("wide", "narrow"), None, None)
    vec, mat = P("narrow"), P("narrow", None)
    return jax.shard_map(
        shards,
        mesh=mesh,
        in_specs=(rows, P(("wide", "narrow")), vec, vec, mat, mat, vec, vec, mat, mat, rows),
        out_specs=(rows, rows, vec, vec, mat, mat, vec, vec, mat, mat),
        check_vma=False,
    )
```
